32 devices in a mesh: seq: 2 (over core), fsdp: 16 (over z, y, x).
Axes of the slice: x: 2, y: 2, z: 4, core: 2. Of those that a mesh axis runs over, the one named last changes fastest.
Arguments:
- tokens: bfloat16 [2, 16, 1280, 768], P(None, 'fsdp', 'seq'), may hold values from -6 to 6
- permutation: int32 [2, 16, 1280], P(None, 'fsdp'), may hold values from 0 to 1279, each once within a row
- segment_ids: int32 [2, 16, 1280], P(None, 'fsdp'), may hold values from 0 to 3, never falling along the last dimension, each value on 1 to 1024 neighbouring positions
- cotangent: bfloat16 [2, 16, 1280, 768], P(None, 'fsdp', 'seq'), may hold values from -6 to 6
- w_qkv: bfloat16 [768, 2304], P(('seq', 'fsdp')), may hold values from -0.21875 to 0.21875
- b_qkv: bfloat16 [2304], P(('seq', 'fsdp')), may hold values from -3 to 3
- w_out: bfloat16 [768, 768], P(('seq', 'fsdp')), may hold values from -0.875 to 0.875
- b_out: bfloat16 [768], P(('seq', 'fsdp')), may hold values from -2 to 2
- gain_one: bfloat16 [768], P(('seq', 'fsdp')), may hold values from 0.5 to 1.5
- shift_one: bfloat16 [768], P(('seq', 'fsdp')), may hold values from -2 to 2
- w_up: bfloat16 [768, 3072], P(('seq', 'fsdp')), may hold values from -0.21875 to 0.21875
- b_up: bfloat16 [3072], P(('seq', 'fsdp')), may hold values from -2 to 2
- w_down: bfloat16 [3072, 768], P(('seq', 'fsdp')), may hold values from -0.109375 to 0.109375
- b_down: bfloat16 [768], P(('seq', 'fsdp')), may hold values from -2 to 2
- gain_two: bfloat16 [768], P(('seq', 'fsdp')), may hold values from 0.5 to 1.5
- shift_two: bfloat16 [768], P(('seq', 'fsdp')), may hold values from -2 to 2
Outputs:
- outputs: bfloat16 [2, 16, 1280, 768], P(None, 'fsdp', 'seq')
- token_grad: bfloat16 [2, 16, 1280, 768], P(None, 'fsdp', 'seq')
- grad_w_qkv: float32 [768, 2304], P(('seq', 'fsdp'))
- grad_b_qkv: float32 [2304], P(('seq', 'fsdp'))
- grad_w_out: float32 [768, 768], P(('seq', 'fsdp'))
- grad_b_out: float32 [768], P(('seq', 'fsdp'))
- grad_gain_one: float32 [768], P(('seq', 'fsdp'))
- grad_shift_one: float32 [768], P(('seq', 'fsdp'))
- grad_w_up: float32 [768, 3072], P(('seq', 'fsdp'))
- grad_b_up: float32 [3072], P(('seq', 'fsdp'))
- grad_w_down: float32 [3072, 768], P(('seq', 'fsdp'))
- grad_b_down: float32 [768], P(('seq', 'fsdp'))
- grad_gain_two: float32 [768], P(('seq', 'fsdp'))
- grad_shift_two: float32 [768], P(('seq', 'fsdp'))
The draws below stay inside these ranges and needn't reach their ends.
Inputs may be any that keep to these rules, and one draw needn't show every extreme that they name: Each row is a permutation of the 1280 rows of one pack. `segment_ids`: within each pack the ids never fall, begin at 0 and take every value up to 3; each sequence has 1 to 1024 tokens and one has exactly 1024.
All inputs are finite; a program needn't handle non-finite values.
Results may differ from the reference program's by a relative error of at most 0.015.
Values may be sent and summed in bfloat16 or wider, within the bound.
No kernel may reach another device: no remote copies, remote signals or barrier semaphores. Data moves between devices by JAX's collectives and lax.ppermute only.
A program may use at most 192 MiB of HBM per device.

```python
import math
import jax
import jax.numpy as jnp
import numpy as np
from jax import lax

D = 768
HEADS = 12
FF = 3072
MB = 2
SEGS = 4
GROUP = 1280
LONGEST = 1024
N_FSDP = 16


def spiked(entries, own_key, source, target, blocks, factor):
    def block_of(axis_at):
        return (jnp.arange(entries.shape[axis_at]) // (entries.shape[axis_at] // blocks)).reshape((-1,) + (1,) * (entries.ndim - 1 - axis_at))

    one_side = jax.random.permutation(own_key, blocks)[block_of(target)]
    second = (block_of(target) + blocks // 2) % blocks
    return jnp.where((block_of(source) == one_side) | (block_of(source) == second), factor * entries, entries)


def levels(rng, extent, split, least, largest):
    level = 1.0
    for axis_at, shards_of in split:
        heights = jax.random.uniform(jax.random.fold_in(jax.random.fold_in(rng, 6), axis_at), (shards_of,), jnp.float32, least / len(split), largest / len(split))
        level = level * jnp.repeat(jnp.exp(heights), extent[axis_at] // shards_of).reshape((-1,) + (1,) * (len(extent) - 1 - axis_at))
    return level


def profile(amount, total, bound, lean):
    loads = [(1 << 20) // math.isqrt(grade ** lean) + 1 for grade in range(2, amount + 1)]
    rest, holding = total - bound - (amount - 1), [1] * (amount - 1)
    while rest > 0:
        candidates = [i for i in range(amount - 1) if holding[i] < bound]
        mass, remaining = sum([loads[i] for i in candidates]), rest
        for i in candidates:
            addition = min(bound - holding[i], max(1, remaining * loads[i] // mass), rest)
            holding[i] = holding[i] + addition
            rest = rest - addition
    return np.array([bound] + holding)


def ragged_sizes(rng, count, total, limit, lean):
    if count == 2:
        one = jax.random.randint(rng, (), max(1, total - limit), min(limit, total - 1) + 1)
        return jnp.stack([one, total - one])
    sizes = jnp.asarray(profile(count, total, limit, lean), jnp.int32)
    twos = (count - 1) // 2
    source_of, receiver = sizes[1:1 + 2 * twos:2], sizes[2:2 + 2 * twos:2]
    room = jnp.minimum(source_of - 1, limit - receiver)
    passed = jax.random.randint(jax.random.fold_in(rng, 1), (twos,), 0, 1 << 20) % (room + 1)
    sizes = sizes.at[1:1 + 2 * twos:2].set(source_of - passed).at[2:2 + 2 * twos:2].set(receiver + passed)
    return sizes[jax.random.permutation(jax.random.fold_in(rng, 2), count)]


def noise(stream_key, dims, scale, bound, split=(), kind=jnp.bfloat16):
    array = scale * jax.random.normal(stream_key, dims, jnp.float32)
    if split:
        array = array * levels(stream_key, dims, split, -0.22, 0.18)
    return jnp.clip(array, -bound, bound).astype(kind)


def heavy_noise(key, shape, scale, reach, shards, heavy, held_as=jnp.bfloat16):
    drawn = scale * jax.random.normal(key, shape, jnp.float32)
    if shards:
        drawn = drawn * levels(key, shape, shards, -0.22, 0.18)
    return jnp.clip(spiked(drawn, jax.random.fold_in(key, 3), *heavy), -reach, reach).astype(held_as)


def setup_inputs(seed: int = 0) -> dict:
    seeds = jax.random.split(jax.random.key(seed), 17)
    return {
        "tokens": noise(seeds[0], (MB, N_FSDP, GROUP, D), 1.0, 6.0, ((1, 16), (2, 2))),
        "permutation": jax.vmap(lambda own: jax.random.permutation(own, GROUP))(jax.random.split(seeds[1], MB * N_FSDP)).reshape((MB, N_FSDP, GROUP)).astype(jnp.int32),
        "segment_ids": jax.vmap(lambda own: jnp.searchsorted(jnp.cumsum(ragged_sizes(own, SEGS, GROUP, LONGEST, 2)), jnp.arange(GROUP), side="right"))(jax.random.split(seeds[2], MB * N_FSDP)).reshape((MB, N_FSDP, GROUP)).astype(jnp.int32),
        "cotangent": heavy_noise(seeds[3], (MB, N_FSDP, GROUP, D), 1.0, 6.0, ((1, 16), (2, 2)), (1, 3, 16, 2.0)),
        "w_qkv": noise(seeds[4], (D, 3 * D), D ** -0.5, 0.21875, ((0, 32),)),
        "b_qkv": noise(seeds[5], (3 * D,), 0.5, 3.0, ((0, 32),)),
        "w_out": noise(seeds[6], (D, D), (D // 16) ** -0.5, 0.875, ((0, 32),)),
        "b_out": noise(seeds[7], (D,), 0.3, 2.0, ((0, 32),)),
        "gain_one": jnp.clip(1.0 + 0.1 * jax.random.normal(seeds[8], (D,), jnp.float32), 0.5, 1.5).astype(jnp.bfloat16),
        "shift_one": noise(seeds[9], (D,), 0.3, 2.0, ((0, 32),)),
        "w_up": noise(seeds[10], (D, FF), D ** -0.5, 0.21875, ((0, 32),)),
        "b_up": noise(seeds[11], (FF,), 0.3, 2.0, ((0, 32),)),
        "w_down": noise(seeds[12], (FF, D), FF ** -0.5, 0.109375, ((0, 32),)),
        "b_down": noise(seeds[13], (D,), 0.3, 2.0, ((0, 32),)),
        "gain_two": jnp.clip(1.0 + 0.1 * jax.random.normal(seeds[14], (D,), jnp.float32), 0.5, 1.5).astype(jnp.bfloat16),
        "shift_two": noise(seeds[15], (D,), 0.3, 2.0, ((0, 32),)),
    }


@jax.custom_vjp
def low(v):
    return lax.optimization_barrier(v.astype(jnp.bfloat16)).astype(jnp.float32)

@jax.custom_vjp
def low_back(v):
    return v

def low_keep(v):
    return (low(v), None)

def low_pass(kept, grad):
    return (grad,)

def back_keep(v):
    return (v, None)

def back_low(kept, grad):
    return (low(grad),)
low.defvjp(low_keep, low_pass)
low_back.defvjp(back_keep, back_low)
eps_norm = 1e-06
highest = lax.Precision.HIGHEST

def positions(segments):
    count_rows = segments.shape[0]
    places = jnp.arange(count_rows, dtype=jnp.int32)
    starts = jnp.concatenate([jnp.ones((1,), dtype=jnp.bool_), segments[1:] != segments[:-1]])
    firsts = lax.cummax(jnp.where(starts, places, jnp.zeros_like(places)), axis=0)
    return (places - firsts).astype(jnp.float32)

def rotate(values, angles, head_size):
    count_rows = values.shape[0]
    halves = head_size // 2
    paired = values.reshape(count_rows, -1, halves, 2)
    freqs = jnp.exp(jnp.arange(halves, dtype=jnp.float32) * (-2.0 * math.log(10000.0) / head_size))
    phase = angles[:, None, None] * freqs[None, None, :]
    cosine = jnp.cos(phase)
    sine = jnp.sin(phase)
    first_part = paired[..., 0]
    second_part = paired[..., 1]
    turned = jnp.stack([first_part * cosine - second_part * sine, second_part * cosine + first_part * sine], axis=-1)
    return turned.reshape(count_rows, -1)

def normalize(hidden, gain, shift):
    centre = hidden - lax.optimization_barrier(jnp.mean(hidden, axis=-1, keepdims=True))
    spread = lax.optimization_barrier(jnp.mean(centre * centre, axis=-1, keepdims=True))
    return centre * lax.rsqrt(spread + eps_norm) * gain + shift

def gelu_exact(values):
    return jax.nn.gelu(values, approximate=False)

def pack_layer(token_rows, order, segments, params):
    w_qkv, b_qkv, w_out, b_out, gain_one, shift_one, w_up, b_up, w_down, b_down, gain_two, shift_two = params
    count_rows = token_rows.shape[0]
    model_width = token_rows.shape[1]
    head_size = model_width // HEADS
    working = token_rows[order]
    angles = positions(segments)
    projected = low_back(jnp.dot(working, w_qkv, precision=highest) + b_qkv)
    queries = low(rotate(projected[:, :model_width], angles, head_size)).reshape(count_rows, HEADS, head_size)
    keys_all = low(rotate(projected[:, model_width:2 * model_width], angles, head_size)).reshape(count_rows, HEADS, head_size)
    values_all = low(projected[:, 2 * model_width:]).reshape(count_rows, HEADS, head_size)
    scores = jnp.einsum('qhd,khd->hqk', queries, keys_all, precision=highest) * (1.0 / math.sqrt(head_size))
    same_seq = segments[:, None] == segments[None, :]
    scores = low_back(jnp.where(same_seq[None], scores, -1000000000.0))
    top_score = lax.optimization_barrier(jnp.max(scores, axis=-1, keepdims=True))
    expo = jnp.exp(scores - top_score)
    probs = expo / lax.optimization_barrier(jnp.sum(expo, axis=-1, keepdims=True))
    context = jnp.einsum('hqk,khd->qhd', low(probs), values_all, precision=highest).reshape(count_rows, model_width)
    context = low_back(low(context))
    attended = low_back(jnp.dot(context, w_out, precision=highest) + b_out)
    first_norm = normalize(working + attended, gain_one, shift_one)
    upper = low_back(jnp.dot(low(first_norm), w_up, precision=highest) + b_up)
    lowered = low_back(jnp.dot(low(gelu_exact(upper)), w_down, precision=highest) + b_down)
    result = normalize(first_norm + lowered, gain_two, shift_two)
    inverse = jnp.zeros_like(order).at[order].set(jnp.arange(count_rows, dtype=jnp.int32))
    return result[inverse]

def reference(tokens, permutation, segment_ids, cotangent, w_qkv, b_qkv, w_out, b_out, gain_one, shift_one, w_up, b_up, w_down, b_down, gain_two, shift_two):
    params = tuple((weight.astype(jnp.float32) for weight in (w_qkv, b_qkv, w_out, b_out, gain_one, shift_one, w_up, b_up, w_down, b_down, gain_two, shift_two)))
    flat_tokens = tokens.astype(jnp.float32).reshape(-1, GROUP, D)
    flat_order = permutation.reshape(-1, GROUP)
    flat_segments = segment_ids.reshape(-1, GROUP)

    def forward(all_tokens, weights):

        def step_pack(carry, item):
            pack_tokens, pack_order, pack_segments = item
            return (carry, jax.checkpoint(pack_layer)(pack_tokens, pack_order, pack_segments, weights))
        _, results = lax.scan(step_pack, jnp.zeros((), jnp.float32), (all_tokens, flat_order, flat_segments))
        return results
    results, pullback = jax.vjp(forward, flat_tokens, params)
    grad_tokens, grad_params = pullback(cotangent.astype(jnp.float32).reshape(results.shape))
    return (results.reshape(tokens.shape).astype(jnp.bfloat16), grad_tokens.reshape(tokens.shape).astype(jnp.bfloat16), grad_params[0], grad_params[1], grad_params[2], grad_params[3], grad_params[4], grad_params[5], grad_params[6], grad_params[7], grad_params[8], grad_params[9], grad_params[10], grad_params[11])
```

```python
import functools
import math

import jax
import jax.numpy as jnp
from jax import lax
from jax.experimental import pallas as pl
from jax.experimental.pallas import tpu as pltpu
from jax.sharding import PartitionSpec as P

HEAD = 64
PAIR = 2 * HEAD
SEG_COUNT = 4
LOG2E = math.log2(math.e)
LN2 = math.log(2.0)
FAR = float(2**30)
BF = jnp.bfloat16
F32 = jnp.float32


def dot(left, right):
    return jnp.dot(left, right, preferred_element_type=F32)


def dot_rt(left, right):
    return lax.dot_general(left, right, (((1,), (1,)), ((), ())), preferred_element_type=F32)


def dot_lt(left, right):
    return lax.dot_general(left, right, (((0,), (0,)), ((), ())), preferred_element_type=F32)


def pair_swap(values):
    lanes = lax.broadcasted_iota(jnp.int32, values.shape, 1)
    width = values.shape[1]
    return jnp.where(
        lanes % 2 == 0, pltpu.roll(values, width - 1, 1), pltpu.roll(values, 1, 1)
    )


def project_body(block, share, idx_ref, own_ref, other_ref, wq_ref, wk_ref, wv_ref, bias_ref,
                 cos_ref, sin_ref, xw_ref, q_ref, k_ref, v_ref):
    half = own_ref.shape[0]

    def step(i, carry):
        rows = pl.ds(pl.multiple_of(i * block, block), block)
        picks = lax.broadcasted_iota(jnp.int32, (block, half), 1)
        where_from = idx_ref[rows, :]
        near = (picks == where_from).astype(BF)
        away = (picks + half == where_from).astype(BF)
        work = (dot(near, own_ref[...]) + dot(away, other_ref[...])).astype(BF)
        xw_ref[rows, :] = work
        cosine, sine = cos_ref[rows, :], sin_ref[rows, :]
        for w_ref, out_ref, place, scale in (
            (wq_ref, q_ref, 0, LOG2E / math.sqrt(HEAD)),
            (wk_ref, k_ref, 1, 1.0),
        ):
            pre = dot(work, w_ref[...]) + bias_ref[:, place * share:(place + 1) * share]
            for j in range(share // PAIR):
                cols = slice(j * PAIR, (j + 1) * PAIR)
                part = pre[:, cols]
                out_ref[rows, cols] = (
                    (part * cosine + pair_swap(part) * sine) * scale
                ).astype(BF)
        v_ref[rows, :] = (dot(work, wv_ref[...]) + bias_ref[:, 2 * share:]).astype(BF)
        return carry

    lax.fori_loop(0, idx_ref.shape[0] // block, step, 0)


def project(idx_col, own, other, w_qkv, bias_own, cosine, sine, part, block=256):
    rows = idx_col.shape[0]
    width = own.shape[1]
    share = bias_own.shape[1] // 3
    parts = w_qkv.shape[1] // (3 * share)
    whole = lambda shape: pl.BlockSpec(shape, lambda g, p: (0,) * len(shape))
    return pl.pallas_call(
        lambda part_ref, *refs: project_body(block, share, *refs),
        grid_spec=pltpu.PrefetchScalarGridSpec(
            num_scalar_prefetch=1,
            grid=(1,),
            in_specs=[
                whole((rows, 1)),
                whole(own.shape),
                whole(other.shape),
                pl.BlockSpec((width, share), lambda g, p: (0, p[0])),
                pl.BlockSpec((width, share), lambda g, p: (0, parts + p[0])),
                pl.BlockSpec((width, share), lambda g, p: (0, 2 * parts + p[0])),
                whole(bias_own.shape),
                whole(cosine.shape),
                whole(sine.shape),
            ],
            out_specs=[whole((rows, width))] + [whole((rows, share))] * 3,
        ),
        out_shape=[jax.ShapeDtypeStruct((rows, width), BF)]
        + [jax.ShapeDtypeStruct((rows, share), BF)] * 3,
        compiler_params=pltpu.CompilerParams(vmem_limit_bytes=60 << 20),
        cost_estimate=pl.CostEstimate(
            flops=2 * rows * width * (rows + 3 * share),
            bytes_accessed=2 * (2 * rows * width + 3 * width * share + 3 * rows * share),
            transcendentals=0,
        ),
        name="project",
    )(part, idx_col, own, other, w_qkv, w_qkv, w_qkv, bias_own, cosine, sine)


def attend_body(block, idx_ref, q_ref, k_ref, v_ref, seg_col_ref, seg_row_ref,
                near_ref, away_ref, ctxt_ref, lse_ref, pick, ka, vt, qt, augt):
    rows = q_ref.shape[0]
    half = near_ref.shape[0]

    @pl.when(pl.program_id(0) == 0)
    def _():
        def fill(i, carry):
            span = pl.ds(pl.multiple_of(i * block, block), block)
            pick[span, :] = (
                lax.broadcasted_iota(jnp.int32, (block, rows), 1) == idx_ref[span, :]
            ).astype(BF)
            return carry

        lax.fori_loop(0, rows // block, fill, 0)
        lanes = lax.broadcasted_iota(jnp.int32, (rows, PAIR), 1)
        ka[:, PAIR:] = ((lanes == seg_col_ref[...]) | (lanes >= SEG_COUNT)).astype(BF)
        places = lax.broadcasted_iota(jnp.int32, (PAIR, rows), 0)
        augt[...] = jnp.where(
            (places < SEG_COUNT) & (places != seg_row_ref[...]), -FAR, 0.0
        ).astype(BF)

    ka[:, :PAIR] = k_ref[...]
    vt[...] = v_ref[...].T
    qt[...] = q_ref[...].T
    empty = jnp.zeros((HEAD, block), BF)

    def step(i, carry):
        span = pl.ds(pl.multiple_of(i * block, block), block)
        extra = augt[:, span]
        for h in range(2):
            mine = qt[h * HEAD:(h + 1) * HEAD, span]
            mixed = jnp.concatenate([mine, empty, extra] if h == 0 else [empty, mine, extra], axis=0)
            scores = dot(ka[...], mixed)
            top = jnp.max(scores, axis=0, keepdims=True)
            expo = jnp.exp2(scores - top)
            total = jnp.sum(expo, axis=0, keepdims=True)
            context = dot(vt[h * HEAD:(h + 1) * HEAD, :], expo.astype(BF))
            ctxt_ref[h * HEAD:(h + 1) * HEAD, span] = (context / total).astype(BF)
            lse_ref[0, h:h + 1, span] = top + jnp.log2(total)
        return carry

    lax.fori_loop(0, rows // block, step, 0)
    given = dot(ctxt_ref[...], pick[...]).astype(BF)
    near_ref[...] = given[:, :half].T
    away_ref[...] = given[:, half:].T


def attend(idx_col, q, k, v, seg_col, seg_row, block=256):
    rows, share = q.shape
    pairs = share // PAIR
    half = rows // 2
    whole = lambda shape: pl.BlockSpec(shape, lambda j: (0,) * len(shape))
    column = lambda n: pl.BlockSpec((n, PAIR), lambda j: (0, j))
    return pl.pallas_call(
        functools.partial(attend_body, block),
        grid=(pairs,),
        in_specs=[whole((rows, 1)), column(rows), column(rows), column(rows),
                  whole((rows, 1)), whole((1, rows))],
        out_specs=[column(half), column(half), pl.BlockSpec((PAIR, rows), lambda j: (j, 0)),
                   pl.BlockSpec((1, 8, rows), lambda j: (j, 0, 0))],
        out_shape=[jax.ShapeDtypeStruct((half, share), BF), jax.ShapeDtypeStruct((half, share), BF),
                   jax.ShapeDtypeStruct((share, rows), BF),
                   jax.ShapeDtypeStruct((pairs, 8, rows), F32)],
        scratch_shapes=[pltpu.VMEM((rows, rows), BF), pltpu.VMEM((rows, 2 * PAIR), BF),
                        pltpu.VMEM((PAIR, rows), BF), pltpu.VMEM((PAIR, rows), BF),
                        pltpu.VMEM((PAIR, rows), BF)],
        compiler_params=pltpu.CompilerParams(vmem_limit_bytes=60 << 20),
        cost_estimate=pl.CostEstimate(
            flops=pairs * 2 * 2 * rows * rows * 3 * PAIR, bytes_accessed=2 * 6 * rows * share,
            transcendentals=2 * pairs * rows * rows,
        ),
        name="attend",
    )(idx_col, q, k, v, seg_col, seg_row)


def attend_back_body(block, idx_ref, q_ref, k_ref, v_ref, seg_col_ref, seg_row_ref, lse_ref,
                     ctxt_ref, gnear_ref, gaway_ref, cos_ref, sin_ref,
                     dq_ref, dk_ref, dv_ref,
                     pick, ka, va, kt, qt, dt, go, delta, dkacc, dvacc, dqt, augt):
    rows = q_ref.shape[0]
    half = gnear_ref.shape[0]

    @pl.when(pl.program_id(0) == 0)
    def _():
        def fill(i, carry):
            span = pl.ds(pl.multiple_of(i * block, block), block)
            pick[span, :] = (
                lax.broadcasted_iota(jnp.int32, (block, rows), 1) == idx_ref[span, :]
            ).astype(BF)
            return carry

        lax.fori_loop(0, rows // block, fill, 0)
        lanes = lax.broadcasted_iota(jnp.int32, (rows, PAIR), 1)
        ones = ((lanes == seg_col_ref[...]) | (lanes >= SEG_COUNT)).astype(BF)
        ka[:, PAIR:] = ones
        va[:, PAIR:] = jnp.ones((rows, PAIR), BF)
        places = lax.broadcasted_iota(jnp.int32, (8, rows), 0)
        augt[...] = jnp.where(
            (places < SEG_COUNT) & (places != seg_row_ref[...]), -FAR, 0.0
        )

    ka[:, :PAIR] = k_ref[...]
    va[:, :PAIR] = v_ref[...]
    kt[...] = k_ref[...].T
    qt[...] = q_ref[...].T
    grad = dot(pick[:, :half], gnear_ref[...]) + dot(pick[:, half:], gaway_ref[...])
    go[...] = grad.astype(BF)
    dt[...] = go[...].T
    weighed = dt[...].astype(F32) * ctxt_ref[...].astype(F32)
    delta[0:1, :] = jnp.sum(weighed[:HEAD], axis=0, keepdims=True)
    delta[1:2, :] = jnp.sum(weighed[HEAD:], axis=0, keepdims=True)
    dkacc[...] = jnp.zeros_like(dkacc)
    dvacc[...] = jnp.zeros_like(dvacc)
    empty = jnp.zeros((HEAD, block), BF)
    blank = jnp.zeros((PAIR - 16, block), BF)
    wide = lax.broadcasted_iota(jnp.int32, (block, PAIR), 1)
    zero = jnp.zeros((block, PAIR), BF)

    def thirds(row, start):
        first = row.astype(BF).astype(F32)
        second = (row - first).astype(BF).astype(F32)
        third = row - first - second
        places = lax.broadcasted_iota(jnp.int32, (16, block), 0)
        return jnp.where(places == start, first,
                         jnp.where(places == start + 1, second,
                                   jnp.where(places == start + 2, third, 0.0)))

    def step(i, carry):
        span = pl.ds(pl.multiple_of(i * block, block), block)
        base = jnp.concatenate([augt[:, span], jnp.zeros((8, block), F32)], axis=0)
        for h in range(2):
            part = slice(h * HEAD, (h + 1) * HEAD)
            low = (base + thirds(-lse_ref[0, h:h + 1, span], SEG_COUNT)).astype(BF)
            mine = qt[part, span]
            order = (mine, empty) if h == 0 else (empty, mine)
            scores = dot(ka[...], jnp.concatenate(order + (low, blank), axis=0))
            probs = jnp.exp2(scores)
            low = thirds(-delta[h:h + 1, span], 0).astype(BF)
            mine = dt[part, span]
            order = (mine, empty) if h == 0 else (empty, mine)
            slope = dot(va[...], jnp.concatenate(order + (low, blank), axis=0))
            grads = (probs * slope).astype(BF)
            keep = wide < HEAD if h == 0 else wide >= HEAD
            dvacc[...] += dot(probs.astype(BF), jnp.where(keep, go[span, :], zero))
            dkacc[...] += dot(grads, jnp.where(keep, q_ref[span, :], zero))
            dqt[part, span] = dot(kt[part, :], grads)
        return carry

    lax.fori_loop(0, rows // block, step, 0)
    cosine, sine = cos_ref[...], sin_ref[...]
    turned = dqt[...].T
    dq_ref[...] = ((turned * cosine - pair_swap(turned) * sine) * (1.0 / math.sqrt(HEAD))).astype(BF)
    turned = dkacc[...]
    dk_ref[...] = ((turned * cosine - pair_swap(turned) * sine) * LN2).astype(BF)
    dv_ref[...] = dvacc[...].astype(BF)


def attend_back(idx_col, q, k, v, seg_col, seg_row, lse, ctxt, gnear, gaway, cosine, sine, block=256):
    rows, share = q.shape
    pairs = share // PAIR
    half = rows // 2
    whole = lambda shape: pl.BlockSpec(shape, lambda j: (0,) * len(shape))
    column = lambda n: pl.BlockSpec((n, PAIR), lambda j: (0, j))
    return pl.pallas_call(
        functools.partial(attend_back_body, block),
        grid=(pairs,),
        in_specs=[whole((rows, 1)), column(rows), column(rows), column(rows),
                  whole((rows, 1)), whole((1, rows)),
                  pl.BlockSpec((1, 8, rows), lambda j: (j, 0, 0)),
                  pl.BlockSpec((PAIR, rows), lambda j: (j, 0)),
                  column(half), column(half), whole(cosine.shape), whole(sine.shape)],
        out_specs=[column(rows)] * 3,
        out_shape=[jax.ShapeDtypeStruct((rows, share), BF)] * 3,
        scratch_shapes=[pltpu.VMEM((rows, rows), BF), pltpu.VMEM((rows, 2 * PAIR), BF),
                        pltpu.VMEM((rows, 2 * PAIR), BF), pltpu.VMEM((PAIR, rows), BF),
                        pltpu.VMEM((PAIR, rows), BF), pltpu.VMEM((PAIR, rows), BF),
                        pltpu.VMEM((rows, PAIR), BF), pltpu.VMEM((8, rows), F32),
                        pltpu.VMEM((rows, PAIR), F32), pltpu.VMEM((rows, PAIR), F32),
                        pltpu.VMEM((PAIR, rows), F32), pltpu.VMEM((8, rows), F32)],
        compiler_params=pltpu.CompilerParams(vmem_limit_bytes=60 << 20),
        cost_estimate=pl.CostEstimate(
            flops=pairs * 2 * 2 * rows * rows * 7 * PAIR, bytes_accessed=2 * 9 * rows * share,
            transcendentals=2 * pairs * rows * rows,
        ),
        name="attend_back",
    )(idx_col, q, k, v, seg_col, seg_row, lse, ctxt, gnear, gaway, cosine, sine)


def project_back_body(block, rows, xw_ref, dq_ref, dk_ref, dv_ref, row_ref, wq_ref, wk_ref, wv_ref,
                      near_ref, away_ref, gw_ref, gb_ref, work):
    half = near_ref.shape[1]
    share = dq_ref.shape[2]
    batch = pl.program_id(0)

    @pl.when(batch == 0)
    def _():
        gw_ref[...] = jnp.zeros_like(gw_ref)
        gb_ref[...] = jnp.zeros_like(gb_ref)

    def step(i, carry):
        span = pl.ds(pl.multiple_of(i * block, block), block)
        total = None
        for place, (g_ref, w_ref) in enumerate(((dq_ref, wq_ref), (dk_ref, wk_ref), (dv_ref, wv_ref))):
            piece = g_ref[0, span, :]
            cols = slice(place * share, (place + 1) * share)
            gb_ref[0:1, cols] += jnp.sum(piece.astype(F32), axis=0, keepdims=True)
            term = dot_rt(piece, w_ref[...])
            total = term if total is None else total + term
        work[span, :] = total.astype(BF)
        return carry

    lax.fori_loop(0, rows // block, step, 0)
    for place, g_ref in enumerate((dq_ref, dk_ref, dv_ref)):
        cols = slice(place * share, (place + 1) * share)
        gw_ref[:, cols] += dot_lt(xw_ref[0], g_ref[0])
    small = block // 2

    def back(i, carry):
        span = pl.ds(pl.multiple_of(i * small, small), small)
        for base, out_ref in ((0, near_ref), (half, away_ref)):
            pick = (lax.broadcasted_iota(jnp.int32, (small, rows), 0) + (base + i * small) == row_ref[0]).astype(BF)
            out_ref[0, span, :] = dot(pick, work[...]).astype(BF)
        return carry

    lax.fori_loop(0, half // small, back, 0)


def project_back(xw, dq, dk, dv, idx_row, w_qkv, part, block=256):
    batches, rows, width = xw.shape
    share = dq.shape[2]
    parts = w_qkv.shape[1] // (3 * share)
    half = rows // 2
    each = lambda shape: pl.BlockSpec((1,) + shape, lambda b, p: (b,) + (0,) * len(shape))
    fixed = lambda shape: pl.BlockSpec(shape, lambda b, p: (0,) * len(shape))
    return pl.pallas_call(
        lambda part_ref, *refs: project_back_body(block, rows, *refs),
        grid_spec=pltpu.PrefetchScalarGridSpec(
            num_scalar_prefetch=1,
            grid=(batches,),
            in_specs=[each((rows, width)), each((rows, share)), each((rows, share)), each((rows, share)),
                      each((1, rows)),
                      pl.BlockSpec((width, share), lambda b, p: (0, p[0])),
                      pl.BlockSpec((width, share), lambda b, p: (0, parts + p[0])),
                      pl.BlockSpec((width, share), lambda b, p: (0, 2 * parts + p[0]))],
            out_specs=[each((half, width)), each((half, width)), fixed((width, 3 * share)),
                       fixed((8, 3 * share))],
            scratch_shapes=[pltpu.VMEM((rows, width), BF)],
        ),
        out_shape=[jax.ShapeDtypeStruct((batches, half, width), BF),
                   jax.ShapeDtypeStruct((batches, half, width), BF),
                   jax.ShapeDtypeStruct((width, 3 * share), F32),
                   jax.ShapeDtypeStruct((8, 3 * share), F32)],
        compiler_params=pltpu.CompilerParams(vmem_limit_bytes=60 << 20),
        cost_estimate=pl.CostEstimate(
            flops=2 * batches * rows * width * (rows + 6 * share),
            bytes_accessed=2 * batches * rows * (2 * width + 3 * share) + 12 * width * share,
            transcendentals=0,
        ),
        name="project_back",
    )(part, xw, dq, dk, dv, idx_row, w_qkv, w_qkv, w_qkv)


EPS = 1e-6
ERF_SCALE = 0.3275911


def gauss_parts(u):
    return jax.nn.gelu(u, approximate=False), 0.5 * (1.0 + lax.erf(u * math.sqrt(0.5))) + u * jnp.exp(
        -0.5 * u * u
    ) * (1.0 / math.sqrt(2.0 * math.pi))


def positions(segments):
    places = jnp.arange(segments.shape[0], dtype=jnp.int32)
    counts = jnp.sum(
        segments[None, :] < segments[:, None], axis=1, dtype=jnp.int32
    )
    return (places - counts).astype(F32)


def turn_tables(segments):
    halves = HEAD // 2
    freqs = jnp.exp(jnp.arange(halves, dtype=F32) * (-2.0 * math.log(10000.0) / HEAD))
    phase = positions(segments)[:, None] * freqs[None, :]
    cosine = jnp.tile(jnp.repeat(jnp.cos(phase), 2, axis=1), (1, 2))
    signs = jnp.tile(jnp.array([-1.0, 1.0], F32), halves)[None, :]
    sine = jnp.tile(jnp.repeat(jnp.sin(phase), 2, axis=1) * signs, (1, 2))
    return cosine, sine


def standard(hidden):
    centre = hidden - jnp.mean(hidden, axis=-1, keepdims=True)
    root = lax.rsqrt(jnp.mean(centre * centre, axis=-1, keepdims=True) + EPS)
    return centre * root, root


def standard_back(grad, norm, root):
    return root * (
        grad
        - jnp.mean(grad, axis=-1, keepdims=True)
        - norm * jnp.mean(grad * norm, axis=-1, keepdims=True)
    )


def swap_cores(value):
    return lax.ppermute(value, "seq", [(0, 1), (1, 0)])


def on_device(tokens, permutation, segment_ids, cotangent, *shards):
    batches = tokens.shape[0]
    half, width = tokens.shape[2], tokens.shape[3]
    core = lax.axis_index("seq")
    rows = 2 * half
    share = width // 2
    owners = 2 * lax.axis_size("fsdp")
    both = ("seq", "fsdp")
    gather = lambda value: lax.all_gather(value, both, axis=0, tiled=True)
    thin = [i for i, piece in enumerate(shards) if piece.ndim == 1]
    sizes = [shards[i].shape[0] for i in thin]
    count = sum(sizes)
    room = -(-count // 128) * 128
    packed = jnp.concatenate([shards[i] for i in thin] + [jnp.zeros((room - count,), BF)])
    w_qkv = gather(shards[0])
    vectors = gather(packed.reshape(1, room)).astype(F32)
    w_out = gather(shards[2])
    w_up = gather(shards[6])
    w_down = gather(shards[8])
    spread, at = [], 0
    for size in sizes:
        spread.append(vectors[:, at:at + size].reshape(1, owners * size))
        at += size
    b_qkv, b_out, gain_one, shift_one, b_up, b_down, gain_two, shift_two = spread
    bias_own = jnp.concatenate(
        [lax.dynamic_slice_in_dim(b_qkv, core * share + s * width, share, 1) for s in range(3)], axis=1
    )
    part = jnp.full((1,), core, jnp.int32)
    away_tokens = swap_cores(tokens[:, 0])
    kept = []
    for b in range(batches):
        order = permutation[b, 0]
        owner_half = order // half
        place = jnp.where(owner_half == core, order - core * half, order - (1 - core) * half + half)
        segments = segment_ids[b, 0]
        cosine, sine = turn_tables(segments)
        col, row = segments[:, None], segments[None, :]
        idx_col, idx_row = place[:, None], place[None, :]
        xw, q, k, v = project(idx_col, tokens[b, 0], away_tokens[b], w_qkv, bias_own, cosine, sine, part)
        near, away, ctxt, lse = attend(idx_col, q, k, v, col, row)
        kept.append((idx_col, idx_row, col, row, cosine, sine, xw, q, k, v, ctxt, lse, near, swap_cores(away)))
    near = jnp.concatenate([item[12] for item in kept], axis=0)
    away = jnp.concatenate([item[13] for item in kept], axis=0)
    context = jnp.concatenate(
        [jnp.where(core == 0, near, away), jnp.where(core == 0, away, near)], axis=1
    )
    own = tokens[:, 0].reshape(batches * half, width).astype(F32)
    norm_one, root_one = standard(own + dot(context, w_out) + b_out)
    first = norm_one * gain_one + shift_one
    first_low = first.astype(BF)
    active, slope = gauss_parts(dot(first_low, w_up) + b_up)
    active, slope = active.astype(BF), slope.astype(BF)
    norm_two, root_two = standard(first + dot(active, w_down) + b_down)
    outputs = (norm_two * gain_two + shift_two).astype(BF)
    grad_out = cotangent[:, 0].reshape(batches * half, width).astype(F32)
    g_gain_two = jnp.sum(grad_out * norm_two, axis=0)
    g_shift_two = jnp.sum(grad_out, axis=0)
    grad_two = standard_back(grad_out * gain_two, norm_two, root_two)
    low_two = grad_two.astype(BF)
    g_down = dot_lt(active, low_two)
    g_b_down = jnp.sum(low_two.astype(F32), axis=0)
    grad_up = (dot_rt(low_two, w_down) * slope.astype(F32)).astype(BF)
    g_up = dot_lt(first_low, grad_up)
    g_b_up = jnp.sum(grad_up.astype(F32), axis=0)
    grad_first = grad_two + dot_rt(grad_up, w_up)
    g_gain_one = jnp.sum(grad_first * norm_one, axis=0)
    g_shift_one = jnp.sum(grad_first, axis=0)
    grad_one = standard_back(grad_first * gain_one, norm_one, root_one)
    low_one = grad_one.astype(BF)
    g_out = dot_lt(context, low_one)
    g_b_out = jnp.sum(low_one.astype(F32), axis=0)
    grad_ctx = dot_rt(low_one, w_out).astype(BF)
    ctx_near = jnp.where(core == 0, grad_ctx[:, :share], grad_ctx[:, share:])
    ctx_away = swap_cores(jnp.where(core == 0, grad_ctx[:, share:], grad_ctx[:, :share]))
    scatter = lambda value, axes: lax.psum_scatter(value, axes, scatter_dimension=0, tiled=True)
    g_down = scatter(g_down.astype(BF), both).astype(F32)
    g_up = scatter(g_up.astype(BF), both).astype(F32)
    g_out = scatter(g_out.astype(BF), both).astype(F32)
    backs = []
    for b in range(batches):
        idx_col, idx_row, col, row, cosine, sine, xw, q, k, v, ctxt, lse = kept[b][:12]
        span = slice(b * half, (b + 1) * half)
        backs.append(
            attend_back(idx_col, q, k, v, col, row, lse, ctxt, ctx_near[span], ctx_away[span], cosine, sine)
        )
    stack = lambda pick: jnp.stack([pick(b) for b in range(batches)])
    near_grad, away_grad, gw_own, gb_own = project_back(
        stack(lambda b: kept[b][6]),
        stack(lambda b: backs[b][0]),
        stack(lambda b: backs[b][1]),
        stack(lambda b: backs[b][2]),
        stack(lambda b: kept[b][1]),
        w_qkv,
        part,
    )
    other = swap_cores(away_grad)
    token_grad = (
        grad_one.reshape(batches, half, width) + near_grad.astype(F32) + other.astype(F32)
    ).astype(BF)
    mine = lax.dynamic_slice_in_dim(gw_own, core * share, share, 0).astype(BF)
    theirs = swap_cores(lax.dynamic_slice_in_dim(gw_own, (1 - core) * share, share, 0).astype(BF))
    columns, thin_columns = [], []
    blank = jnp.zeros((share,), F32)
    for s in range(3):
        span = slice(s * share, (s + 1) * share)
        columns += [jnp.where(core == 0, mine[:, span], theirs[:, span]),
                    jnp.where(core == 0, theirs[:, span], mine[:, span])]
        thin_columns += [jnp.where(core == 0, gb_own[0, span], blank),
                         jnp.where(core == 0, blank, gb_own[0, span])]
    g_qkv = scatter(jnp.concatenate(columns, axis=1), "fsdp").astype(F32)
    thin_grads = [jnp.concatenate(thin_columns), g_b_out, g_gain_one, g_shift_one, g_b_up, g_b_down,
                  g_gain_two, g_shift_two]
    slab = jnp.concatenate(
        [value.reshape(owners, -1) for value in thin_grads]
        + [jnp.zeros((owners, 1024 - count), F32)], axis=1
    )
    slab = scatter(slab.reshape(owners * 8, 128), both).reshape(1024)
    thin_out, at = [], 0
    for size in sizes:
        thin_out.append(slab[at:at + size])
        at += size
    g_bqkv, g_bout, g_g1, g_s1, g_bup, g_bdown, g_g2, g_s2 = thin_out
    return (
        outputs.reshape(batches, 1, half, width), token_grad[:, None],
        g_qkv, g_bqkv, g_out, g_bout, g_g1, g_s1, g_up, g_bup, g_down, g_bdown, g_g2, g_s2,
    )


def solution(mesh):
    packs = P(None, "fsdp", "seq", None)
    ids = P(None, "fsdp", None)
    deep, flat = P(("seq", "fsdp"), None), P(("seq", "fsdp"))
    layers = (deep, flat, deep, flat, flat, flat, deep, flat, deep, flat, flat, flat)
    return jax.shard_map(
        on_device, mesh=mesh, in_specs=(packs, ids, ids, packs) + layers,
        out_specs=(packs, packs) + layers, check_vma=False,
    )
```

```python
import functools
import math

import jax
import jax.numpy as jnp
from jax import lax
from jax.experimental import pallas as pl
from jax.experimental.pallas import tpu as pltpu
from jax.sharding import PartitionSpec as P

HEAD = 64
PAIR = 2 * HEAD
SEG_COUNT = 4
LOG2E = math.log2(math.e)
LN2 = math.log(2.0)
FAR = float(2**30)
BF = jnp.bfloat16
F32 = jnp.float32


def dot(left, right):
    return jnp.dot(left, right, preferred_element_type=F32)


def dot_rt(left, right):
    return lax.dot_general(left, right, (((1,), (1,)), ((), ())), preferred_element_type=F32)


def dot_lt(left, right):
    return lax.dot_general(left, right, (((0,), (0,)), ((), ())), preferred_element_type=F32)


def pair_swap(values):
    lanes = lax.broadcasted_iota(jnp.int32, values.shape, 1)
    width = values.shape[1]
    return jnp.where(
        lanes % 2 == 0, pltpu.roll(values, width - 1, 1), pltpu.roll(values, 1, 1)
    )


def arrange_body(block, idx_ref, own_ref, other_ref, xw_ref):
    half = own_ref.shape[0]

    def step(i, carry):
        rows = pl.ds(pl.multiple_of(i * block, block), block)
        picks = lax.broadcasted_iota(jnp.int32, (block, half), 1)
        source = idx_ref[rows, :]
        near = (picks == source).astype(BF)
        away = (picks + half == source).astype(BF)
        xw_ref[rows, :] = (dot(near, own_ref[...]) + dot(away, other_ref[...])).astype(BF)
        return carry

    lax.fori_loop(0, idx_ref.shape[0] // block, step, 0)


def arrange(idx_col, own, other, block=256):
    rows, width = idx_col.shape[0], own.shape[1]
    return pl.pallas_call(
        functools.partial(arrange_body, block),
        out_shape=jax.ShapeDtypeStruct((rows, width), BF),
        compiler_params=pltpu.CompilerParams(vmem_limit_bytes=40 << 20),
        cost_estimate=pl.CostEstimate(
            flops=2 * rows * rows * width, bytes_accessed=4 * rows * width, transcendentals=0
        ),
        name="arrange",
    )(idx_col, own, other)


def own_columns(core, near_ref, away_ref, hold, sems):
    span, share = near_ref.shape[0], hold.shape[1] // 3
    copies = []
    for s in range(3):
        for t, ref in enumerate((near_ref, away_ref)):
            side = core if t == 0 else 1 - core
            copies.append(
                pltpu.make_async_copy(
                    ref.at[:, pl.ds(pl.multiple_of(core * share + 2 * s * share, 128), share)],
                    hold.at[pl.ds(pl.multiple_of(side * span, 128), span), s * share:(s + 1) * share],
                    sems.at[2 * s + t],
                )
            )
    for copy in copies:
        copy.start()
    return copies


def project_body(block, part_ref, xw_ref, near_ref, away_ref, bias_ref, cos_ref, sin_ref,
                 q_ref, k_ref, v_ref, hold, sems):
    share = q_ref.shape[1]
    for copy in own_columns(part_ref[0], near_ref, away_ref, hold, sems):
        copy.wait()

    def step(i, carry):
        rows = pl.ds(pl.multiple_of(i * block, block), block)
        work = xw_ref[rows, :]
        cosine, sine = cos_ref[rows, :], sin_ref[rows, :]
        for out_ref, place, scale in ((q_ref, 0, LOG2E / math.sqrt(HEAD)), (k_ref, 1, 1.0)):
            whole = slice(place * share, (place + 1) * share)
            pre = dot(work, hold[:, whole]) + bias_ref[:, whole]
            for j in range(share // PAIR):
                cols = slice(j * PAIR, (j + 1) * PAIR)
                piece = pre[:, cols]
                out_ref[rows, cols] = (
                    (piece * cosine + pair_swap(piece) * sine) * scale
                ).astype(BF)
        v_ref[rows, :] = (dot(work, hold[:, 2 * share:]) + bias_ref[:, 2 * share:]).astype(BF)
        return carry

    lax.fori_loop(0, xw_ref.shape[0] // block, step, 0)


def project(part, xw, near_w, away_w, bias_own, cosine, sine, block=256):
    rows, width = xw.shape
    share = bias_own.shape[1] // 3
    vmem, smem, anywhere = (pl.BlockSpec(memory_space=s) for s in (pltpu.VMEM, pltpu.SMEM, pl.ANY))
    return pl.pallas_call(
        functools.partial(project_body, block),
        in_specs=[smem, vmem, anywhere, anywhere, vmem, vmem, vmem],
        out_shape=[jax.ShapeDtypeStruct((rows, share), BF)] * 3,
        scratch_shapes=[pltpu.VMEM((width, 3 * share), BF), pltpu.SemaphoreType.DMA((6,))],
        compiler_params=pltpu.CompilerParams(vmem_limit_bytes=40 << 20),
        cost_estimate=pl.CostEstimate(
            flops=2 * rows * width * 3 * share,
            bytes_accessed=2 * (rows * width + 3 * width * share + 3 * rows * share),
            transcendentals=0,
        ),
        name="project",
    )(part, xw, near_w, away_w, bias_own, cosine, sine)


def attend_body(block, idx_ref, q_ref, k_ref, v_ref, seg_col_ref, seg_row_ref,
                near_ref, away_ref, ctxt_ref, lse_ref, pick, ka, vt, qt, augt):
    rows = q_ref.shape[0]
    half = near_ref.shape[0]

    @pl.when(pl.program_id(0) == 0)
    def _():
        def fill(i, carry):
            span = pl.ds(pl.multiple_of(i * block, block), block)
            pick[span, :] = (
                lax.broadcasted_iota(jnp.int32, (block, rows), 1) == idx_ref[span, :]
            ).astype(BF)
            return carry

        lax.fori_loop(0, rows // block, fill, 0)
        lanes = lax.broadcasted_iota(jnp.int32, (rows, PAIR), 1)
        ka[:, PAIR:] = ((lanes == seg_col_ref[...]) | (lanes >= SEG_COUNT)).astype(BF)
        places = lax.broadcasted_iota(jnp.int32, (PAIR, rows), 0)
        augt[...] = jnp.where(
            (places < SEG_COUNT) & (places != seg_row_ref[...]), -FAR, 0.0
        ).astype(BF)

    ka[:, :PAIR] = k_ref[...]
    vt[...] = v_ref[...].T
    qt[...] = q_ref[...].T
    empty = jnp.zeros((HEAD, block), BF)

    def step(i, carry):
        span = pl.ds(pl.multiple_of(i * block, block), block)
        extra = augt[:, span]
        for h in range(2):
            mine = qt[h * HEAD:(h + 1) * HEAD, span]
            mixed = jnp.concatenate([mine, empty, extra] if h == 0 else [empty, mine, extra], axis=0)
            scores = dot(ka[...], mixed)
            top = jnp.max(scores, axis=0, keepdims=True)
            expo = jnp.exp2(scores - top)
            total = jnp.sum(expo, axis=0, keepdims=True)
            context = dot(vt[h * HEAD:(h + 1) * HEAD, :], expo.astype(BF))
            ctxt_ref[h * HEAD:(h + 1) * HEAD, span] = (context / total).astype(BF)
            lse_ref[0, h:h + 1, span] = top + jnp.log2(total)
        return carry

    lax.fori_loop(0, rows // block, step, 0)
    given = dot(ctxt_ref[...], pick[...]).astype(BF)
    near_ref[...] = given[:, :half].T
    away_ref[...] = given[:, half:].T


def attend(idx_col, q, k, v, seg_col, seg_row, block=256):
    rows, share = q.shape
    pairs = share // PAIR
    half = rows // 2
    whole = lambda shape: pl.BlockSpec(shape, lambda j: (0,) * len(shape))
    column = lambda n: pl.BlockSpec((n, PAIR), lambda j: (0, j))
    return pl.pallas_call(
        functools.partial(attend_body, block),
        grid=(pairs,),
        in_specs=[whole((rows, 1)), column(rows), column(rows), column(rows),
                  whole((rows, 1)), whole((1, rows))],
        out_specs=[column(half), column(half), pl.BlockSpec((PAIR, rows), lambda j: (j, 0)),
                   pl.BlockSpec((1, 8, rows), lambda j: (j, 0, 0))],
        out_shape=[jax.ShapeDtypeStruct((half, share), BF), jax.ShapeDtypeStruct((half, share), BF),
                   jax.ShapeDtypeStruct((share, rows), BF),
                   jax.ShapeDtypeStruct((pairs, 8, rows), F32)],
        scratch_shapes=[pltpu.VMEM((rows, rows), BF), pltpu.VMEM((rows, 2 * PAIR), BF),
                        pltpu.VMEM((PAIR, rows), BF), pltpu.VMEM((PAIR, rows), BF),
                        pltpu.VMEM((PAIR, rows), BF)],
        compiler_params=pltpu.CompilerParams(vmem_limit_bytes=60 << 20),
        cost_estimate=pl.CostEstimate(
            flops=pairs * 2 * 2 * rows * rows * 3 * PAIR, bytes_accessed=2 * 6 * rows * share,
            transcendentals=2 * pairs * rows * rows,
        ),
        name="attend",
    )(idx_col, q, k, v, seg_col, seg_row)


def attend_back_body(block, idx_ref, q_ref, k_ref, v_ref, seg_col_ref, seg_row_ref, lse_ref,
                     ctxt_ref, gnear_ref, gaway_ref, cos_ref, sin_ref,
                     dq_ref, dk_ref, dv_ref,
                     pick, ka, va, kt, qt, dt, go, delta, dkacc, dvacc, dqt, augt):
    rows = q_ref.shape[0]
    half = gnear_ref.shape[0]

    @pl.when(pl.program_id(0) == 0)
    def _():
        def fill(i, carry):
            span = pl.ds(pl.multiple_of(i * block, block), block)
            pick[span, :] = (
                lax.broadcasted_iota(jnp.int32, (block, rows), 1) == idx_ref[span, :]
            ).astype(BF)
            return carry

        lax.fori_loop(0, rows // block, fill, 0)
        lanes = lax.broadcasted_iota(jnp.int32, (rows, PAIR), 1)
        ones = ((lanes == seg_col_ref[...]) | (lanes >= SEG_COUNT)).astype(BF)
        ka[:, PAIR:] = ones
        va[:, PAIR:] = jnp.ones((rows, PAIR), BF)
        places = lax.broadcasted_iota(jnp.int32, (8, rows), 0)
        augt[...] = jnp.where(
            (places < SEG_COUNT) & (places != seg_row_ref[...]), -FAR, 0.0
        )

    ka[:, :PAIR] = k_ref[...]
    va[:, :PAIR] = v_ref[...]
    kt[...] = k_ref[...].T
    qt[...] = q_ref[...].T
    grad = dot(pick[:, :half], gnear_ref[...]) + dot(pick[:, half:], gaway_ref[...])
    go[...] = grad.astype(BF)
    dt[...] = go[...].T
    weighed = dt[...].astype(F32) * ctxt_ref[...].astype(F32)
    delta[0:1, :] = jnp.sum(weighed[:HEAD], axis=0, keepdims=True)
    delta[1:2, :] = jnp.sum(weighed[HEAD:], axis=0, keepdims=True)
    dkacc[...] = jnp.zeros_like(dkacc)
    dvacc[...] = jnp.zeros_like(dvacc)
    empty = jnp.zeros((HEAD, block), BF)
    blank = jnp.zeros((PAIR - 16, block), BF)
    wide = lax.broadcasted_iota(jnp.int32, (block, PAIR), 1)
    zero = jnp.zeros((block, PAIR), BF)

    def thirds(row, start):
        first = row.astype(BF).astype(F32)
        second = (row - first).astype(BF).astype(F32)
        third = row - first - second
        places = lax.broadcasted_iota(jnp.int32, (16, block), 0)
        return jnp.where(places == start, first,
                         jnp.where(places == start + 1, second,
                                   jnp.where(places == start + 2, third, 0.0)))

    def step(i, carry):
        span = pl.ds(pl.multiple_of(i * block, block), block)
        base = jnp.concatenate([augt[:, span], jnp.zeros((8, block), F32)], axis=0)
        for h in range(2):
            part = slice(h * HEAD, (h + 1) * HEAD)
            low = (base + thirds(-lse_ref[0, h:h + 1, span], SEG_COUNT)).astype(BF)
            mine = qt[part, span]
            order = (mine, empty) if h == 0 else (empty, mine)
            scores = dot(ka[...], jnp.concatenate(order + (low, blank), axis=0))
            probs = jnp.exp2(scores)
            low = thirds(-delta[h:h + 1, span], 0).astype(BF)
            mine = dt[part, span]
            order = (mine, empty) if h == 0 else (empty, mine)
            slope = dot(va[...], jnp.concatenate(order + (low, blank), axis=0))
            grads = (probs * slope).astype(BF)
            keep = wide < HEAD if h == 0 else wide >= HEAD
            dvacc[...] += dot(probs.astype(BF), jnp.where(keep, go[span, :], zero))
            dkacc[...] += dot(grads, jnp.where(keep, q_ref[span, :], zero))
            dqt[part, span] = dot(kt[part, :], grads)
        return carry

    lax.fori_loop(0, rows // block, step, 0)
    cosine, sine = cos_ref[...], sin_ref[...]
    turned = dqt[...].T
    dq_ref[...] = ((turned * cosine - pair_swap(turned) * sine) * (1.0 / math.sqrt(HEAD))).astype(BF)
    turned = dkacc[...]
    dk_ref[...] = ((turned * cosine - pair_swap(turned) * sine) * LN2).astype(BF)
    dv_ref[...] = dvacc[...].astype(BF)


def attend_back(idx_col, q, k, v, seg_col, seg_row, lse, ctxt, gnear, gaway, cosine, sine, block=256):
    rows, share = q.shape
    pairs = share // PAIR
    half = rows // 2
    whole = lambda shape: pl.BlockSpec(shape, lambda j: (0,) * len(shape))
    column = lambda n: pl.BlockSpec((n, PAIR), lambda j: (0, j))
    return pl.pallas_call(
        functools.partial(attend_back_body, block),
        grid=(pairs,),
        in_specs=[whole((rows, 1)), column(rows), column(rows), column(rows),
                  whole((rows, 1)), whole((1, rows)),
                  pl.BlockSpec((1, 8, rows), lambda j: (j, 0, 0)),
                  pl.BlockSpec((PAIR, rows), lambda j: (j, 0)),
                  column(half), column(half), whole(cosine.shape), whole(sine.shape)],
        out_specs=[column(rows)] * 3,
        out_shape=[jax.ShapeDtypeStruct((rows, share), BF)] * 3,
        scratch_shapes=[pltpu.VMEM((rows, rows), BF), pltpu.VMEM((rows, 2 * PAIR), BF),
                        pltpu.VMEM((rows, 2 * PAIR), BF), pltpu.VMEM((PAIR, rows), BF),
                        pltpu.VMEM((PAIR, rows), BF), pltpu.VMEM((PAIR, rows), BF),
                        pltpu.VMEM((rows, PAIR), BF), pltpu.VMEM((8, rows), F32),
                        pltpu.VMEM((rows, PAIR), F32), pltpu.VMEM((rows, PAIR), F32),
                        pltpu.VMEM((PAIR, rows), F32), pltpu.VMEM((8, rows), F32)],
        compiler_params=pltpu.CompilerParams(vmem_limit_bytes=60 << 20),
        cost_estimate=pl.CostEstimate(
            flops=pairs * 2 * 2 * rows * rows * 7 * PAIR, bytes_accessed=2 * 9 * rows * share,
            transcendentals=2 * pairs * rows * rows,
        ),
        name="attend_back",
    )(idx_col, q, k, v, seg_col, seg_row, lse, ctxt, gnear, gaway, cosine, sine)


def project_back_body(block, part_ref, xw_ref, dq_ref, dk_ref, dv_ref, row_ref, wnear_ref, waway_ref,
                      near_ref, away_ref, work, hold, sems):
    rows, share = dq_ref.shape[1], dq_ref.shape[2]
    half = near_ref.shape[1]

    @pl.when(pl.program_id(0) == 0)
    def _():
        for copy in own_columns(part_ref[0], wnear_ref, waway_ref, hold, sems):
            copy.wait()

    def step(i, carry):
        span = pl.ds(pl.multiple_of(i * block, block), block)
        total = None
        for place, g_ref in enumerate((dq_ref, dk_ref, dv_ref)):
            term = dot_rt(g_ref[0, span, :], hold[:, place * share:(place + 1) * share])
            total = term if total is None else total + term
        work[span, :] = total.astype(BF)
        return carry

    lax.fori_loop(0, rows // block, step, 0)
    small = block // 2

    def back(i, carry):
        span = pl.ds(pl.multiple_of(i * small, small), small)
        for base, out_ref in ((0, near_ref), (half, away_ref)):
            pick = (lax.broadcasted_iota(jnp.int32, (small, rows), 0) + (base + i * small) == row_ref[0]).astype(BF)
            out_ref[0, span, :] = dot(pick, work[...]).astype(BF)
        return carry

    lax.fori_loop(0, half // small, back, 0)


def project_back(part, xw, dq, dk, dv, idx_row, near_w, away_w, block=256):
    batches, rows, width = xw.shape
    share = dq.shape[2]
    half = rows // 2
    each = lambda shape: pl.BlockSpec((1,) + shape, lambda b: (b,) + (0,) * len(shape))
    anywhere = pl.BlockSpec(memory_space=pl.ANY)
    return pl.pallas_call(
        functools.partial(project_back_body, block),
        grid=(batches,),
        in_specs=[pl.BlockSpec(memory_space=pltpu.SMEM), each((rows, width)), each((rows, share)),
                  each((rows, share)), each((rows, share)), each((1, rows)), anywhere, anywhere],
        out_specs=[each((half, width)), each((half, width))],
        scratch_shapes=[pltpu.VMEM((rows, width), BF), pltpu.VMEM((width, 3 * share), BF),
                        pltpu.SemaphoreType.DMA((6,))],
        out_shape=[jax.ShapeDtypeStruct((batches, half, width), BF)] * 2,
        compiler_params=pltpu.CompilerParams(vmem_limit_bytes=60 << 20),
        cost_estimate=pl.CostEstimate(
            flops=2 * batches * rows * width * (rows + 3 * share),
            bytes_accessed=2 * batches * rows * (2 * width + 3 * share) + 6 * width * share,
            transcendentals=0,
        ),
        name="project_back",
    )(part, xw, dq, dk, dv, idx_row, near_w, away_w)


def weight_back_body(xw_ref, dq_ref, dk_ref, dv_ref, gw_ref, gb_ref, acc):
    batch, share = pl.program_id(0), dq_ref.shape[2]
    for place, g_ref in enumerate((dq_ref, dk_ref, dv_ref)):
        cols = slice(place * share, (place + 1) * share)
        term = dot_lt(xw_ref[0], g_ref[0])
        thin = jnp.sum(g_ref[0].astype(F32), axis=0, keepdims=True)

        @pl.when(batch == 0)
        def _():
            acc[:, cols] = term
            gb_ref[0:1, cols] = thin

        @pl.when(batch > 0)
        def _():
            acc[:, cols] += term
            gb_ref[0:1, cols] += thin

        @pl.when(batch == pl.num_programs(0) - 1)
        def _():
            gw_ref[:, cols] = acc[:, cols].astype(BF)


def weight_back(xw, dq, dk, dv):
    batches, rows, width = xw.shape
    share = dq.shape[2]
    each = lambda shape: pl.BlockSpec((1,) + shape, lambda b: (b,) + (0,) * len(shape))
    return pl.pallas_call(
        weight_back_body,
        grid=(batches,),
        in_specs=[each((rows, width)), each((rows, share)), each((rows, share)), each((rows, share))],
        out_specs=[pl.BlockSpec((width, 3 * share), lambda b: (0, 0)),
                   pl.BlockSpec((8, 3 * share), lambda b: (0, 0))],
        out_shape=[jax.ShapeDtypeStruct((width, 3 * share), BF), jax.ShapeDtypeStruct((8, 3 * share), F32)],
        scratch_shapes=[pltpu.VMEM((width, 3 * share), F32)],
        compiler_params=pltpu.CompilerParams(vmem_limit_bytes=60 << 20),
        cost_estimate=pl.CostEstimate(
            flops=2 * batches * rows * width * 3 * share,
            bytes_accessed=2 * batches * rows * (width + 3 * share) + 6 * width * share,
            transcendentals=0,
        ),
        name="weight_back",
    )(xw, dq, dk, dv)


EPS = 1e-6
ERF_SLOPE = 0.3275911 * math.sqrt(0.5)
ERF_TERMS = (0.254829592, -0.284496736, 1.421413741, -1.453152027, 1.061405429)


def gauss_parts(u):
    bell = jnp.exp2(u * u * (-0.5 * LOG2E))
    t = 1.0 / (1.0 + ERF_SLOPE * jnp.abs(u))
    poly = 0.5 * ERF_TERMS[4]
    for term in ERF_TERMS[3::-1]:
        poly = poly * t + 0.5 * term
    tail = poly * t * bell
    below = jnp.where(u < 0.0, tail, 1.0 - tail)
    return u * below, below + u * bell * (1.0 / math.sqrt(2.0 * math.pi))


def row_mean(value):
    return jnp.sum(value, axis=1, keepdims=True) * (1.0 / value.shape[1])


def standard(hidden):
    centre = hidden - row_mean(hidden)
    root = lax.rsqrt(row_mean(centre * centre) + EPS)
    return centre * root, root


def standard_back(grad, norm, root):
    return root * (grad - row_mean(grad) - norm * row_mean(grad * norm))


def feed_body(chunk, part_ref, x_ref, near_ref, away_ref, dy_ref, thin_ref, bup_ref,
              unear_ref, uaway_ref, dnear_ref, daway_ref,
              out_ref, dh_ref, low_ref, act_ref, dup_ref, dlow_ref, da_ref, cnear_ref, caway_ref,
              sums_ref, bsum_ref, wo_near, wo_away, wup, wdown, slopes, sems):
    first_step = pl.program_id(0) == 0
    core = part_ref[0]
    width, wide = wup.shape
    share = near_ref.shape[1]
    half_w, half_f = width // 2, wide // 2

    def loads():
        copies = []
        for t, (u_ref, d_ref) in enumerate(((unear_ref, dnear_ref), (uaway_ref, daway_ref))):
            side = core if t == 0 else 1 - core
            hold = wo_near if t == 0 else wo_away
            copies += [
                pltpu.make_async_copy(u_ref.at[:, :width], hold, sems.at[t]),
                pltpu.make_async_copy(
                    u_ref.at[:, width:], wup.at[pl.ds(pl.multiple_of(side * half_w, 128), half_w), :],
                    sems.at[2 + t]),
                pltpu.make_async_copy(
                    d_ref, wdown.at[pl.ds(pl.multiple_of(side * half_f, 128), half_f), :], sems.at[4 + t]),
            ]
        return copies

    @pl.when(first_step)
    def _():
        copies = loads()
        for copy in copies:
            copy.start()
        sums_ref[...] = jnp.zeros_like(sums_ref)
        bsum_ref[...] = jnp.zeros_like(bsum_ref)
        for copy in copies:
            copy.wait()

    b_out, gain_one, shift_one, b_down, gain_two, shift_two = (thin_ref[i:i + 1, :] for i in range(6))

    def tally(row, value):
        sums_ref[row:row + 1, :] += jnp.sum(value, axis=0, keepdims=True)

    attended = dot(near_ref[...], wo_near[...]) + dot(away_ref[...], wo_away[...]) + b_out
    norm_one, root_one = standard(x_ref[...].astype(F32) + attended)
    first = norm_one * gain_one + shift_one
    low = first.astype(BF)
    low_ref[...] = low
    lowered = None
    for c in range(wide // chunk):
        cols = slice(c * chunk, (c + 1) * chunk)
        act, slope = gauss_parts(dot(low, wup[:, cols]) + bup_ref[:, cols])
        act = act.astype(BF)
        act_ref[:, cols] = act
        slopes[:, cols] = slope.astype(BF)
        term = dot(act, wdown[cols, :])
        lowered = term if lowered is None else lowered + term
    norm_two, root_two = standard(first + lowered + b_down)
    out_ref[...] = (norm_two * gain_two + shift_two).astype(BF)
    dy = dy_ref[...].astype(F32)
    tally(4, dy * norm_two)
    tally(5, dy)
    grad_two = standard_back(dy * gain_two, norm_two, root_two)
    dlow = grad_two.astype(BF)
    dlow_ref[...] = dlow
    tally(3, dlow.astype(F32))
    total = grad_two
    for c in range(wide // chunk):
        cols = slice(c * chunk, (c + 1) * chunk)
        dup = (dot_rt(dlow, wdown[cols, :]) * slopes[:, cols].astype(F32)).astype(BF)
        dup_ref[:, cols] = dup
        bsum_ref[0:1, cols] += jnp.sum(dup.astype(F32), axis=0, keepdims=True)
        total = total + dot_rt(dup, wup[:, cols])
    tally(1, total * norm_one)
    tally(2, total)
    grad_one = standard_back(total * gain_one, norm_one, root_one)
    dh_ref[...] = grad_one
    da = grad_one.astype(BF)
    da_ref[...] = da
    tally(0, da.astype(F32))
    cnear_ref[...] = dot_rt(da, wo_near[...]).astype(BF)
    caway_ref[...] = dot_rt(da, wo_away[...]).astype(BF)


def feed(part, x, near, away, dy, thin, bup, unear, uaway, dnear, daway, block=256, chunk=768):
    rows, width = x.shape
    share = near.shape[1]
    wide = bup.shape[1]
    line = lambda n: pl.BlockSpec((block, n), lambda i: (i, 0))
    fixed = lambda shape: pl.BlockSpec(shape, lambda i: (0, 0))
    anywhere = pl.BlockSpec(memory_space=pl.ANY)
    shape = lambda n, dt: jax.ShapeDtypeStruct((rows, n), dt)
    return pl.pallas_call(
        functools.partial(feed_body, chunk),
        grid=(rows // block,),
        in_specs=[pl.BlockSpec(memory_space=pltpu.SMEM), line(width), line(share), line(share), line(width),
                  fixed(thin.shape), fixed(bup.shape), anywhere, anywhere, anywhere, anywhere],
        out_specs=[line(width), line(width), line(width), line(wide), line(wide), line(width), line(width),
                   line(share), line(share), fixed((8, width)), fixed((8, wide))],
        out_shape=[shape(width, BF), shape(width, F32), shape(width, BF), shape(wide, BF), shape(wide, BF),
                   shape(width, BF), shape(width, BF), shape(share, BF), shape(share, BF),
                   jax.ShapeDtypeStruct((8, width), F32), jax.ShapeDtypeStruct((8, wide), F32)],
        scratch_shapes=[pltpu.VMEM((share, width), BF), pltpu.VMEM((share, width), BF),
                        pltpu.VMEM((width, wide), BF), pltpu.VMEM((wide, width), BF),
                        pltpu.VMEM((block, wide), BF), pltpu.SemaphoreType.DMA((6,))],
        compiler_params=pltpu.CompilerParams(vmem_limit_bytes=60 << 20),
        cost_estimate=pl.CostEstimate(
            flops=2 * rows * width * (2 * width + 4 * wide),
            bytes_accessed=2 * rows * (7 * width + 2 * wide) + 4 * width * (wide + width),
            transcendentals=2 * rows * wide,
        ),
        name="feed",
    )(part, x, near, away, dy, thin, bup, unear, uaway, dnear, daway)


def swap_cores(value):
    return lax.ppermute(value, "seq", [(0, 1), (1, 0)])


def swap_x(value):
    return lax.ppermute(value, "fsdp", [(i, i ^ 1) for i in range(16)])


def swap_y(value):
    return lax.ppermute(value, "fsdp", [(i, i ^ 2) for i in range(16)])


def shift_z(value, k):
    return lax.ppermute(value, "fsdp", [(i, (i + 4 * k) % 16) for i in range(16)])


def assemble_body(place_ref, ax_ref, ay_ref, bx_ref, by_ref, out_ref):
    place = place_ref[0]
    z, y, x = place // 4, (place // 2) % 2, place % 2
    for j in range(4):
        k, o = j % 2, j // 2
        near_z, far_z = lax.rem(z - k + 4, 4), lax.rem(z - k + 2, 4)
        flip_x = lax.rem(x + o, 2)
        flip_y = lax.rem(y + o, 2)
        out_ref[near_z * 4 + y * 2 + flip_x] = ax_ref[j]
        out_ref[near_z * 4 + (1 - y) * 2 + flip_x] = ay_ref[j]
        out_ref[far_z * 4 + flip_y * 2 + x] = by_ref[j]
        out_ref[far_z * 4 + flip_y * 2 + 1 - x] = bx_ref[j]


def assemble(place, parts):
    n, width = parts[0].shape[1:]
    vmem = pl.BlockSpec(memory_space=pltpu.VMEM)
    return pl.pallas_call(
        assemble_body,
        in_specs=[pl.BlockSpec(memory_space=pltpu.SMEM)] + [vmem] * 4,
        out_shape=jax.ShapeDtypeStruct((16, n, width), BF),
        compiler_params=pltpu.CompilerParams(vmem_limit_bytes=24 << 20),
        cost_estimate=pl.CostEstimate(flops=0, bytes_accessed=4 * 16 * n * width, transcendentals=0),
        name="assemble",
    )(place, *parts)


def gather_half(shard):
    n, width = shard.shape
    if lax.axis_size("fsdp") != 16:
        return lax.all_gather(shard, "fsdp", axis=0, tiled=True)
    first = jnp.stack([shard, shift_z(shard, 1)])
    second = jnp.stack([shift_z(shard, 2), shift_z(shard, 3)])
    first = jnp.concatenate([first, swap_x(first)], axis=0)
    second = jnp.concatenate([second, swap_y(second)], axis=0)
    place = jnp.full((1,), lax.axis_index("fsdp"), jnp.int32)
    whole = assemble(place, (first, swap_y(first), swap_x(second), second))
    return whole.reshape(16 * n, width)


def scatter_half(value):
    rows, width = value.shape
    count = lax.axis_size("fsdp")
    n = rows // count
    if count != 16:
        return lax.psum_scatter(value.astype(BF), "fsdp", scatter_dimension=0, tiled=True).astype(F32)
    place = lax.axis_index("fsdp")
    z, y, x = place // 4, (place // 2) % 2, place % 2
    cube = value.reshape(2, 2, 2, 2, n, width)
    pick = lambda part, at, axis: lax.dynamic_index_in_dim(part, at, axis, keepdims=False)
    first, second = cube[0], cube[1]
    first = pick(first, y, 1) + swap_y(pick(first, 1 - y, 1).astype(BF)).astype(F32)
    second = pick(second, x, 2) + swap_x(pick(second, 1 - x, 2).astype(BF)).astype(F32)
    first = pick(first, x, 1) + swap_x(pick(first, 1 - x, 1).astype(BF)).astype(F32)
    second = pick(second, y, 1) + swap_y(pick(second, 1 - y, 1).astype(BF)).astype(F32)
    stack = jnp.concatenate([first, second], axis=0)
    total = pick(stack, z, 0)
    for k in (1, 2, 3):
        total = total + shift_z(pick(stack, lax.rem(z + k, 4), 0).astype(BF), k).astype(F32)
    return total


def positions(segments):
    places = jnp.arange(segments.shape[0], dtype=jnp.int32)
    counts = jnp.sum(segments[None, :] < segments[:, None], axis=1, dtype=jnp.int32)
    return (places - counts).astype(F32)


def turn_tables(segments):
    halves = HEAD // 2
    freqs = jnp.exp(jnp.arange(halves, dtype=F32) * (-2.0 * math.log(10000.0) / HEAD))
    phase = positions(segments)[:, None] * freqs[None, :]
    cosine = jnp.tile(jnp.repeat(jnp.cos(phase), 2, axis=1), (1, 2))
    signs = jnp.tile(jnp.array([-1.0, 1.0], F32), halves)[None, :]
    sine = jnp.tile(jnp.repeat(jnp.sin(phase), 2, axis=1) * signs, (1, 2))
    return cosine, sine


def on_device(tokens, permutation, segment_ids, cotangent, *shards):
    batches = tokens.shape[0]
    half, width = tokens.shape[2], tokens.shape[3]
    core = lax.axis_index("seq")
    share = width // 2
    owners = 2 * lax.axis_size("fsdp")
    part = jnp.full((1,), core, jnp.int32)
    thin = [i for i, piece in enumerate(shards) if piece.ndim == 1]
    sizes = [shards[i].shape[0] for i in thin]
    count = sum(sizes)
    n_qkv = shards[0].shape[0]
    room = n_qkv * 128

    away_tokens = swap_cores(tokens[:, 0])
    packed = jnp.concatenate([shards[i] for i in thin] + [jnp.zeros((room - count,), BF)])
    q_near = gather_half(jnp.concatenate([shards[0], packed.reshape(n_qkv, 128)], axis=1))
    q_away = swap_cores(q_near)
    u_near = gather_half(jnp.concatenate([shards[2], shards[6]], axis=1))
    u_away = swap_cores(u_near)
    d_near = gather_half(shards[8])
    d_away = swap_cores(d_near)

    slabs = [value[:, 3 * width:].reshape(owners // 2, room)[:, :count] for value in (q_near, q_away)]
    vectors = jnp.concatenate(
        [jnp.where(core == 0, slabs[0], slabs[1]), jnp.where(core == 0, slabs[1], slabs[0])], axis=0
    ).astype(F32)
    spread, at = [], 0
    for size in sizes:
        spread.append(vectors[:, at:at + size].reshape(1, owners * size))
        at += size
    b_qkv, b_out, gain_one, shift_one, b_up, b_down, gain_two, shift_two = spread
    bias_own = jnp.concatenate(
        [lax.dynamic_slice_in_dim(b_qkv, core * share + s * width, share, 1) for s in range(3)], axis=1
    )
    blank_row = jnp.zeros((1, width), F32)
    thin_rows = jnp.concatenate(
        [b_out, gain_one, shift_one, b_down, gain_two, shift_two, blank_row, blank_row], axis=0
    )

    kept = []
    for b in range(batches):
        order = permutation[b, 0]
        place = jnp.where(
            order // half == core, order - core * half, order - (1 - core) * half + half
        )
        segments = segment_ids[b, 0]
        cosine, sine = turn_tables(segments)
        col, row = segments[:, None], segments[None, :]
        idx_col, idx_row = place[:, None], place[None, :]
        xw = arrange(idx_col, tokens[b, 0], away_tokens[b])
        q, k, v = project(part, xw, q_near, q_away, bias_own, cosine, sine)
        near, away, ctxt, lse = attend(idx_col, q, k, v, col, row)
        kept.append((idx_col, idx_row, col, row, cosine, sine, xw, q, k, v, ctxt, lse, near, swap_cores(away)))
    join = lambda i: jnp.concatenate([item[i] for item in kept], axis=0)
    near, away = join(12), join(13)
    (outputs, grad_one, low, act, dup, dlow, da, cnear, caway, sums, bsum) = feed(
        part, tokens[:, 0].reshape(batches * half, width), near, away,
        cotangent[:, 0].reshape(batches * half, width), thin_rows, b_up, u_near, u_away, d_near, d_away,
    )
    caway = swap_cores(caway)

    def halves(value):
        size = value.shape[0] // 2
        return (lax.dynamic_slice_in_dim(value, core * size, size, 0),
                lax.dynamic_slice_in_dim(value, (1 - core) * size, size, 0))

    def summed(value):
        mine, theirs = halves(value)
        return mine.astype(F32) + swap_cores(theirs).astype(F32)

    g_down = scatter_half(summed(dot_lt(act, dlow).astype(BF)))
    g_up = scatter_half(summed(dot_lt(low, dup).astype(BF)))
    g_out = scatter_half(
        dot_lt(near, da).astype(BF).astype(F32) + swap_cores(dot_lt(away, da).astype(BF)).astype(F32)
    )
    backs = []
    for b in range(batches):
        idx_col, idx_row, col, row, cosine, sine, xw, q, k, v, ctxt, lse = kept[b][:12]
        span = slice(b * half, (b + 1) * half)
        backs.append(
            attend_back(idx_col, q, k, v, col, row, lse, ctxt, cnear[span], caway[span], cosine, sine)
        )
    pile = lambda items: jnp.stack(items)
    xws = pile([item[6] for item in kept])
    dq, dk, dv = (pile([back[i] for back in backs]) for i in range(3))
    gw_own, gb_own = weight_back(xws, dq, dk, dv)
    mine, theirs = halves(gw_own)
    theirs = swap_cores(theirs)
    blank = jnp.zeros((share,), F32)
    columns, thin_columns = [], []
    for s in range(3):
        span = slice(s * share, (s + 1) * share)
        columns += [jnp.where(core == 0, mine[:, span], theirs[:, span]),
                    jnp.where(core == 0, theirs[:, span], mine[:, span])]
        thin_columns += [jnp.where(core == 0, gb_own[0, span], blank),
                         jnp.where(core == 0, blank, gb_own[0, span])]
    thin_grads = [jnp.concatenate(thin_columns), sums[0], sums[1], sums[2], bsum[0], sums[3], sums[4], sums[5]]
    slab = jnp.concatenate(
        [value.reshape(owners, -1) for value in thin_grads] + [jnp.zeros((owners, room - count), F32)], axis=1
    ).astype(BF).reshape(owners * n_qkv, 128)
    columns.append(summed(slab).astype(BF))
    g_qkv = scatter_half(jnp.concatenate(columns, axis=1).astype(F32))
    near_grad, away_grad = project_back(
        part, xws, dq, dk, dv, pile([item[1] for item in kept]), q_near, q_away
    )
    token_grad = (
        grad_one.reshape(batches, half, width) + near_grad.astype(F32) + swap_cores(away_grad).astype(F32)
    ).astype(BF)
    flat = g_qkv[:, 3 * width:].reshape(room)
    thin_out, at = [], 0
    for size in sizes:
        thin_out.append(flat[at:at + size])
        at += size
    g_bqkv, g_bout, g_g1, g_s1, g_bup, g_bdown, g_g2, g_s2 = thin_out
    return (
        outputs.reshape(batches, 1, half, width), token_grad[:, None],
        g_qkv[:, :3 * width], g_bqkv, g_out, g_bout, g_g1, g_s1, g_up, g_bup, g_down, g_bdown, g_g2, g_s2,
    )


def solution(mesh):
    packs = P(None, "fsdp", "seq", None)
    ids = P(None, "fsdp", None)
    deep, flat = P(("seq", "fsdp"), None), P(("seq", "fsdp"))
    layers = (deep, flat, deep, flat, flat, flat, deep, flat, deep, flat, flat, flat)
    return jax.shard_map(
        on_device, mesh=mesh, in_specs=(packs, ids, ids, packs) + layers,
        out_specs=(packs, packs) + layers, check_vma=False,
    )
```

```python
import functools
import math

import jax
import jax.numpy as jnp
from jax import lax
from jax.experimental import pallas as pl
from jax.experimental.pallas import tpu as pltpu
from jax.sharding import PartitionSpec as P

HEAD = 64
PAIR = 2 * HEAD
SEG_COUNT = 4
LONGEST = 1024
LOG2E = math.log2(math.e)
LN2 = math.log(2.0)
FAR = float(2**30)
BF = jnp.bfloat16
F32 = jnp.float32


def dot(left, right):
    return jnp.dot(left, right, preferred_element_type=F32)


def dot_rt(left, right):
    return lax.dot_general(left, right, (((1,), (1,)), ((), ())), preferred_element_type=F32)


def dot_lt(left, right):
    return lax.dot_general(left, right, (((0,), (0,)), ((), ())), preferred_element_type=F32)


def pair_swap(values):
    lanes = lax.broadcasted_iota(jnp.int32, values.shape, 1)
    width = values.shape[1]
    return jnp.where(
        lanes % 2 == 0, pltpu.roll(values, width - 1, 1), pltpu.roll(values, 1, 1)
    )


def arrange_body(block, idx_ref, own_ref, other_ref, xw_ref):
    half = own_ref.shape[0]

    def step(i, carry):
        rows = pl.ds(pl.multiple_of(i * block, block), block)
        picks = lax.broadcasted_iota(jnp.int32, (block, half), 1)
        source = idx_ref[rows, :]
        near = (picks == source).astype(BF)
        away = (picks + half == source).astype(BF)
        xw_ref[rows, :] = (dot(near, own_ref[...]) + dot(away, other_ref[...])).astype(BF)
        return carry

    lax.fori_loop(0, idx_ref.shape[0] // block, step, 0)


def arrange(idx_col, own, other, block=256):
    rows, width = idx_col.shape[0], own.shape[1]
    return pl.pallas_call(
        functools.partial(arrange_body, block),
        out_shape=jax.ShapeDtypeStruct((rows, width), BF),
        compiler_params=pltpu.CompilerParams(vmem_limit_bytes=40 << 20),
        cost_estimate=pl.CostEstimate(
            flops=2 * rows * rows * width, bytes_accessed=4 * rows * width, transcendentals=0
        ),
        name="arrange",
    )(idx_col, own, other)


def own_columns(core, near_ref, away_ref, hold, sems):
    span, share = near_ref.shape[0], hold.shape[1] // 3
    copies = []
    for s in range(3):
        for t, ref in enumerate((near_ref, away_ref)):
            side = core if t == 0 else 1 - core
            copies.append(
                pltpu.make_async_copy(
                    ref.at[:, pl.ds(pl.multiple_of(core * share + 2 * s * share, 128), share)],
                    hold.at[pl.ds(pl.multiple_of(side * span, 128), span), s * share:(s + 1) * share],
                    sems.at[2 * s + t],
                )
            )
    for copy in copies:
        copy.start()
    return copies


def project_body(block, part_ref, xw_ref, near_ref, away_ref, bias_ref, cos_ref, sin_ref,
                 q_ref, k_ref, v_ref, hold, sems):
    share = q_ref.shape[1]
    for copy in own_columns(part_ref[0], near_ref, away_ref, hold, sems):
        copy.wait()

    def step(i, carry):
        rows = pl.ds(pl.multiple_of(i * block, block), block)
        work = xw_ref[rows, :]
        cosine, sine = cos_ref[rows, :], sin_ref[rows, :]
        for out_ref, place, scale in ((q_ref, 0, LOG2E / math.sqrt(HEAD)), (k_ref, 1, 1.0)):
            whole = slice(place * share, (place + 1) * share)
            pre = dot(work, hold[:, whole]) + bias_ref[:, whole]
            for j in range(share // PAIR):
                cols = slice(j * PAIR, (j + 1) * PAIR)
                piece = pre[:, cols]
                out_ref[rows, cols] = (
                    (piece * cosine + pair_swap(piece) * sine) * scale
                ).astype(BF)
        v_ref[rows, :] = (dot(work, hold[:, 2 * share:]) + bias_ref[:, 2 * share:]).astype(BF)
        return carry

    lax.fori_loop(0, xw_ref.shape[0] // block, step, 0)


def project(part, xw, near_w, away_w, bias_own, cosine, sine, block=256):
    rows, width = xw.shape
    share = bias_own.shape[1] // 3
    vmem, smem, anywhere = (pl.BlockSpec(memory_space=s) for s in (pltpu.VMEM, pltpu.SMEM, pl.ANY))
    return pl.pallas_call(
        functools.partial(project_body, block),
        in_specs=[smem, vmem, anywhere, anywhere, vmem, vmem, vmem],
        out_shape=[jax.ShapeDtypeStruct((rows, share), BF)] * 3,
        scratch_shapes=[pltpu.VMEM((width, 3 * share), BF), pltpu.SemaphoreType.DMA((6,))],
        compiler_params=pltpu.CompilerParams(vmem_limit_bytes=40 << 20),
        cost_estimate=pl.CostEstimate(
            flops=2 * rows * width * 3 * share,
            bytes_accessed=2 * (rows * width + 3 * width * share + 3 * rows * share),
            transcendentals=0,
        ),
        name="project",
    )(part, xw, near_w, away_w, bias_own, cosine, sine)


def attend_body(block, idx_ref, q_ref, k_ref, v_ref, seg_col_ref, seg_row_ref,
                near_ref, away_ref, ctxt_ref, lse_ref, pick, ka, vt, qt, augt):
    rows = q_ref.shape[0]
    half = near_ref.shape[0]

    @pl.when(pl.program_id(0) == 0)
    def _():
        def fill(i, carry):
            span = pl.ds(pl.multiple_of(i * block, block), block)
            pick[span, :] = (
                lax.broadcasted_iota(jnp.int32, (block, rows), 1) == idx_ref[span, :]
            ).astype(BF)
            return carry

        lax.fori_loop(0, rows // block, fill, 0)
        lanes = lax.broadcasted_iota(jnp.int32, (rows, PAIR), 1)
        ka[:, PAIR:] = ((lanes == seg_col_ref[...]) | (lanes >= SEG_COUNT)).astype(BF)
        places = lax.broadcasted_iota(jnp.int32, (PAIR, rows), 0)
        augt[...] = jnp.where(
            (places < SEG_COUNT) & (places != seg_row_ref[...]), -FAR, 0.0
        ).astype(BF)

    ka[:, :PAIR] = k_ref[...]
    vt[...] = v_ref[...].T
    qt[...] = q_ref[...].T
    empty = jnp.zeros((HEAD, block), BF)

    def attended(span, keys):
        extra = augt[:, span]
        for h in range(2):
            mine = qt[h * HEAD:(h + 1) * HEAD, span]
            mixed = jnp.concatenate([mine, empty, extra] if h == 0 else [empty, mine, extra], axis=0)
            scores = dot(ka[keys, :], mixed)
            top = jnp.max(scores, axis=0, keepdims=True)
            expo = jnp.exp2(scores - top)
            total = jnp.sum(expo, axis=0, keepdims=True)
            context = dot(vt[h * HEAD:(h + 1) * HEAD, keys], expo.astype(BF))
            ctxt_ref[h * HEAD:(h + 1) * HEAD, span] = (context / total).astype(BF)
            lse_ref[0, h:h + 1, span] = top + jnp.log2(total)

    def step(i, carry):
        attended(pl.ds(pl.multiple_of(i * block, block), block), slice(0, LONGEST))
        return carry

    lax.fori_loop(0, LONGEST // block, step, 0)
    attended(slice(LONGEST, rows), slice(LONGEST, rows))
    given = dot(ctxt_ref[...], pick[...]).astype(BF)
    near_ref[...] = given[:, :half].T
    away_ref[...] = given[:, half:].T


def attend(idx_col, q, k, v, seg_col, seg_row, block=256):
    rows, share = q.shape
    pairs = share // PAIR
    half = rows // 2
    whole = lambda shape: pl.BlockSpec(shape, lambda j: (0,) * len(shape))
    column = lambda n: pl.BlockSpec((n, PAIR), lambda j: (0, j))
    return pl.pallas_call(
        functools.partial(attend_body, block),
        grid=(pairs,),
        in_specs=[whole((rows, 1)), column(rows), column(rows), column(rows),
                  whole((rows, 1)), whole((1, rows))],
        out_specs=[column(half), column(half), pl.BlockSpec((PAIR, rows), lambda j: (j, 0)),
                   pl.BlockSpec((1, 8, rows), lambda j: (j, 0, 0))],
        out_shape=[jax.ShapeDtypeStruct((half, share), BF), jax.ShapeDtypeStruct((half, share), BF),
                   jax.ShapeDtypeStruct((share, rows), BF),
                   jax.ShapeDtypeStruct((pairs, 8, rows), F32)],
        scratch_shapes=[pltpu.VMEM((rows, rows), BF), pltpu.VMEM((rows, 2 * PAIR), BF),
                        pltpu.VMEM((PAIR, rows), BF), pltpu.VMEM((PAIR, rows), BF),
                        pltpu.VMEM((PAIR, rows), BF)],
        compiler_params=pltpu.CompilerParams(vmem_limit_bytes=60 << 20),
        cost_estimate=pl.CostEstimate(
            flops=pairs * 2 * 2 * rows * rows * 3 * PAIR, bytes_accessed=2 * 6 * rows * share,
            transcendentals=2 * pairs * rows * rows,
        ),
        name="attend",
    )(idx_col, q, k, v, seg_col, seg_row)


def attend_back_body(block, idx_ref, q_ref, k_ref, v_ref, seg_col_ref, seg_row_ref, lse_ref,
                     ctxt_ref, gnear_ref, gaway_ref, cos_ref, sin_ref,
                     grads_ref,
                     pick, ka, va, kt, qt, dt, go, delta, dkacc, dvacc, dqt, augt):
    rows = q_ref.shape[0]
    half = gnear_ref.shape[0]

    @pl.when(pl.program_id(0) == 0)
    def _():
        def fill(i, carry):
            span = pl.ds(pl.multiple_of(i * block, block), block)
            pick[span, :] = (
                lax.broadcasted_iota(jnp.int32, (block, rows), 1) == idx_ref[span, :]
            ).astype(BF)
            return carry

        lax.fori_loop(0, rows // block, fill, 0)
        lanes = lax.broadcasted_iota(jnp.int32, (rows, PAIR), 1)
        ones = ((lanes == seg_col_ref[...]) | (lanes >= SEG_COUNT)).astype(BF)
        ka[:, PAIR:] = ones
        va[:, PAIR:] = jnp.ones((rows, PAIR), BF)
        places = lax.broadcasted_iota(jnp.int32, (8, rows), 0)
        augt[...] = jnp.where(
            (places < SEG_COUNT) & (places != seg_row_ref[...]), -FAR, 0.0
        )

    ka[:, :PAIR] = k_ref[...]
    va[:, :PAIR] = v_ref[...]
    kt[...] = k_ref[...].T
    qt[...] = q_ref[...].T
    grad = dot(pick[:, :half], gnear_ref[...]) + dot(pick[:, half:], gaway_ref[...])
    go[...] = grad.astype(BF)
    dt[...] = go[...].T
    weighed = dt[...].astype(F32) * ctxt_ref[...].astype(F32)
    delta[0:1, :] = jnp.sum(weighed[:HEAD], axis=0, keepdims=True)
    delta[1:2, :] = jnp.sum(weighed[HEAD:], axis=0, keepdims=True)
    dkacc[...] = jnp.zeros_like(dkacc)
    dvacc[...] = jnp.zeros_like(dvacc)
    empty = jnp.zeros((HEAD, block), BF)
    blank = jnp.zeros((PAIR - 16, block), BF)
    wide = lax.broadcasted_iota(jnp.int32, (block, PAIR), 1)
    zero = jnp.zeros((block, PAIR), BF)

    def thirds(row, start):
        first = row.astype(BF).astype(F32)
        second = (row - first).astype(BF).astype(F32)
        third = row - first - second
        places = lax.broadcasted_iota(jnp.int32, (16, block), 0)
        return jnp.where(places == start, first,
                         jnp.where(places == start + 1, second,
                                   jnp.where(places == start + 2, third, 0.0)))

    def attended(span, keys):
        base = jnp.concatenate([augt[:, span], jnp.zeros((8, block), F32)], axis=0)
        for h in range(2):
            part = slice(h * HEAD, (h + 1) * HEAD)
            low = (base + thirds(-lse_ref[0, h:h + 1, span], SEG_COUNT)).astype(BF)
            mine = qt[part, span]
            order = (mine, empty) if h == 0 else (empty, mine)
            scores = dot(ka[keys, :], jnp.concatenate(order + (low, blank), axis=0))
            probs = jnp.exp2(scores)
            low = thirds(-delta[h:h + 1, span], 0).astype(BF)
            mine = dt[part, span]
            order = (mine, empty) if h == 0 else (empty, mine)
            slope = dot(va[keys, :], jnp.concatenate(order + (low, blank), axis=0))
            grads = (probs * slope).astype(BF)
            keep = wide < HEAD if h == 0 else wide >= HEAD
            dvacc[keys, :] += dot(probs.astype(BF), jnp.where(keep, go[span, :], zero))
            dkacc[keys, :] += dot(grads, jnp.where(keep, q_ref[span, :], zero))
            dqt[part, span] = dot(kt[part, keys], grads)

    def step(i, carry):
        attended(pl.ds(pl.multiple_of(i * block, block), block), slice(0, LONGEST))
        return carry

    lax.fori_loop(0, LONGEST // block, step, 0)
    attended(slice(LONGEST, rows), slice(LONGEST, rows))
    cosine, sine = cos_ref[...], sin_ref[...]
    turned = dqt[...].T
    grads_ref[0] = ((turned * cosine - pair_swap(turned) * sine) * (1.0 / math.sqrt(HEAD))).astype(BF)
    turned = dkacc[...]
    grads_ref[1] = ((turned * cosine - pair_swap(turned) * sine) * LN2).astype(BF)
    grads_ref[2] = dvacc[...].astype(BF)


def attend_back(idx_col, q, k, v, seg_col, seg_row, lse, ctxt, gnear, gaway, cosine, sine, block=256):
    rows, share = q.shape
    pairs = share // PAIR
    half = rows // 2
    whole = lambda shape: pl.BlockSpec(shape, lambda j: (0,) * len(shape))
    column = lambda n: pl.BlockSpec((n, PAIR), lambda j: (0, j))
    return pl.pallas_call(
        functools.partial(attend_back_body, block),
        grid=(pairs,),
        in_specs=[whole((rows, 1)), column(rows), column(rows), column(rows),
                  whole((rows, 1)), whole((1, rows)),
                  pl.BlockSpec((1, 8, rows), lambda j: (j, 0, 0)),
                  pl.BlockSpec((PAIR, rows), lambda j: (j, 0)),
                  column(half), column(half), whole(cosine.shape), whole(sine.shape)],
        out_specs=pl.BlockSpec((3, rows, PAIR), lambda j: (0, 0, j)),
        out_shape=jax.ShapeDtypeStruct((3, rows, share), BF),
        scratch_shapes=[pltpu.VMEM((rows, rows), BF), pltpu.VMEM((rows, 2 * PAIR), BF),
                        pltpu.VMEM((rows, 2 * PAIR), BF), pltpu.VMEM((PAIR, rows), BF),
                        pltpu.VMEM((PAIR, rows), BF), pltpu.VMEM((PAIR, rows), BF),
                        pltpu.VMEM((rows, PAIR), BF), pltpu.VMEM((8, rows), F32),
                        pltpu.VMEM((rows, PAIR), F32), pltpu.VMEM((rows, PAIR), F32),
                        pltpu.VMEM((PAIR, rows), F32), pltpu.VMEM((8, rows), F32)],
        compiler_params=pltpu.CompilerParams(vmem_limit_bytes=60 << 20),
        cost_estimate=pl.CostEstimate(
            flops=pairs * 2 * 2 * rows * rows * 7 * PAIR, bytes_accessed=2 * 9 * rows * share,
            transcendentals=2 * pairs * rows * rows,
        ),
        name="attend_back",
    )(idx_col, q, k, v, seg_col, seg_row, lse, ctxt, gnear, gaway, cosine, sine)


def project_back_body(block, part_ref, g_ref, row_ref, wnear_ref, waway_ref,
                      near_ref, away_ref, work, hold, sems):
    rows, share = g_ref.shape[1:]
    half = near_ref.shape[0]
    for copy in own_columns(part_ref[0], wnear_ref, waway_ref, hold, sems):
        copy.wait()

    def step(i, carry):
        span = pl.ds(pl.multiple_of(i * block, block), block)
        total = None
        for place in range(3):
            term = dot_rt(g_ref[place, span, :], hold[:, place * share:(place + 1) * share])
            total = term if total is None else total + term
        work[span, :] = total.astype(BF)
        return carry

    lax.fori_loop(0, rows // block, step, 0)
    small = block // 2

    def back(i, carry):
        span = pl.ds(pl.multiple_of(i * small, small), small)
        for base, out_ref in ((half, away_ref), (0, near_ref)):
            pick = (lax.broadcasted_iota(jnp.int32, (small, rows), 0) + (base + i * small) == row_ref[...]).astype(BF)
            out_ref[span, :] = dot(pick, work[...]).astype(BF)
        return carry

    lax.fori_loop(0, half // small, back, 0)


def project_back(part, grads, idx_row, near_w, away_w, block=256):
    rows, share = grads.shape[1:]
    width = 2 * share
    half = rows // 2
    vmem, smem, anywhere = (pl.BlockSpec(memory_space=s) for s in (pltpu.VMEM, pltpu.SMEM, pl.ANY))
    return pl.pallas_call(
        functools.partial(project_back_body, block),
        in_specs=[smem, vmem, vmem, anywhere, anywhere],
        scratch_shapes=[pltpu.VMEM((rows, width), BF), pltpu.VMEM((width, 3 * share), BF),
                        pltpu.SemaphoreType.DMA((6,))],
        out_shape=[jax.ShapeDtypeStruct((half, width), BF)] * 2,
        compiler_params=pltpu.CompilerParams(vmem_limit_bytes=40 << 20),
        cost_estimate=pl.CostEstimate(
            flops=2 * rows * width * (rows + 3 * share),
            bytes_accessed=2 * rows * (width + 3 * share) + 6 * width * share,
            transcendentals=0,
        ),
        name="project_back",
    )(part, grads, idx_row, near_w, away_w)


def weight_back_body(batches, *refs):
    xw_refs, g_refs, (gw_ref, gb_ref) = refs[:batches], refs[batches:2 * batches], refs[2 * batches:]
    total, thin = None, None
    for xw_ref, g_ref in zip(xw_refs, g_refs):
        term = dot_lt(xw_ref[...], g_ref[0])
        line = jnp.sum(g_ref[0].astype(F32), axis=0, keepdims=True)
        total = term if total is None else total + term
        thin = line if thin is None else thin + line
    gw_ref[...] = total.astype(BF)
    gb_ref[...] = jnp.broadcast_to(thin, gb_ref.shape)


def weight_back(xws, grads):
    batches, (rows, width), share = len(xws), xws[0].shape, grads[0].shape[2]
    whole = pl.BlockSpec((rows, width), lambda s: (0, 0))
    each = pl.BlockSpec((1, rows, share), lambda s: (s, 0, 0))
    return pl.pallas_call(
        functools.partial(weight_back_body, batches),
        grid=(3,),
        in_specs=[whole] * batches + [each] * batches,
        out_specs=[pl.BlockSpec((width, share), lambda s: (0, s)),
                   pl.BlockSpec((8, share), lambda s: (0, s))],
        out_shape=[jax.ShapeDtypeStruct((width, 3 * share), BF), jax.ShapeDtypeStruct((8, 3 * share), F32)],
        compiler_params=pltpu.CompilerParams(vmem_limit_bytes=60 << 20),
        cost_estimate=pl.CostEstimate(
            flops=2 * batches * rows * width * 3 * share,
            bytes_accessed=2 * batches * rows * (width + 3 * share) + 6 * width * share,
            transcendentals=0,
        ),
        name="weight_back",
    )(*xws, *grads)


EPS = 1e-6
ERF_SLOPE = 0.3275911 * math.sqrt(0.5)
ERF_TERMS = (0.254829592, -0.284496736, 1.421413741, -1.453152027, 1.061405429)


def gauss_parts(u):
    bell = jnp.exp2(u * u * (-0.5 * LOG2E))
    t = 1.0 / (1.0 + ERF_SLOPE * jnp.abs(u))
    poly = 0.5 * ERF_TERMS[4]
    for term in ERF_TERMS[3::-1]:
        poly = poly * t + 0.5 * term
    tail = poly * t * bell
    below = jnp.where(u < 0.0, tail, 1.0 - tail)
    return u * below, below + u * bell * (1.0 / math.sqrt(2.0 * math.pi))


def row_mean(value):
    return jnp.sum(value, axis=1, keepdims=True) * (1.0 / value.shape[1])


def standard(hidden):
    centre = hidden - row_mean(hidden)
    root = lax.rsqrt(row_mean(centre * centre) + EPS)
    return centre * root, root


def standard_back(grad, norm, root):
    return root * (grad - row_mean(grad) - norm * row_mean(grad * norm))


def feed_body(chunk, part_ref, x_ref, near_ref, away_ref, dy_ref, thin_ref, bup_ref,
              unear_ref, uaway_ref, dnear_ref, daway_ref,
              out_ref, dh_ref, lmine_ref, ltheirs_ref, amine_ref, atheirs_ref, dup_ref, dlow_ref, da_ref, cnear_ref, caway_ref,
              sums_ref, bsum_ref, wo_near, wo_away, wup, wdown, slopes, sems):
    first_step = pl.program_id(0) == 0
    core = part_ref[0]
    width, wide = wup.shape
    share = near_ref.shape[1]
    half_w, half_f = width // 2, wide // 2

    def loads():
        copies = []
        for t, (u_ref, d_ref) in enumerate(((unear_ref, dnear_ref), (uaway_ref, daway_ref))):
            side = core if t == 0 else 1 - core
            hold = wo_near if t == 0 else wo_away
            copies += [
                pltpu.make_async_copy(u_ref.at[:, :width], hold, sems.at[t]),
                pltpu.make_async_copy(
                    u_ref.at[:, width:], wup.at[pl.ds(pl.multiple_of(side * half_w, 128), half_w), :],
                    sems.at[2 + t]),
                pltpu.make_async_copy(
                    d_ref, wdown.at[pl.ds(pl.multiple_of(side * half_f, 128), half_f), :], sems.at[4 + t]),
            ]
        return copies

    @pl.when(first_step)
    def _():
        copies = loads()
        for copy in copies:
            copy.start()
        sums_ref[...] = jnp.zeros_like(sums_ref)
        bsum_ref[...] = jnp.zeros_like(bsum_ref)
        for copy in copies:
            copy.wait()

    b_out, gain_one, shift_one, b_down, gain_two, shift_two = (thin_ref[i:i + 1, :] for i in range(6))

    def tally(row, value):
        sums_ref[row:row + 1, :] += jnp.sum(value, axis=0, keepdims=True)

    attended = dot(near_ref[...], wo_near[...]) + dot(away_ref[...], wo_away[...]) + b_out
    norm_one, root_one = standard(x_ref[...].astype(F32) + attended)
    first = norm_one * gain_one + shift_one
    low = first.astype(BF)

    def split(value, at, mine_ref, theirs_ref):
        size = mine_ref.shape[1]
        cols = slice(at % size, at % size + value.shape[1])

        @pl.when(core == at // size)
        def _():
            mine_ref[:, cols] = value

        @pl.when(core != at // size)
        def _():
            theirs_ref[:, cols] = value

    split(low[:, :half_w], 0, lmine_ref, ltheirs_ref)
    split(low[:, half_w:], half_w, lmine_ref, ltheirs_ref)
    lowered = None
    for c in range(wide // chunk):
        cols = slice(c * chunk, (c + 1) * chunk)
        act, slope = gauss_parts(dot(low, wup[:, cols]) + bup_ref[:, cols])
        act = act.astype(BF)
        split(act, c * chunk, amine_ref, atheirs_ref)
        slopes[:, cols] = slope.astype(BF)
        term = dot(act, wdown[cols, :])
        lowered = term if lowered is None else lowered + term
    norm_two, root_two = standard(first + lowered + b_down)
    out_ref[...] = (norm_two * gain_two + shift_two).astype(BF)
    dy = dy_ref[...].astype(F32)
    tally(4, dy * norm_two)
    tally(5, dy)
    grad_two = standard_back(dy * gain_two, norm_two, root_two)
    dlow = grad_two.astype(BF)
    dlow_ref[...] = dlow
    tally(3, dlow.astype(F32))
    total = grad_two
    for c in range(wide // chunk):
        cols = slice(c * chunk, (c + 1) * chunk)
        dup = (dot_rt(dlow, wdown[cols, :]) * slopes[:, cols].astype(F32)).astype(BF)
        dup_ref[:, cols] = dup
        bsum_ref[0:1, cols] += jnp.sum(dup.astype(F32), axis=0, keepdims=True)
        total = total + dot_rt(dup, wup[:, cols])
    tally(1, total * norm_one)
    tally(2, total)
    grad_one = standard_back(total * gain_one, norm_one, root_one)
    dh_ref[...] = grad_one
    da = grad_one.astype(BF)
    da_ref[...] = da
    tally(0, da.astype(F32))
    cnear_ref[...] = dot_rt(da, wo_near[...]).astype(BF)
    caway_ref[...] = dot_rt(da, wo_away[...]).astype(BF)


def feed(part, x, near, away, dy, thin, bup, unear, uaway, dnear, daway, block=256, chunk=768):
    rows, width = x.shape
    share = near.shape[1]
    wide = bup.shape[1]
    line = lambda n: pl.BlockSpec((block, n), lambda i: (i, 0))
    fixed = lambda shape: pl.BlockSpec(shape, lambda i: (0, 0))
    anywhere = pl.BlockSpec(memory_space=pl.ANY)
    shape = lambda n, dt: jax.ShapeDtypeStruct((rows, n), dt)
    return pl.pallas_call(
        functools.partial(feed_body, chunk),
        grid=(rows // block,),
        in_specs=[pl.BlockSpec(memory_space=pltpu.SMEM), line(width), line(share), line(share), line(width),
                  fixed(thin.shape), fixed(bup.shape), anywhere, anywhere, anywhere, anywhere],
        out_specs=[line(width), line(width), line(width // 2), line(width // 2), line(wide // 2),
                   line(wide // 2), line(wide), line(width), line(width),
                   line(share), line(share), fixed((8, width)), fixed((8, wide))],
        out_shape=[shape(width, BF), shape(width, F32), shape(width // 2, BF), shape(width // 2, BF),
                   shape(wide // 2, BF), shape(wide // 2, BF), shape(wide, BF), shape(width, BF), shape(width, BF), shape(share, BF), shape(share, BF),
                   jax.ShapeDtypeStruct((8, width), F32), jax.ShapeDtypeStruct((8, wide), F32)],
        scratch_shapes=[pltpu.VMEM((share, width), BF), pltpu.VMEM((share, width), BF),
                        pltpu.VMEM((width, wide), BF), pltpu.VMEM((wide, width), BF),
                        pltpu.VMEM((block, wide), BF), pltpu.SemaphoreType.DMA((6,))],
        compiler_params=pltpu.CompilerParams(vmem_limit_bytes=60 << 20),
        cost_estimate=pl.CostEstimate(
            flops=2 * rows * width * (2 * width + 4 * wide),
            bytes_accessed=2 * rows * (7 * width + 2 * wide) + 4 * width * (wide + width),
            transcendentals=2 * rows * wide,
        ),
        name="feed",
    )(part, x, near, away, dy, thin, bup, unear, uaway, dnear, daway)


def swap_cores(value):
    return lax.ppermute(value, "seq", [(0, 1), (1, 0)])


def swap_x(value):
    return lax.ppermute(value, "fsdp", [(i, i ^ 1) for i in range(16)])


def swap_y(value):
    return lax.ppermute(value, "fsdp", [(i, i ^ 2) for i in range(16)])


def shift_z(value, k):
    return lax.ppermute(value, "fsdp", [(i, (i + 4 * k) % 16) for i in range(16)])


def assemble_body(place_ref, ax_ref, ay_ref, bx_ref, by_ref, out_ref):
    place = place_ref[0]
    z, y, x = place // 4, (place // 2) % 2, place % 2
    for j in range(4):
        k, o = j % 2, j // 2
        near_z, far_z = lax.rem(z - k + 4, 4), lax.rem(z - k + 2, 4)
        flip_x = lax.rem(x + o, 2)
        flip_y = lax.rem(y + o, 2)
        out_ref[near_z * 4 + y * 2 + flip_x] = ax_ref[j]
        out_ref[near_z * 4 + (1 - y) * 2 + flip_x] = ay_ref[j]
        out_ref[far_z * 4 + flip_y * 2 + x] = by_ref[j]
        out_ref[far_z * 4 + flip_y * 2 + 1 - x] = bx_ref[j]


def assemble(place, parts):
    n, width = parts[0].shape[1:]
    vmem = pl.BlockSpec(memory_space=pltpu.VMEM)
    return pl.pallas_call(
        assemble_body,
        in_specs=[pl.BlockSpec(memory_space=pltpu.SMEM)] + [vmem] * 4,
        out_shape=jax.ShapeDtypeStruct((16, n, width), BF),
        compiler_params=pltpu.CompilerParams(vmem_limit_bytes=24 << 20),
        cost_estimate=pl.CostEstimate(flops=0, bytes_accessed=4 * 16 * n * width, transcendentals=0),
        name="assemble",
    )(place, *parts)


def tie(values, after=()):
    return lax.optimization_barrier((values, after))[0]


def reach_z(shard):
    first = jnp.stack([shard, shift_z(shard, 1)])
    second = jnp.stack([shift_z(shard, 2), shift_z(shard, 3)])
    return first, second


def reach_one(first, second):
    return jnp.concatenate([first, swap_x(first)], axis=0), jnp.concatenate([second, swap_y(second)], axis=0)


def reach_two(first, second):
    return first, swap_y(first), swap_x(second), second


def joined(parts):
    n, width = parts[0].shape[1:]
    place = jnp.full((1,), lax.axis_index("fsdp"), jnp.int32)
    return assemble(place, parts).reshape(16 * n, width)


def pick(part, at, axis):
    return lax.dynamic_index_in_dim(part, at, axis, keepdims=False)


def corner():
    place = lax.axis_index("fsdp")
    return place // 4, (place // 2) % 2, place % 2


def fold_one(value):
    z, y, x = corner()
    rows, width = value.shape
    cube = value.reshape(2, 2, 2, 2, rows // 16, width)
    return (value,), (pick(cube[0], 1 - y, 1).astype(BF), pick(cube[1], 1 - x, 2).astype(BF))


def fold_two(stay, sends, after=()):
    z, y, x = corner()
    rows, width = stay[0].shape
    cube = stay[0].reshape(2, 2, 2, 2, rows // 16, width)
    came = tie((swap_y(sends[0]), swap_x(sends[1])), after)
    first = pick(cube[0], y, 1).astype(F32) + came[0].astype(F32)
    second = pick(cube[1], x, 2).astype(F32) + came[1].astype(F32)
    return (first, second), (pick(first, 1 - x, 1).astype(BF), pick(second, 1 - y, 1).astype(BF))


def fold_cross(stay, sends):
    z, y, x = corner()
    first = pick(stay[0], x, 1) + swap_x(sends[0]).astype(F32)
    second = pick(stay[1], y, 1) + swap_y(sends[1]).astype(F32)
    return jnp.concatenate([first, second], axis=0)


def fold_three(stack):
    z = corner()[0]
    return (pick(stack, z, 0),), tuple(pick(stack, lax.rem(z + k, 4), 0).astype(BF) for k in (1, 2, 3))


def fold_end(stay, sends, after=()):
    total = stay[0]
    for came in tie([shift_z(send, k) for k, send in zip((1, 2, 3), sends)], after):
        total = total + came.astype(F32)
    return total


def spread_rows(segments, order):
    rows = segments.shape[0]
    ids = jnp.arange(SEG_COUNT, dtype=jnp.int32)
    counts = jnp.sum(segments[:, None] == ids[None, :], axis=0, dtype=jnp.int32)
    long_id = jnp.sum(jnp.where(counts == LONGEST, ids, 0))
    starts = jnp.sum(jnp.where(ids[:, None] < ids[None, :], counts[:, None], 0), axis=0)
    start = jnp.sum(jnp.where(ids == long_id, starts, 0))
    places = jnp.arange(rows, dtype=jnp.int32)
    table = jnp.stack([order, segments, places])
    main = lax.dynamic_slice_in_dim(table, start, LONGEST, 1)
    rest = jnp.where(places[None, :rows - LONGEST] < start, table[:, :rows - LONGEST], table[:, LONGEST:])
    order, segments, places = jnp.concatenate([main, rest], axis=1)
    origin = jnp.sum(jnp.where(segments[:, None] == ids[None, :], starts[None, :], 0), axis=1)
    return order, segments, (places - origin).astype(F32)


def turn_tables(position):
    halves = HEAD // 2
    freqs = jnp.exp(jnp.arange(halves, dtype=F32) * (-2.0 * math.log(10000.0) / HEAD))
    phase = position[:, None] * freqs[None, :]
    cosine = jnp.tile(jnp.repeat(jnp.cos(phase), 2, axis=1), (1, 2))
    signs = jnp.tile(jnp.array([-1.0, 1.0], F32), halves)[None, :]
    sine = jnp.tile(jnp.repeat(jnp.sin(phase), 2, axis=1) * signs, (1, 2))
    return cosine, sine


def on_device(tokens, permutation, segment_ids, cotangent, *shards):
    batches = tokens.shape[0]
    half, width = tokens.shape[2], tokens.shape[3]
    core = lax.axis_index("seq")
    share = width // 2
    owners = 2 * lax.axis_size("fsdp")
    staged = owners == 32
    part = jnp.full((1,), core, jnp.int32)
    thin = [i for i, piece in enumerate(shards) if piece.ndim == 1]
    sizes = [shards[i].shape[0] for i in thin]
    count = sum(sizes)
    n_qkv = shards[0].shape[0]
    room = n_qkv * 128
    tokens, cotangent = tokens[:, 0], cotangent[:, 0]

    packed = jnp.concatenate([shards[i] for i in thin] + [jnp.zeros((room - count,), BF)])
    q_shard = jnp.concatenate([shards[0], packed.reshape(n_qkv, 128)], axis=1)
    u_shard = jnp.concatenate([shards[2], shards[6]], axis=1)
    d_shard = shards[8]
    if staged:
        q_pair = reach_z(q_shard)
        u_shard, d_shard = tie((u_shard, d_shard), q_pair)
        q_parts = reach_two(*reach_one(*q_pair))
        u_pair, d_pair = tie((reach_z(u_shard), reach_z(d_shard)), q_parts)
        pairs = (reach_one(*u_pair), reach_one(*d_pair))
        q_near = joined(q_parts)
    else:
        q_near = lax.all_gather(q_shard, "fsdp", axis=0, tiled=True)
    q_away = swap_cores(q_near)
    away_tokens = swap_cores(tokens)

    slabs = [value[:, 3 * width:].reshape(owners // 2, room)[:, :count] for value in (q_near, q_away)]
    vectors = jnp.concatenate(
        [jnp.where(core == 0, slabs[0], slabs[1]), jnp.where(core == 0, slabs[1], slabs[0])], axis=0
    ).astype(F32)
    spread, at = [], 0
    for size in sizes:
        spread.append(vectors[:, at:at + size].reshape(1, owners * size))
        at += size
    b_qkv, b_out, gain_one, shift_one, b_up, b_down, gain_two, shift_two = spread
    bias_own = jnp.concatenate(
        [lax.dynamic_slice_in_dim(b_qkv, core * share + s * width, share, 1) for s in range(3)], axis=1
    )
    blank_row = jnp.zeros((1, width), F32)
    thin_rows = jnp.concatenate(
        [b_out, gain_one, shift_one, b_down, gain_two, shift_two, blank_row, blank_row], axis=0
    )

    kept = []
    for b in range(batches):
        order, segments, position = spread_rows(segment_ids[b, 0], permutation[b, 0])
        place = jnp.where(
            order // half == core, order - core * half, order - (1 - core) * half + half
        )
        cosine, sine = turn_tables(position)
        col, row = segments[:, None], segments[None, :]
        idx_col, idx_row = place[:, None], place[None, :]
        xw = arrange(idx_col, tokens[b], away_tokens[b])
        kept.append((idx_col, idx_row, col, row, cosine, sine, xw))
    ctxs = []
    for b in range(batches):
        idx_col, idx_row, col, row, cosine, sine, xw = kept[b]
        q, k, v = project(part, xw, q_near, q_away, bias_own, cosine, sine)
        if staged and b == 0:
            q, pairs = tie((q, pairs))
            u_parts, d_parts = reach_two(*pairs[0]), reach_two(*pairs[1])
        if staged and b == 1:
            u_parts, d_parts = tie((u_parts, d_parts), (ctxs[0][0], q))
            u_near, d_near = joined(u_parts), joined(d_parts)
            q, u_near, d_near = tie((q, u_near, d_near))
        near, away, ctxt, lse = attend(idx_col, q, k, v, col, row)
        kept[b] += (q, k, v, ctxt, lse)
        ctxs.append((near, swap_cores(away)))
    if not staged:
        u_near = lax.all_gather(u_shard, "fsdp", axis=0, tiled=True)
        d_near = lax.all_gather(d_shard, "fsdp", axis=0, tiled=True)
    u_away, d_away = swap_cores(u_near), swap_cores(d_near)
    near, away = (jnp.concatenate([item[i] for item in ctxs], axis=0) for i in range(2))
    (outputs, grad_one, low_mine, low_theirs, act_mine, act_theirs, dup, dlow, da, cnear, caway, sums, bsum) = feed(
        part, tokens.reshape(batches * half, width), near, away,
        cotangent.reshape(batches * half, width), thin_rows, b_up, u_near, u_away, d_near, d_away,
    )
    caway = swap_cores(caway)

    d_theirs = swap_cores(dot_lt(act_theirs, dlow).astype(BF))
    uo_theirs = swap_cores(
        jnp.concatenate([dot_lt(low_theirs, dup).astype(BF), dot_lt(away, da).astype(BF)], axis=1)
    )
    d_sum = (dot_lt(act_mine, dlow) + d_theirs.astype(F32)).astype(BF)
    uo_sum = jnp.concatenate([
        (dot_lt(low_mine, dup) + uo_theirs[:, :4 * width].astype(F32)).astype(BF),
        (dot_lt(near, da) + uo_theirs[:, 4 * width:].astype(F32)).astype(BF),
    ], axis=1)

    def back(b, given):
        idx_col, idx_row, col, row, cosine, sine, xw, q, k, v, ctxt, lse = kept[b]
        return attend_back(
            idx_col, q, k, v, col, row, lse, ctxt, *given, cosine, sine
        )

    givens = [(cnear[b * half:(b + 1) * half], caway[b * half:(b + 1) * half]) for b in range(batches)]
    if staged:
        given, d_step, uo_step = tie((givens[0], fold_one(d_sum), fold_one(uo_sum)))
        first_back = back(0, given)
        given, d_step, uo_step = tie((givens[1], fold_two(*d_step), fold_two(*uo_step)), first_back)
        grads = [first_back, back(1, given)]
        wide, lines = fold_cross(*uo_step), fold_cross(*d_step)
        lines = [lines[:, i * n_qkv:(i + 1) * n_qkv] for i in range(4)]
        du_step = fold_three(jnp.concatenate([wide] + lines, axis=2))
        grads, du_step = tie((grads, du_step))
    else:
        grads = [back(b, givens[b]) for b in range(batches)]
    xws = [item[6] for item in kept]
    gw_own, gb_own = weight_back(xws, grads)

    def halves(value):
        size = value.shape[0] // 2
        return (lax.dynamic_slice_in_dim(value, core * size, size, 0),
                lax.dynamic_slice_in_dim(value, (1 - core) * size, size, 0))

    blank = jnp.zeros((share,), F32)
    thin_columns = []
    for s in range(3):
        span = slice(s * share, (s + 1) * share)
        thin_columns += [jnp.where(core == 0, gb_own[0, span], blank),
                         jnp.where(core == 0, blank, gb_own[0, span])]
    thin_grads = [jnp.concatenate(thin_columns), sums[0], sums[1], sums[2], bsum[0], sums[3], sums[4], sums[5]]
    slab = jnp.concatenate(
        [value.reshape(owners, -1) for value in thin_grads] + [jnp.zeros((owners, room - count), F32)], axis=1
    ).astype(BF).reshape(owners * n_qkv, 128)
    mine, theirs = (jnp.concatenate(pair, axis=1) for pair in zip(halves(gw_own), halves(slab)))
    theirs = swap_cores(theirs)
    q_sum = jnp.concatenate([
        mine[:, :3 * share], theirs[:, :3 * share],
        (mine[:, 3 * share:].astype(F32) + theirs[:, 3 * share:].astype(F32)).astype(BF),
    ], axis=1)
    backs = [project_back(part, grads[0], kept[0][1], q_near, q_away)]
    if staged:
        last, q_step, backs = tie((grads[1], fold_one(q_sum), backs))
        backs.append(project_back(part, last, kept[1][1], q_near, q_away))
        q_step = fold_two(*q_step, backs[1])
        q_last = fold_three(fold_cross(*q_step))
        g_uo = fold_end(*du_step, q_last)
        g_qkv = fold_end(*q_last, g_uo)
        g_down = jnp.concatenate([g_uo[:, (5 + i) * width:(6 + i) * width] for i in range(4)], axis=0)
    else:
        backs.append(project_back(part, grads[1], kept[1][1], q_near, q_away))
        summed = lambda value: lax.psum_scatter(
            value.astype(BF), "fsdp", scatter_dimension=0, tiled=True
        ).astype(F32)
        g_qkv, g_down, g_uo = summed(q_sum), summed(d_sum), summed(uo_sum)
    own, other = g_qkv[:, :3 * share], g_qkv[:, 3 * share:6 * share]
    columns = []
    for s in range(3):
        span = slice(s * share, (s + 1) * share)
        columns += [jnp.where(core == 0, own[:, span], other[:, span]),
                    jnp.where(core == 0, other[:, span], own[:, span])]
    g_out, g_up = g_uo[:, 4 * width:5 * width], g_uo[:, :4 * width]
    grad_one = grad_one.reshape(batches, half, width)
    token_grad = jnp.stack([
        (grad_one[b] + backs[b][0].astype(F32) + swap_cores(backs[b][1]).astype(F32)).astype(BF)
        for b in range(batches)
    ])
    flat = g_qkv[:, 3 * width:].reshape(room)
    thin_out, at = [], 0
    for size in sizes:
        thin_out.append(flat[at:at + size])
        at += size
    g_bqkv, g_bout, g_g1, g_s1, g_bup, g_bdown, g_g2, g_s2 = thin_out
    return (
        outputs.reshape(batches, 1, half, width), token_grad[:, None],
        jnp.concatenate(columns, axis=1), g_bqkv, g_out, g_bout, g_g1, g_s1, g_up, g_bup, g_down, g_bdown, g_g2, g_s2,
    )


def solution(mesh):
    packs = P(None, "fsdp", "seq", None)
    ids = P(None, "fsdp", None)
    deep, flat = P(("seq", "fsdp"), None), P(("seq", "fsdp"))
    layers = (deep, flat, deep, flat, flat, flat, deep, flat, deep, flat, flat, flat)
    return jax.shard_map(
        on_device, mesh=mesh, in_specs=(packs, ids, ids, packs) + layers,
        out_specs=(packs, packs) + layers, check_vma=False,
    )
```

```python
import functools
import math

import jax
import jax.numpy as jnp
from jax import lax
from jax.experimental import pallas as pl
from jax.experimental.pallas import tpu as pltpu
from jax.sharding import PartitionSpec as P

HEAD = 64
PAIR = 2 * HEAD
SEG_COUNT = 4
LONGEST = 1024
LOG2E = math.log2(math.e)
LN2 = math.log(2.0)
FAR = float(2**30)
BF = jnp.bfloat16
F32 = jnp.float32


def dot(left, right):
    return jnp.dot(left, right, preferred_element_type=F32)


def dot_rt(left, right):
    return lax.dot_general(left, right, (((1,), (1,)), ((), ())), preferred_element_type=F32)


def dot_lt(left, right):
    return lax.dot_general(left, right, (((0,), (0,)), ((), ())), preferred_element_type=F32)


def pair_swap(values):
    lanes = lax.broadcasted_iota(jnp.int32, values.shape, 1)
    width = values.shape[1]
    return jnp.where(
        lanes % 2 == 0, pltpu.roll(values, width - 1, 1), pltpu.roll(values, 1, 1)
    )


def ready_body(part_ref, order_ref, seg_ref, freq_ref, idx_col, idx_row, seg_col, seg_row, cos_ref, sin_ref):
    core = part_ref[0]
    batches, rows = order_ref.shape
    half = rows // 2
    lanes = lax.broadcasted_iota(jnp.int32, (1, rows), 1)
    wide = lax.broadcasted_iota(jnp.int32, (8, rows), 1)
    halves = freq_ref.shape[0]
    cols = lax.broadcasted_iota(jnp.int32, (halves, PAIR), 1)
    lines = lax.broadcasted_iota(jnp.int32, (halves, PAIR), 0)
    grow = ((cols % HEAD) // 2 == lines).astype(F32)
    turn = jnp.where(cols % 2 == 0, -grow, grow)
    expand = lambda value, by: lax.dot_general(
        value, by, (((0,), (0,)), ((), ())), preferred_element_type=F32, precision=lax.Precision.HIGHEST)
    for b in range(batches):
        order, seg = order_ref[b:b + 1, :], seg_ref[b:b + 1, :]
        starts, start, total = [], 0, 0
        for s in range(SEG_COUNT):
            size = jnp.sum((seg == s).astype(F32)).astype(jnp.int32)
            starts.append(total)
            start = start + jnp.where(size == LONGEST, total, 0)
            total = total + size
        table = jnp.concatenate([order, seg, lanes, jnp.zeros((5, rows), jnp.int32)], axis=0)
        main = pltpu.roll(table, rows - start, 1)
        early = pltpu.roll(table, LONGEST, 1)
        table = jnp.where(wide < LONGEST, main, jnp.where(wide - LONGEST < start, early, table))
        order, seg, place = table[0:1], table[1:2], table[2:3]
        origin = jnp.zeros_like(seg)
        for s in range(1, SEG_COUNT):
            origin = jnp.where(seg == s, starts[s], origin)
        position = (place - origin).astype(F32)
        near = (order >= half).astype(jnp.int32) == core
        idx = jnp.where(near, order - core * half, order + core * half)
        idx_row[b] = idx
        seg_row[b] = seg
        both = jnp.concatenate([idx.astype(F32), seg.astype(F32), jnp.zeros((6, rows), F32)], axis=0).T
        idx_col[b] = both[:, 0:1].astype(jnp.int32)
        seg_col[b] = both[:, 1:2].astype(jnp.int32)
        phase = freq_ref[...] * position
        cos_ref[b] = expand(jnp.cos(phase), grow)
        sin_ref[b] = expand(jnp.sin(phase), turn)


def ready(part, order, segments):
    batches, rows = order.shape
    halves = HEAD // 2
    freqs = jnp.exp(jnp.arange(halves, dtype=F32) * (-2.0 * math.log(10000.0) / HEAD))[:, None]
    vmem, smem = (pl.BlockSpec(memory_space=s) for s in (pltpu.VMEM, pltpu.SMEM))
    ints = lambda *shape: jax.ShapeDtypeStruct(shape, jnp.int32)
    return pl.pallas_call(
        ready_body,
        in_specs=[smem, vmem, vmem, vmem],
        out_shape=[ints(batches, rows, 1), ints(batches, 1, rows), ints(batches, rows, 1), ints(batches, 1, rows),
                   jax.ShapeDtypeStruct((batches, rows, PAIR), F32), jax.ShapeDtypeStruct((batches, rows, PAIR), F32)],
        compiler_params=pltpu.CompilerParams(vmem_limit_bytes=40 << 20),
        cost_estimate=pl.CostEstimate(
            flops=1 << 30, bytes_accessed=8 * batches * rows * 3 * PAIR, transcendentals=2 * batches * rows * halves
        ),
        name="ready",
    )(part, order, segments, freqs)


def arrange_body(block, idx_ref, own_ref, other_ref, xw_ref):
    half = own_ref.shape[1]

    def step(i, carry):
        rows = pl.ds(pl.multiple_of(i * block, block), block)
        picks = lax.broadcasted_iota(jnp.int32, (block, half), 1)
        source = idx_ref[0, rows, :]
        near = (picks == source).astype(BF)
        away = (picks + half == source).astype(BF)
        xw_ref[0, rows, :] = (dot(near, own_ref[0]) + dot(away, other_ref[0])).astype(BF)
        return carry

    lax.fori_loop(0, idx_ref.shape[1] // block, step, 0)


def arrange(idx_col, own, other, block=256):
    batches, rows = idx_col.shape[:2]
    half, width = own.shape[1:]
    each = lambda *shape: pl.BlockSpec((1,) + shape, lambda b: (b, 0, 0))
    return pl.pallas_call(
        functools.partial(arrange_body, block),
        grid=(batches,),
        in_specs=[each(rows, 1), each(half, width), each(half, width)],
        out_specs=each(rows, width),
        out_shape=jax.ShapeDtypeStruct((batches, rows, width), BF),
        compiler_params=pltpu.CompilerParams(vmem_limit_bytes=40 << 20),
        cost_estimate=pl.CostEstimate(
            flops=2 * batches * rows * rows * width, bytes_accessed=4 * batches * rows * width, transcendentals=0
        ),
        name="arrange",
    )(idx_col, own, other)


def own_columns(core, near_ref, away_ref, hold, sems):
    span, share = near_ref.shape[0], hold.shape[1] // 3
    copies = []
    for s in range(3):
        for t, ref in enumerate((near_ref, away_ref)):
            side = core if t == 0 else 1 - core
            copies.append(
                pltpu.make_async_copy(
                    ref.at[:, pl.ds(pl.multiple_of(core * share + 2 * s * share, 128), share)],
                    hold.at[pl.ds(pl.multiple_of(side * span, 128), span), s * share:(s + 1) * share],
                    sems.at[2 * s + t],
                )
            )
    for copy in copies:
        copy.start()
    return copies


def project_body(block, part_ref, xw_ref, near_ref, away_ref, bias_ref, cos_ref, sin_ref,
                 qkv_ref, hold, sems):
    share = qkv_ref.shape[2]
    for copy in own_columns(part_ref[0], near_ref, away_ref, hold, sems):
        copy.wait()

    def step(i, carry):
        rows = pl.ds(pl.multiple_of(i * block, block), block)
        work = xw_ref[0, rows, :]
        cosine, sine = cos_ref[0, rows, :], sin_ref[0, rows, :]
        for place, scale in ((0, LOG2E / math.sqrt(HEAD)), (1, 1.0)):
            whole = slice(place * share, (place + 1) * share)
            pre = dot(work, hold[:, whole]) + bias_ref[:, whole]
            for j in range(share // PAIR):
                cols = slice(j * PAIR, (j + 1) * PAIR)
                piece = pre[:, cols]
                qkv_ref[place, rows, cols] = (
                    (piece * cosine + pair_swap(piece) * sine) * scale
                ).astype(BF)
        qkv_ref[2, rows, :] = (dot(work, hold[:, 2 * share:]) + bias_ref[:, 2 * share:]).astype(BF)
        return carry

    lax.fori_loop(0, xw_ref.shape[1] // block, step, 0)


def project(b, part, xws, near_w, away_w, bias_own, cosine, sine, block=256):
    rows, width = xws.shape[1:]
    share = bias_own.shape[1] // 3
    each = lambda n: pl.BlockSpec((1, rows, n), lambda i: (b, 0, 0))
    vmem, smem, anywhere = (pl.BlockSpec(memory_space=s) for s in (pltpu.VMEM, pltpu.SMEM, pl.ANY))
    return pl.pallas_call(
        functools.partial(project_body, block),
        grid=(1,),
        in_specs=[smem, each(width), anywhere, anywhere, vmem, each(PAIR), each(PAIR)],
        out_specs=pl.BlockSpec((3, rows, share), lambda i: (0, 0, 0)),
        out_shape=jax.ShapeDtypeStruct((3, rows, share), BF),
        scratch_shapes=[pltpu.VMEM((width, 3 * share), BF), pltpu.SemaphoreType.DMA((6,))],
        compiler_params=pltpu.CompilerParams(vmem_limit_bytes=40 << 20),
        cost_estimate=pl.CostEstimate(
            flops=2 * rows * width * 3 * share,
            bytes_accessed=2 * (rows * width + 3 * width * share + 3 * rows * share),
            transcendentals=0,
        ),
        name="project",
    )(part, xws, near_w, away_w, bias_own, cosine, sine)


def attend_body(block, idx_ref, qkv_ref, seg_col_ref, seg_row_ref,
                near_ref, away_ref, ctxt_ref, lse_ref, pick, ka, vt, qt, augt):
    rows = qkv_ref.shape[1]
    half = near_ref.shape[0]

    @pl.when(pl.program_id(0) == 0)
    def _():
        def fill(i, carry):
            span = pl.ds(pl.multiple_of(i * block, block), block)
            pick[span, :] = (
                lax.broadcasted_iota(jnp.int32, (block, rows), 1) == idx_ref[0, span, :]
            ).astype(BF)
            return carry

        lax.fori_loop(0, rows // block, fill, 0)
        lanes = lax.broadcasted_iota(jnp.int32, (rows, PAIR), 1)
        ka[:, PAIR:] = ((lanes == seg_col_ref[0]) | (lanes >= SEG_COUNT)).astype(BF)
        places = lax.broadcasted_iota(jnp.int32, (PAIR, rows), 0)
        augt[...] = jnp.where(
            (places < SEG_COUNT) & (places != seg_row_ref[0]), -FAR, 0.0
        ).astype(BF)

    ka[:, :PAIR] = qkv_ref[1]
    vt[...] = qkv_ref[2].T
    qt[...] = qkv_ref[0].T
    empty = jnp.zeros((HEAD, block), BF)

    def attended(span, keys):
        extra = augt[:, span]
        for h in range(2):
            mine = qt[h * HEAD:(h + 1) * HEAD, span]
            mixed = jnp.concatenate([mine, empty, extra] if h == 0 else [empty, mine, extra], axis=0)
            scores = dot(ka[keys, :], mixed)
            top = jnp.max(scores, axis=0, keepdims=True)
            expo = jnp.exp2(scores - top)
            total = jnp.sum(expo, axis=0, keepdims=True)
            context = dot(vt[h * HEAD:(h + 1) * HEAD, keys], expo.astype(BF))
            ctxt_ref[h * HEAD:(h + 1) * HEAD, span] = (context / total).astype(BF)
            lse_ref[0, h:h + 1, span] = top + jnp.log2(total)

    def step(i, carry):
        attended(pl.ds(pl.multiple_of(i * block, block), block), slice(0, LONGEST))
        return carry

    lax.fori_loop(0, LONGEST // block, step, 0)
    attended(slice(LONGEST, rows), slice(LONGEST, rows))
    given = dot(ctxt_ref[...], pick[...]).astype(BF)
    near_ref[...] = given[:, :half].T
    away_ref[...] = given[:, half:].T


def attend(b, idx_col, qkv, seg_col, seg_row, block=256):
    rows, share = qkv.shape[1:]
    pairs = share // PAIR
    half = rows // 2
    whole = lambda shape: pl.BlockSpec((1,) + shape, lambda j: (b, 0, 0))
    three = pl.BlockSpec((3, rows, PAIR), lambda j: (0, 0, j))
    column = lambda n: pl.BlockSpec((n, PAIR), lambda j: (0, j))
    return pl.pallas_call(
        functools.partial(attend_body, block),
        grid=(pairs,),
        in_specs=[whole((rows, 1)), three, whole((rows, 1)), whole((1, rows))],
        out_specs=[column(half), column(half), pl.BlockSpec((PAIR, rows), lambda j: (j, 0)),
                   pl.BlockSpec((1, 8, rows), lambda j: (j, 0, 0))],
        out_shape=[jax.ShapeDtypeStruct((half, share), BF), jax.ShapeDtypeStruct((half, share), BF),
                   jax.ShapeDtypeStruct((share, rows), BF),
                   jax.ShapeDtypeStruct((pairs, 8, rows), F32)],
        scratch_shapes=[pltpu.VMEM((rows, rows), BF), pltpu.VMEM((rows, 2 * PAIR), BF),
                        pltpu.VMEM((PAIR, rows), BF), pltpu.VMEM((PAIR, rows), BF),
                        pltpu.VMEM((PAIR, rows), BF)],
        compiler_params=pltpu.CompilerParams(vmem_limit_bytes=60 << 20),
        cost_estimate=pl.CostEstimate(
            flops=pairs * 2 * 2 * rows * rows * 3 * PAIR, bytes_accessed=2 * 6 * rows * share,
            transcendentals=2 * pairs * rows * rows,
        ),
        name="attend",
    )(idx_col, qkv, seg_col, seg_row)


def attend_back_body(block, idx_ref, qkv_ref, seg_col_ref, seg_row_ref, lse_ref,
                     ctxt_ref, gnear_ref, gaway_ref, cos_ref, sin_ref,
                     grads_ref,
                     pick, ka, va, kt, qt, dt, go, delta, dkacc, dvacc, dqt, augt):
    rows = qkv_ref.shape[1]
    half = gnear_ref.shape[0]

    @pl.when(pl.program_id(0) == 0)
    def _():
        def fill(i, carry):
            span = pl.ds(pl.multiple_of(i * block, block), block)
            pick[span, :] = (
                lax.broadcasted_iota(jnp.int32, (block, rows), 1) == idx_ref[0, span, :]
            ).astype(BF)
            return carry

        lax.fori_loop(0, rows // block, fill, 0)
        lanes = lax.broadcasted_iota(jnp.int32, (rows, PAIR), 1)
        ones = ((lanes == seg_col_ref[0]) | (lanes >= SEG_COUNT)).astype(BF)
        ka[:, PAIR:] = ones
        va[:, PAIR:] = jnp.ones((rows, PAIR), BF)
        places = lax.broadcasted_iota(jnp.int32, (8, rows), 0)
        augt[...] = jnp.where(
            (places < SEG_COUNT) & (places != seg_row_ref[0]), -FAR, 0.0
        )

    ka[:, :PAIR] = qkv_ref[1]
    va[:, :PAIR] = qkv_ref[2]
    kt[...] = qkv_ref[1].T
    qt[...] = qkv_ref[0].T
    grad = dot(pick[:, :half], gnear_ref[...]) + dot(pick[:, half:], gaway_ref[...])
    go[...] = grad.astype(BF)
    dt[...] = go[...].T
    weighed = dt[...].astype(F32) * ctxt_ref[...].astype(F32)
    delta[0:1, :] = jnp.sum(weighed[:HEAD], axis=0, keepdims=True)
    delta[1:2, :] = jnp.sum(weighed[HEAD:], axis=0, keepdims=True)
    dkacc[...] = jnp.zeros_like(dkacc)
    dvacc[...] = jnp.zeros_like(dvacc)
    empty = jnp.zeros((HEAD, block), BF)
    blank = jnp.zeros((PAIR - 16, block), BF)
    wide = lax.broadcasted_iota(jnp.int32, (block, PAIR), 1)
    zero = jnp.zeros((block, PAIR), BF)

    def thirds(row, start):
        first = row.astype(BF).astype(F32)
        second = (row - first).astype(BF).astype(F32)
        third = row - first - second
        places = lax.broadcasted_iota(jnp.int32, (16, block), 0)
        return jnp.where(places == start, first,
                         jnp.where(places == start + 1, second,
                                   jnp.where(places == start + 2, third, 0.0)))

    def attended(span, keys):
        base = jnp.concatenate([augt[:, span], jnp.zeros((8, block), F32)], axis=0)
        for h in range(2):
            part = slice(h * HEAD, (h + 1) * HEAD)
            low = (base + thirds(-lse_ref[0, h:h + 1, span], SEG_COUNT)).astype(BF)
            mine = qt[part, span]
            order = (mine, empty) if h == 0 else (empty, mine)
            scores = dot(ka[keys, :], jnp.concatenate(order + (low, blank), axis=0))
            probs = jnp.exp2(scores)
            low = thirds(-delta[h:h + 1, span], 0).astype(BF)
            mine = dt[part, span]
            order = (mine, empty) if h == 0 else (empty, mine)
            slope = dot(va[keys, :], jnp.concatenate(order + (low, blank), axis=0))
            grads = (probs * slope).astype(BF)
            keep = wide < HEAD if h == 0 else wide >= HEAD
            dvacc[keys, :] += dot(probs.astype(BF), jnp.where(keep, go[span, :], zero))
            dkacc[keys, :] += dot(grads, jnp.where(keep, qkv_ref[0, span, :], zero))
            dqt[part, span] = dot(kt[part, keys], grads)

    def step(i, carry):
        attended(pl.ds(pl.multiple_of(i * block, block), block), slice(0, LONGEST))
        return carry

    lax.fori_loop(0, LONGEST // block, step, 0)
    attended(slice(LONGEST, rows), slice(LONGEST, rows))
    cosine, sine = cos_ref[0], sin_ref[0]
    turned = dqt[...].T
    grads_ref[0] = ((turned * cosine - pair_swap(turned) * sine) * (1.0 / math.sqrt(HEAD))).astype(BF)
    turned = dkacc[...]
    grads_ref[1] = ((turned * cosine - pair_swap(turned) * sine) * LN2).astype(BF)
    grads_ref[2] = dvacc[...].astype(BF)


def attend_back(b, idx_col, qkv, seg_col, seg_row, lse, ctxt, gnear, gaway, cosine, sine, block=256):
    rows, share = qkv.shape[1:]
    pairs = share // PAIR
    half = rows // 2
    whole = lambda shape: pl.BlockSpec((1,) + shape, lambda j: (b, 0, 0))
    three = pl.BlockSpec((3, rows, PAIR), lambda j: (0, 0, j))
    column = lambda n: pl.BlockSpec((n, PAIR), lambda j: (0, j))
    return pl.pallas_call(
        functools.partial(attend_back_body, block),
        grid=(pairs,),
        in_specs=[whole((rows, 1)), three, whole((rows, 1)), whole((1, rows)),
                  pl.BlockSpec((1, 8, rows), lambda j: (j, 0, 0)),
                  pl.BlockSpec((PAIR, rows), lambda j: (j, 0)),
                  column(half), column(half), whole((rows, PAIR)), whole((rows, PAIR))],
        out_specs=pl.BlockSpec((3, rows, PAIR), lambda j: (0, 0, j)),
        out_shape=jax.ShapeDtypeStruct((3, rows, share), BF),
        scratch_shapes=[pltpu.VMEM((rows, rows), BF), pltpu.VMEM((rows, 2 * PAIR), BF),
                        pltpu.VMEM((rows, 2 * PAIR), BF), pltpu.VMEM((PAIR, rows), BF),
                        pltpu.VMEM((PAIR, rows), BF), pltpu.VMEM((PAIR, rows), BF),
                        pltpu.VMEM((rows, PAIR), BF), pltpu.VMEM((8, rows), F32),
                        pltpu.VMEM((rows, PAIR), F32), pltpu.VMEM((rows, PAIR), F32),
                        pltpu.VMEM((PAIR, rows), F32), pltpu.VMEM((8, rows), F32)],
        compiler_params=pltpu.CompilerParams(vmem_limit_bytes=60 << 20),
        cost_estimate=pl.CostEstimate(
            flops=pairs * 2 * 2 * rows * rows * 7 * PAIR, bytes_accessed=2 * 9 * rows * share,
            transcendentals=2 * pairs * rows * rows,
        ),
        name="attend_back",
    )(idx_col, qkv, seg_col, seg_row, lse, ctxt, gnear, gaway, cosine, sine)


def project_back_body(block, part_ref, g_ref, row_ref, wnear_ref, waway_ref,
                      near_ref, away_ref, work, hold, sems):
    rows, share = g_ref.shape[1:]
    half = near_ref.shape[0]
    for copy in own_columns(part_ref[0], wnear_ref, waway_ref, hold, sems):
        copy.wait()

    def step(i, carry):
        span = pl.ds(pl.multiple_of(i * block, block), block)
        total = None
        for place in range(3):
            term = dot_rt(g_ref[place, span, :], hold[:, place * share:(place + 1) * share])
            total = term if total is None else total + term
        work[span, :] = total.astype(BF)
        return carry

    lax.fori_loop(0, rows // block, step, 0)
    small = block // 2

    def back(i, carry):
        span = pl.ds(pl.multiple_of(i * small, small), small)
        for base, out_ref in ((half, away_ref), (0, near_ref)):
            pick = (lax.broadcasted_iota(jnp.int32, (small, rows), 0) + (base + i * small) == row_ref[0]).astype(BF)
            out_ref[span, :] = dot(pick, work[...]).astype(BF)
        return carry

    lax.fori_loop(0, half // small, back, 0)


def project_back(b, part, grads, idx_row, near_w, away_w, block=256):
    rows, share = grads.shape[1:]
    width = 2 * share
    half = rows // 2
    smem, anywhere = (pl.BlockSpec(memory_space=s) for s in (pltpu.SMEM, pl.ANY))
    return pl.pallas_call(
        functools.partial(project_back_body, block),
        grid=(1,),
        in_specs=[smem, pl.BlockSpec((3, rows, share), lambda i: (0, 0, 0)),
                  pl.BlockSpec((1, 1, rows), lambda i: (b, 0, 0)), anywhere, anywhere],
        out_specs=[pl.BlockSpec((half, width), lambda i: (0, 0))] * 2,
        scratch_shapes=[pltpu.VMEM((rows, width), BF), pltpu.VMEM((width, 3 * share), BF),
                        pltpu.SemaphoreType.DMA((6,))],
        out_shape=[jax.ShapeDtypeStruct((half, width), BF)] * 2,
        compiler_params=pltpu.CompilerParams(vmem_limit_bytes=40 << 20),
        cost_estimate=pl.CostEstimate(
            flops=2 * rows * width * (rows + 3 * share),
            bytes_accessed=2 * rows * (width + 3 * share) + 6 * width * share,
            transcendentals=0,
        ),
        name="project_back",
    )(part, grads, idx_row, near_w, away_w)


def weight_back_body(batches, *refs):
    xw_ref, g_refs, (gw_ref, gb_ref) = refs[0], refs[1:1 + batches], refs[1 + batches:]
    total, thin = None, None
    for b, g_ref in enumerate(g_refs):
        term = dot_lt(xw_ref[b], g_ref[0])
        line = jnp.sum(g_ref[0].astype(F32), axis=0, keepdims=True)
        total = term if total is None else total + term
        thin = line if thin is None else thin + line
    gw_ref[...] = total.astype(BF)
    gb_ref[...] = jnp.broadcast_to(thin, gb_ref.shape)


def weight_back(xws, grads):
    (batches, rows, width), share = xws.shape, grads[0].shape[2]
    each = pl.BlockSpec((1, rows, share), lambda s: (s, 0, 0))
    return pl.pallas_call(
        functools.partial(weight_back_body, batches),
        grid=(3,),
        in_specs=[pl.BlockSpec(xws.shape, lambda s: (0, 0, 0))] + [each] * batches,
        out_specs=[pl.BlockSpec((width, share), lambda s: (0, s)),
                   pl.BlockSpec((8, share), lambda s: (0, s))],
        out_shape=[jax.ShapeDtypeStruct((width, 3 * share), BF), jax.ShapeDtypeStruct((8, 3 * share), F32)],
        compiler_params=pltpu.CompilerParams(vmem_limit_bytes=60 << 20),
        cost_estimate=pl.CostEstimate(
            flops=2 * batches * rows * width * 3 * share,
            bytes_accessed=2 * batches * rows * (width + 3 * share) + 6 * width * share,
            transcendentals=0,
        ),
        name="weight_back",
    )(xws, *grads)


EPS = 1e-6
ERF_SLOPE = 0.3275911 * math.sqrt(0.5)
ERF_TERMS = (0.254829592, -0.284496736, 1.421413741, -1.453152027, 1.061405429)


def gauss_parts(u):
    bell = jnp.exp2(u * u * (-0.5 * LOG2E))
    t = 1.0 / (1.0 + ERF_SLOPE * jnp.abs(u))
    poly = 0.5 * ERF_TERMS[4]
    for term in ERF_TERMS[3::-1]:
        poly = poly * t + 0.5 * term
    tail = poly * t * bell
    below = jnp.where(u < 0.0, tail, 1.0 - tail)
    return u * below, below + u * bell * (1.0 / math.sqrt(2.0 * math.pi))


def row_mean(value):
    return jnp.sum(value, axis=1, keepdims=True) * (1.0 / value.shape[1])


def standard(hidden):
    centre = hidden - row_mean(hidden)
    root = lax.rsqrt(row_mean(centre * centre) + EPS)
    return centre * root, root


def standard_back(grad, norm, root):
    return root * (grad - row_mean(grad) - norm * row_mean(grad * norm))


def feed_body(chunk, part_ref, x_ref, near_ref, away_ref, dy_ref, thin_ref, bup_ref,
              unear_ref, uaway_ref, dnear_ref, daway_ref,
              out_ref, dh_ref, low_ref, act_ref, dup_ref, dlow_ref, da_ref, cnear_ref, caway_ref,
              sums_ref, bsum_ref, wo_near, wo_away, wup, wdown, slopes, sems):
    first_step = pl.program_id(0) == 0
    core = part_ref[0]
    width, wide = wup.shape
    share = near_ref.shape[1]
    half_w, half_f = width // 2, wide // 2

    def loads():
        copies = []
        for t, (u_ref, d_ref) in enumerate(((unear_ref, dnear_ref), (uaway_ref, daway_ref))):
            side = core if t == 0 else 1 - core
            hold = wo_near if t == 0 else wo_away
            copies += [
                pltpu.make_async_copy(u_ref.at[:, :width], hold, sems.at[t]),
                pltpu.make_async_copy(
                    u_ref.at[:, width:], wup.at[pl.ds(pl.multiple_of(side * half_w, 128), half_w), :],
                    sems.at[2 + t]),
                pltpu.make_async_copy(
                    d_ref, wdown.at[pl.ds(pl.multiple_of(side * half_f, 128), half_f), :], sems.at[4 + t]),
            ]
        return copies

    @pl.when(first_step)
    def _():
        copies = loads()
        for copy in copies:
            copy.start()
        sums_ref[...] = jnp.zeros_like(sums_ref)
        bsum_ref[...] = jnp.zeros_like(bsum_ref)
        for copy in copies:
            copy.wait()

    b_out, gain_one, shift_one, b_down, gain_two, shift_two = (thin_ref[i:i + 1, :] for i in range(6))

    def tally(row, value):
        sums_ref[row:row + 1, :] += jnp.sum(value, axis=0, keepdims=True)

    attended = dot(near_ref[...], wo_near[...]) + dot(away_ref[...], wo_away[...]) + b_out
    norm_one, root_one = standard(x_ref[...].astype(F32) + attended)
    first = norm_one * gain_one + shift_one
    low = first.astype(BF)

    low_ref[core] = low[:, :half_w]
    low_ref[1 - core] = low[:, half_w:]
    lowered = None
    for c in range(wide // chunk):
        cols = slice(c * chunk, (c + 1) * chunk)
        act, slope = gauss_parts(dot(low, wup[:, cols]) + bup_ref[:, cols])
        act = act.astype(BF)
        side = core if c * chunk < half_f else 1 - core
        act_ref[side, :, c * chunk % half_f:c * chunk % half_f + chunk] = act
        slopes[:, cols] = slope.astype(BF)
        term = dot(act, wdown[cols, :])
        lowered = term if lowered is None else lowered + term
    norm_two, root_two = standard(first + lowered + b_down)
    out_ref[...] = (norm_two * gain_two + shift_two).astype(BF)
    dy = dy_ref[...].astype(F32)
    tally(4, dy * norm_two)
    tally(5, dy)
    grad_two = standard_back(dy * gain_two, norm_two, root_two)
    dlow = grad_two.astype(BF)
    dlow_ref[...] = dlow
    tally(3, dlow.astype(F32))
    total = grad_two
    for c in range(wide // chunk):
        cols = slice(c * chunk, (c + 1) * chunk)
        dup = (dot_rt(dlow, wdown[cols, :]) * slopes[:, cols].astype(F32)).astype(BF)
        dup_ref[:, cols] = dup
        bsum_ref[0:1, cols] += jnp.sum(dup.astype(F32), axis=0, keepdims=True)
        total = total + dot_rt(dup, wup[:, cols])
    tally(1, total * norm_one)
    tally(2, total)
    grad_one = standard_back(total * gain_one, norm_one, root_one)
    dh_ref[...] = grad_one
    da = grad_one.astype(BF)
    da_ref[...] = da
    tally(0, da.astype(F32))
    cnear_ref[...] = dot_rt(da, wo_near[...]).astype(BF)
    caway_ref[...] = dot_rt(da, wo_away[...]).astype(BF)


def feed(part, x, near, away, dy, thin, bup, unear, uaway, dnear, daway, block=256, chunk=768):
    rows, width = x.shape
    share = near.shape[1]
    wide = bup.shape[1]
    line = lambda n: pl.BlockSpec((block, n), lambda i: (i, 0))
    pair = lambda n: pl.BlockSpec((2, block, n), lambda i: (0, i, 0))
    fixed = lambda shape: pl.BlockSpec(shape, lambda i: (0, 0))
    anywhere = pl.BlockSpec(memory_space=pl.ANY)
    shape = lambda n, dt: jax.ShapeDtypeStruct((rows, n), dt)
    return pl.pallas_call(
        functools.partial(feed_body, chunk),
        grid=(rows // block,),
        in_specs=[pl.BlockSpec(memory_space=pltpu.SMEM), line(width), line(share), line(share), line(width),
                  fixed(thin.shape), fixed(bup.shape), anywhere, anywhere, anywhere, anywhere],
        out_specs=[line(width), line(width), pair(width // 2), pair(wide // 2), line(wide), line(width), line(width),
                   line(share), line(share), fixed((8, width)), fixed((8, wide))],
        out_shape=[shape(width, BF), shape(width, F32),
                   jax.ShapeDtypeStruct((2, rows, width // 2), BF), jax.ShapeDtypeStruct((2, rows, wide // 2), BF),
                   shape(wide, BF), shape(width, BF), shape(width, BF), shape(share, BF), shape(share, BF),
                   jax.ShapeDtypeStruct((8, width), F32), jax.ShapeDtypeStruct((8, wide), F32)],
        scratch_shapes=[pltpu.VMEM((share, width), BF), pltpu.VMEM((share, width), BF),
                        pltpu.VMEM((width, wide), BF), pltpu.VMEM((wide, width), BF),
                        pltpu.VMEM((block, wide), BF), pltpu.SemaphoreType.DMA((6,))],
        compiler_params=pltpu.CompilerParams(vmem_limit_bytes=60 << 20),
        cost_estimate=pl.CostEstimate(
            flops=2 * rows * width * (2 * width + 4 * wide),
            bytes_accessed=2 * rows * (7 * width + 2 * wide) + 4 * width * (wide + width),
            transcendentals=2 * rows * wide,
        ),
        name="feed",
    )(part, x, near, away, dy, thin, bup, unear, uaway, dnear, daway)


def swap_cores(value):
    return lax.ppermute(value, "seq", [(0, 1), (1, 0)])


def swap_x(value):
    return lax.ppermute(value, "fsdp", [(i, i ^ 1) for i in range(16)])


def swap_y(value):
    return lax.ppermute(value, "fsdp", [(i, i ^ 2) for i in range(16)])


def shift_z(value, k):
    return lax.ppermute(value, "fsdp", [(i, (i + 4 * k) % 16) for i in range(16)])


def assemble_body(lines, place_ref, ax_ref, ay_ref, bx_ref, by_ref, *out_refs):
    place = place_ref[0]
    z, y, x = place // 4, (place // 2) % 2, place % 2
    n = ax_ref.shape[1]

    def put(owner, piece):
        out_refs[0][owner] = piece[:, :out_refs[0].shape[2]]
        for c in range(lines):
            width = out_refs[1].shape[2]
            at = out_refs[0].shape[2] + c * width
            out_refs[1][owner, c * n:(c + 1) * n, :] = piece[:, at:at + width]

    for j in range(4):
        k, o = j % 2, j // 2
        near_z, far_z = lax.rem(z - k + 4, 4), lax.rem(z - k + 2, 4)
        flip_x = lax.rem(x + o, 2)
        flip_y = lax.rem(y + o, 2)
        put(near_z * 4 + y * 2 + flip_x, ax_ref[j])
        put(near_z * 4 + (1 - y) * 2 + flip_x, ay_ref[j])
        put(far_z * 4 + flip_y * 2 + x, by_ref[j])
        put(far_z * 4 + flip_y * 2 + 1 - x, bx_ref[j])


def assemble(place, parts, lines=0, line=0):
    n, width = parts[0].shape[1:]
    vmem = pl.BlockSpec(memory_space=pltpu.VMEM)
    shapes = [(16, n, width - lines * line)] + ([(16, lines * n, line)] if lines else [])
    return pl.pallas_call(
        functools.partial(assemble_body, lines),
        in_specs=[pl.BlockSpec(memory_space=pltpu.SMEM)] + [vmem] * 4,
        out_shape=[jax.ShapeDtypeStruct(shape, BF) for shape in shapes],
        compiler_params=pltpu.CompilerParams(vmem_limit_bytes=40 << 20),
        cost_estimate=pl.CostEstimate(flops=0, bytes_accessed=4 * 16 * n * width, transcendentals=0),
        name="assemble",
    )(place, *parts)


def tie(values, after=()):
    return lax.optimization_barrier((values, after))[0]


def reach_z(shard):
    first = jnp.stack([shard, shift_z(shard, 1)])
    second = jnp.stack([shift_z(shard, 2), shift_z(shard, 3)])
    return first, second


def reach_one(first, second):
    return jnp.concatenate([first, swap_x(first)], axis=0), jnp.concatenate([second, swap_y(second)], axis=0)


def reach_two(first, second):
    return first, swap_y(first), swap_x(second), second


def joined(parts, lines=0, line=0):
    place = jnp.full((1,), lax.axis_index("fsdp"), jnp.int32)
    return [value.reshape(-1, value.shape[2]) for value in assemble(place, parts, lines, line)]


def pick(part, at, axis):
    return lax.dynamic_index_in_dim(part, at, axis, keepdims=False)


def corner():
    place = lax.axis_index("fsdp")
    return place // 4, (place // 2) % 2, place % 2


def fold_one(value):
    z, y, x = corner()
    rows, width = value.shape
    cube = value.reshape(2, 2, 2, 2, rows // 16, width)
    return (value,), (pick(cube[0], 1 - y, 1).astype(BF), pick(cube[1], 1 - x, 2).astype(BF))


def fold_two(stay, sends, after=()):
    z, y, x = corner()
    rows, width = stay[0].shape
    cube = stay[0].reshape(2, 2, 2, 2, rows // 16, width)
    came = tie((swap_y(sends[0]), swap_x(sends[1])), after)
    first = pick(cube[0], y, 1).astype(F32) + came[0].astype(F32)
    second = pick(cube[1], x, 2).astype(F32) + came[1].astype(F32)
    return (first, second), (pick(first, 1 - x, 1).astype(BF), pick(second, 1 - y, 1).astype(BF))


def fold_cross(stay, sends):
    z, y, x = corner()
    first = pick(stay[0], x, 1) + swap_x(sends[0]).astype(F32)
    second = pick(stay[1], y, 1) + swap_y(sends[1]).astype(F32)
    return jnp.concatenate([first, second], axis=0)


def fold_three(stack):
    z = corner()[0]
    return (pick(stack, z, 0),), tuple(pick(stack, lax.rem(z + k, 4), 0).astype(BF) for k in (1, 2, 3))


def fold_end(stay, sends, after=()):
    total = stay[0]
    for came in tie([shift_z(send, k) for k, send in zip((1, 2, 3), sends)], after):
        total = total + came.astype(F32)
    return total


def on_device(tokens, permutation, segment_ids, cotangent, *shards):
    batches = tokens.shape[0]
    half, width = tokens.shape[2], tokens.shape[3]
    core = lax.axis_index("seq")
    share = width // 2
    owners = 2 * lax.axis_size("fsdp")
    staged = owners == 32
    part = jnp.full((1,), core, jnp.int32)
    thin = [i for i, piece in enumerate(shards) if piece.ndim == 1]
    sizes = [shards[i].shape[0] for i in thin]
    count = sum(sizes)
    n_qkv = shards[0].shape[0]
    room = n_qkv * 128
    tokens, cotangent = tokens[:, 0], cotangent[:, 0]

    away_tokens = swap_cores(tokens)
    idx_col, idx_row, seg_col, seg_row, cosine, sine = ready(part, permutation[:, 0], segment_ids[:, 0])
    xws = arrange(idx_col, tokens, away_tokens)
    if staged:
        lanes = jnp.concatenate(
            [jnp.pad(shards[i][None], ((0, 0), (0, 128 - size))) for i, size in zip(thin, sizes)]
            + [jnp.zeros((n_qkv - len(thin), 128), BF)], axis=0)
        q_shard = jnp.concatenate([shards[0], lanes], axis=1)
        ud_shard = jnp.concatenate(
            [shards[2], shards[6]] + [shards[8][i * n_qkv:(i + 1) * n_qkv] for i in range(4)], axis=1)
        first, second = reach_z(q_shard)
        first_x, second_y = swap_x(first), swap_y(second)
        ud_shard = tie(ud_shard, first_x)
        q_parts = reach_two(jnp.concatenate([first, first_x], axis=0), jnp.concatenate([second, second_y], axis=0))
        ud_z = tuple(shift_z(ud_shard, k) for k in (1, 2, 3))
        q_parts = tie(q_parts, (xws, cosine))
        (q_near,) = joined(q_parts)
    else:
        packed = jnp.concatenate([shards[i] for i in thin] + [jnp.zeros((room - count,), BF)])
        q_shard = jnp.concatenate([shards[0], packed.reshape(n_qkv, 128)], axis=1)
        q_near = lax.all_gather(q_shard, "fsdp", axis=0, tiled=True)
        u_near = lax.all_gather(jnp.concatenate([shards[2], shards[6]], axis=1), "fsdp", axis=0, tiled=True)
        d_near = lax.all_gather(shards[8], "fsdp", axis=0, tiled=True)
    q_away = swap_cores(q_near)

    slabs = [value[:, 3 * width:].reshape(owners // 2, n_qkv, 128) for value in (q_near, q_away)]
    vectors = jnp.concatenate(
        [jnp.where(core == 0, slabs[0], slabs[1]), jnp.where(core == 0, slabs[1], slabs[0])], axis=0
    ).astype(F32)
    spread, at = [], 0
    for i, size in enumerate(sizes):
        if staged:
            spread.append(vectors[:, i, :size].reshape(1, owners * size))
        else:
            spread.append(vectors.reshape(owners, room)[:, at:at + size].reshape(1, owners * size))
        at += size
    b_qkv, b_out, gain_one, shift_one, b_up, b_down, gain_two, shift_two = spread
    bias_own = jnp.concatenate(
        [lax.dynamic_slice_in_dim(b_qkv, core * share + s * width, share, 1) for s in range(3)], axis=1
    )
    blank_row = jnp.zeros((1, width), F32)
    thin_rows = jnp.concatenate(
        [b_out, gain_one, shift_one, b_down, gain_two, shift_two, blank_row, blank_row], axis=0
    )

    qkvs = [project(b, part, xws, q_near, q_away, bias_own, cosine, sine) for b in range(batches)]
    if staged:
        (one, two, three), qkvs = tie((ud_z, qkvs))
        first, second = jnp.stack([ud_shard, one]), jnp.stack([two, three])
        qkvs[0], first, second = tie((qkvs[0], first, second))
        first_x, second_y = swap_x(first), swap_y(second)
    kept, ctxs = [], []
    for b in range(batches):
        if staged and b == 1:
            first_x, second_y = tie((first_x, second_y), ctxs[0][0])
            first, second = jnp.concatenate([first, first_x], axis=0), jnp.concatenate([second, second_y], axis=0)
            qkvs[1], first, second = tie((qkvs[1], first, second))
            first_y, second_x = swap_y(first), swap_x(second)
        near, away, ctxt, lse = attend(b, idx_col, qkvs[b], seg_col, seg_row)
        kept.append((qkvs[b], ctxt, lse))
        ctxs.append((near, swap_cores(away)))
    if staged:
        first_y, second_x = tie((first_y, second_x), ctxs[1][0])
        u_near, d_near = joined((first, first_y, second_x, second), 4, width)
    u_away, d_away = swap_cores(u_near), swap_cores(d_near)
    near, away = (jnp.concatenate([item[i] for item in ctxs], axis=0) for i in range(2))
    (outputs, grad_one, low, act, dup, dlow, da, cnear, caway, sums, bsum) = feed(
        part, tokens.reshape(batches * half, width), near, away,
        cotangent.reshape(batches * half, width), thin_rows, b_up, u_near, u_away, d_near, d_away,
    )
    caway = swap_cores(caway)

    d_theirs = swap_cores(dot_lt(act[1], dlow).astype(BF))
    uo_theirs = swap_cores(
        jnp.concatenate([dot_lt(low[1], dup).astype(BF), dot_lt(away, da).astype(BF)], axis=1)
    )
    d_sum = (dot_lt(act[0], dlow) + d_theirs.astype(F32)).astype(BF)
    uo_sum = jnp.concatenate([
        (dot_lt(low[0], dup) + uo_theirs[:, :4 * width].astype(F32)).astype(BF),
        (dot_lt(near, da) + uo_theirs[:, 4 * width:].astype(F32)).astype(BF),
    ], axis=1)

    def back(b, given):
        qkv, ctxt, lse = kept[b]
        return attend_back(b, idx_col, qkv, seg_col, seg_row, lse, ctxt, *given, cosine, sine)

    givens = [(cnear[b * half:(b + 1) * half], caway[b * half:(b + 1) * half]) for b in range(batches)]
    if staged:
        given, d_step, uo_step = tie((givens[0], fold_one(d_sum), fold_one(uo_sum)))
        first_back = back(0, given)
        given, d_step, uo_step = tie((givens[1], fold_two(*d_step), fold_two(*uo_step)), first_back)
        grads = [first_back, back(1, given)]
        wide, lines = fold_cross(*uo_step), fold_cross(*d_step)
        lines = [lines[:, i * n_qkv:(i + 1) * n_qkv] for i in range(4)]
        du_step = fold_three(jnp.concatenate([wide] + lines, axis=2))
        grads, du_step = tie((grads, du_step))
    else:
        grads = [back(b, givens[b]) for b in range(batches)]
    gw_own, gb_own = weight_back(xws, grads)

    def halves(value):
        size = value.shape[0] // 2
        return (lax.dynamic_slice_in_dim(value, core * size, size, 0),
                lax.dynamic_slice_in_dim(value, (1 - core) * size, size, 0))

    blank = jnp.zeros((share,), F32)
    thin_columns = []
    for s in range(3):
        span = slice(s * share, (s + 1) * share)
        thin_columns += [jnp.where(core == 0, gb_own[0, span], blank),
                         jnp.where(core == 0, blank, gb_own[0, span])]
    thin_grads = [jnp.concatenate(thin_columns), sums[0], sums[1], sums[2], bsum[0], sums[3], sums[4], sums[5]]
    slab = jnp.concatenate(
        [value.reshape(owners, -1) for value in thin_grads] + [jnp.zeros((owners, room - count), F32)], axis=1
    ).astype(BF).reshape(owners * n_qkv, 128)
    mine, theirs = (jnp.concatenate(pair, axis=1) for pair in zip(halves(gw_own), halves(slab)))
    theirs = swap_cores(theirs)
    q_sum = jnp.concatenate([
        mine[:, :3 * share], theirs[:, :3 * share],
        (mine[:, 3 * share:].astype(F32) + theirs[:, 3 * share:].astype(F32)).astype(BF),
    ], axis=1)
    backs = [project_back(0, part, grads[0], idx_row, q_near, q_away)]
    if staged:
        last, q_step, backs = tie((grads[1], fold_one(q_sum), backs))
        backs.append(project_back(1, part, last, idx_row, q_near, q_away))
        q_step = fold_two(*q_step, backs[1])
        q_last = fold_three(fold_cross(*q_step))
        g_uo = fold_end(*du_step, q_last)
        g_qkv = fold_end(*q_last, g_uo)
        g_down = jnp.concatenate([g_uo[:, (5 + i) * width:(6 + i) * width] for i in range(4)], axis=0)
    else:
        backs.append(project_back(1, part, grads[1], idx_row, q_near, q_away))
        summed = lambda value: lax.psum_scatter(
            value.astype(BF), "fsdp", scatter_dimension=0, tiled=True
        ).astype(F32)
        g_qkv, g_down, g_uo = summed(q_sum), summed(d_sum), summed(uo_sum)
    own, other = g_qkv[:, :3 * share], g_qkv[:, 3 * share:6 * share]
    columns = []
    for s in range(3):
        span = slice(s * share, (s + 1) * share)
        columns += [jnp.where(core == 0, own[:, span], other[:, span]),
                    jnp.where(core == 0, other[:, span], own[:, span])]
    g_out, g_up = g_uo[:, 4 * width:5 * width], g_uo[:, :4 * width]
    grad_one = grad_one.reshape(batches, half, width)
    token_grad = jnp.stack([
        (grad_one[b] + backs[b][0].astype(F32) + swap_cores(backs[b][1]).astype(F32)).astype(BF)
        for b in range(batches)
    ])
    flat = g_qkv[:, 3 * width:].reshape(room)
    thin_out, at = [], 0
    for size in sizes:
        thin_out.append(flat[at:at + size])
        at += size
    g_bqkv, g_bout, g_g1, g_s1, g_bup, g_bdown, g_g2, g_s2 = thin_out
    return (
        outputs.reshape(batches, 1, half, width), token_grad[:, None],
        jnp.concatenate(columns, axis=1), g_bqkv, g_out, g_bout, g_g1, g_s1, g_up, g_bup, g_down, g_bdown, g_g2, g_s2,
    )


def solution(mesh):
    packs = P(None, "fsdp", "seq", None)
    ids = P(None, "fsdp", None)
    deep, flat = P(("seq", "fsdp"), None), P(("seq", "fsdp"))
    layers = (deep, flat, deep, flat, flat, flat, deep, flat, deep, flat, flat, flat)
    return jax.shard_map(
        on_device, mesh=mesh, in_specs=(packs, ids, ids, packs) + layers,
        out_specs=(packs, packs) + layers, check_vma=False,
    )
```

```python
import functools
import math

import jax
import jax.numpy as jnp
from jax import lax
from jax.experimental import pallas as pl
from jax.experimental.pallas import tpu as pltpu
from jax.sharding import PartitionSpec as P

HEAD = 64
PAIR = 2 * HEAD
SEG_COUNT = 4
LONGEST = 1024
LOG2E = math.log2(math.e)
LN2 = math.log(2.0)
FAR = float(2**30)
BF = jnp.bfloat16
F32 = jnp.float32


def dot(left, right):
    return jnp.dot(left, right, preferred_element_type=F32)


def dot_rt(left, right):
    return lax.dot_general(left, right, (((1,), (1,)), ((), ())), preferred_element_type=F32)


def dot_lt(left, right):
    return lax.dot_general(left, right, (((0,), (0,)), ((), ())), preferred_element_type=F32)


def pair_swap(values):
    lanes = lax.broadcasted_iota(jnp.int32, values.shape, 1)
    width = values.shape[1]
    return jnp.where(
        lanes % 2 == 0, pltpu.roll(values, width - 1, 1), pltpu.roll(values, 1, 1)
    )


def ready_body(part_ref, order_ref, seg_ref, freq_ref, idx_col, idx_row, seg_col, seg_row, cos_ref, sin_ref):
    core = part_ref[0]
    batches, rows = order_ref.shape
    half = rows // 2
    lanes = lax.broadcasted_iota(jnp.int32, (1, rows), 1)
    wide = lax.broadcasted_iota(jnp.int32, (8, rows), 1)
    halves = freq_ref.shape[0]
    cols = lax.broadcasted_iota(jnp.int32, (halves, PAIR), 1)
    lines = lax.broadcasted_iota(jnp.int32, (halves, PAIR), 0)
    grow = ((cols % HEAD) // 2 == lines).astype(F32)
    turn = jnp.where(cols % 2 == 0, -grow, grow)
    expand = lambda value, by: lax.dot_general(
        value, by, (((0,), (0,)), ((), ())), preferred_element_type=F32, precision=lax.Precision.HIGHEST)
    for b in range(batches):
        order, seg = order_ref[b:b + 1, :], seg_ref[b:b + 1, :]
        starts, start, total = [], 0, 0
        for s in range(SEG_COUNT):
            size = jnp.sum((seg == s).astype(F32)).astype(jnp.int32)
            starts.append(total)
            start = start + jnp.where(size == LONGEST, total, 0)
            total = total + size
        table = jnp.concatenate([order, seg, lanes, jnp.zeros((5, rows), jnp.int32)], axis=0)
        main = pltpu.roll(table, rows - start, 1)
        early = pltpu.roll(table, LONGEST, 1)
        table = jnp.where(wide < LONGEST, main, jnp.where(wide - LONGEST < start, early, table))
        order, seg, place = table[0:1], table[1:2], table[2:3]
        origin = jnp.zeros_like(seg)
        for s in range(1, SEG_COUNT):
            origin = jnp.where(seg == s, starts[s], origin)
        position = (place - origin).astype(F32)
        near = (order >= half).astype(jnp.int32) == core
        idx = jnp.where(near, order - core * half, order + core * half)
        idx_row[b] = idx
        seg_row[b] = seg
        both = jnp.concatenate([idx.astype(F32), seg.astype(F32), jnp.zeros((6, rows), F32)], axis=0).T
        idx_col[b] = both[:, 0:1].astype(jnp.int32)
        seg_col[b] = both[:, 1:2].astype(jnp.int32)
        phase = freq_ref[...] * position
        cos_ref[b] = expand(jnp.cos(phase), grow)
        sin_ref[b] = expand(jnp.sin(phase), turn)


def ready(part, order, segments):
    batches, rows = order.shape
    halves = HEAD // 2
    freqs = jnp.exp(jnp.arange(halves, dtype=F32) * (-2.0 * math.log(10000.0) / HEAD))[:, None]
    vmem, smem = (pl.BlockSpec(memory_space=s) for s in (pltpu.VMEM, pltpu.SMEM))
    ints = lambda *shape: jax.ShapeDtypeStruct(shape, jnp.int32)
    return pl.pallas_call(
        ready_body,
        in_specs=[smem, vmem, vmem, vmem],
        out_shape=[ints(batches, rows, 1), ints(batches, 1, rows), ints(batches, rows, 1), ints(batches, 1, rows),
                   jax.ShapeDtypeStruct((batches, rows, PAIR), F32), jax.ShapeDtypeStruct((batches, rows, PAIR), F32)],
        compiler_params=pltpu.CompilerParams(vmem_limit_bytes=40 << 20),
        cost_estimate=pl.CostEstimate(
            flops=1 << 30, bytes_accessed=8 * batches * rows * 3 * PAIR, transcendentals=2 * batches * rows * halves
        ),
        name="ready",
    )(part, order, segments, freqs)


def pack_body(thin, w_qkv, w_out, w_up, w_down, *refs):
    q_ref, ud_ref = refs[thin:]
    n, width = w_out.shape
    wide = w_qkv.shape[1]
    q_ref[:, :wide] = w_qkv[...]
    q_ref[:, wide:] = jnp.zeros((n, q_ref.shape[1] - wide), BF)
    for i, ref in enumerate(refs[:thin]):
        q_ref[i:i + 1, wide:wide + ref.shape[1]] = ref[...]
    ud_ref[:, :width] = w_out[...]
    ud_ref[:, width:width + w_up.shape[1]] = w_up[...]
    at = width + w_up.shape[1]
    for c in range(w_down.shape[0] // n):
        ud_ref[:, at + c * width:at + (c + 1) * width] = w_down[c * n:(c + 1) * n, :]


def pack(w_qkv, w_out, w_up, w_down, thin):
    n, width = w_out.shape
    wide = width + w_up.shape[1] + w_down.shape[0] // n * width
    return pl.pallas_call(
        functools.partial(pack_body, len(thin)),
        out_shape=[jax.ShapeDtypeStruct((n, w_qkv.shape[1] + 128), BF), jax.ShapeDtypeStruct((n, wide), BF)],
        cost_estimate=pl.CostEstimate(flops=0, bytes_accessed=4 * n * (w_qkv.shape[1] + wide), transcendentals=0),
        name="pack",
    )(w_qkv, w_out, w_up, w_down, *[value[None] for value in thin])


def arrange_body(block, idx_ref, own_ref, other_ref, xw_ref):
    half = own_ref.shape[1]

    def step(i, carry):
        rows = pl.ds(pl.multiple_of(i * block, block), block)
        picks = lax.broadcasted_iota(jnp.int32, (block, half), 1)
        source = idx_ref[0, rows, :]
        near = (picks == source).astype(BF)
        away = (picks + half == source).astype(BF)
        xw_ref[0, rows, :] = (dot(near, own_ref[0]) + dot(away, other_ref[0])).astype(BF)
        return carry

    lax.fori_loop(0, idx_ref.shape[1] // block, step, 0)


def arrange(idx_col, own, other, block=256):
    batches, rows = idx_col.shape[:2]
    half, width = own.shape[1:]
    each = lambda *shape: pl.BlockSpec((1,) + shape, lambda b: (b, 0, 0))
    return pl.pallas_call(
        functools.partial(arrange_body, block),
        grid=(batches,),
        in_specs=[each(rows, 1), each(half, width), each(half, width)],
        out_specs=each(rows, width),
        out_shape=jax.ShapeDtypeStruct((batches, rows, width), BF),
        compiler_params=pltpu.CompilerParams(vmem_limit_bytes=40 << 20),
        cost_estimate=pl.CostEstimate(
            flops=2 * batches * rows * rows * width, bytes_accessed=4 * batches * rows * width, transcendentals=0
        ),
        name="arrange",
    )(idx_col, own, other)


def own_columns(core, near_ref, away_ref, hold, sems):
    span, share = near_ref.shape[0], hold.shape[1] // 3
    copies = []
    for s in range(3):
        for t, ref in enumerate((near_ref, away_ref)):
            side = core if t == 0 else 1 - core
            copies.append(
                pltpu.make_async_copy(
                    ref.at[:, pl.ds(pl.multiple_of(core * share + 2 * s * share, 128), share)],
                    hold.at[pl.ds(pl.multiple_of(side * span, 128), span), s * share:(s + 1) * share],
                    sems.at[2 * s + t],
                )
            )
    for copy in copies:
        copy.start()
    return copies


def project_body(block, part_ref, xw_ref, near_ref, away_ref, bias_ref, cos_ref, sin_ref,
                 qkv_ref, hold, sems):
    share = qkv_ref.shape[2]
    for copy in own_columns(part_ref[0], near_ref, away_ref, hold, sems):
        copy.wait()

    def step(i, carry):
        rows = pl.ds(pl.multiple_of(i * block, block), block)
        work = xw_ref[0, rows, :]
        cosine, sine = cos_ref[0, rows, :], sin_ref[0, rows, :]
        for place, scale in ((0, LOG2E / math.sqrt(HEAD)), (1, 1.0)):
            whole = slice(place * share, (place + 1) * share)
            pre = dot(work, hold[:, whole]) + bias_ref[:, whole]
            for j in range(share // PAIR):
                cols = slice(j * PAIR, (j + 1) * PAIR)
                piece = pre[:, cols]
                qkv_ref[place, rows, cols] = (
                    (piece * cosine + pair_swap(piece) * sine) * scale
                ).astype(BF)
        qkv_ref[2, rows, :] = (dot(work, hold[:, 2 * share:]) + bias_ref[:, 2 * share:]).astype(BF)
        return carry

    lax.fori_loop(0, xw_ref.shape[1] // block, step, 0)


def project(b, part, xws, near_w, away_w, bias_own, cosine, sine, block=256):
    rows, width = xws.shape[1:]
    share = bias_own.shape[1] // 3
    each = lambda n: pl.BlockSpec((1, rows, n), lambda i: (b, 0, 0))
    vmem, smem, anywhere = (pl.BlockSpec(memory_space=s) for s in (pltpu.VMEM, pltpu.SMEM, pl.ANY))
    return pl.pallas_call(
        functools.partial(project_body, block),
        grid=(1,),
        in_specs=[smem, each(width), anywhere, anywhere, vmem, each(PAIR), each(PAIR)],
        out_specs=pl.BlockSpec((3, rows, share), lambda i: (0, 0, 0)),
        out_shape=jax.ShapeDtypeStruct((3, rows, share), BF),
        scratch_shapes=[pltpu.VMEM((width, 3 * share), BF), pltpu.SemaphoreType.DMA((6,))],
        compiler_params=pltpu.CompilerParams(vmem_limit_bytes=40 << 20),
        cost_estimate=pl.CostEstimate(
            flops=2 * rows * width * 3 * share,
            bytes_accessed=2 * (rows * width + 3 * width * share + 3 * rows * share),
            transcendentals=0,
        ),
        name="project",
    )(part, xws, near_w, away_w, bias_own, cosine, sine)


def attend_body(block, idx_ref, qkv_ref, seg_col_ref, seg_row_ref,
                near_ref, away_ref, ctxt_ref, lse_ref, pick, ka, vt, qt, augt):
    rows = qkv_ref.shape[1]
    half = near_ref.shape[0]

    @pl.when(pl.program_id(0) == 0)
    def _():
        def fill(i, carry):
            span = pl.ds(pl.multiple_of(i * block, block), block)
            pick[span, :] = (
                lax.broadcasted_iota(jnp.int32, (block, rows), 1) == idx_ref[0, span, :]
            ).astype(BF)
            return carry

        lax.fori_loop(0, rows // block, fill, 0)
        lanes = lax.broadcasted_iota(jnp.int32, (rows, PAIR), 1)
        ka[:, PAIR:] = ((lanes == seg_col_ref[0]) | (lanes >= SEG_COUNT)).astype(BF)
        places = lax.broadcasted_iota(jnp.int32, (PAIR, rows), 0)
        augt[...] = jnp.where(
            (places < SEG_COUNT) & (places != seg_row_ref[0]), -FAR, 0.0
        ).astype(BF)

    ka[:, :PAIR] = qkv_ref[1]
    vt[...] = qkv_ref[2].T
    qt[...] = qkv_ref[0].T
    empty = jnp.zeros((HEAD, block), BF)

    def attended(span, keys):
        extra = augt[:, span]
        for h in range(2):
            mine = qt[h * HEAD:(h + 1) * HEAD, span]
            mixed = jnp.concatenate([mine, empty, extra] if h == 0 else [empty, mine, extra], axis=0)
            scores = dot(ka[keys, :], mixed)
            top = jnp.max(scores, axis=0, keepdims=True)
            expo = jnp.exp2(scores - top)
            total = jnp.sum(expo, axis=0, keepdims=True)
            context = dot(vt[h * HEAD:(h + 1) * HEAD, keys], expo.astype(BF))
            ctxt_ref[h * HEAD:(h + 1) * HEAD, span] = (context / total).astype(BF)
            lse_ref[0, h:h + 1, span] = top + jnp.log2(total)

    def step(i, carry):
        attended(pl.ds(pl.multiple_of(i * block, block), block), slice(0, LONGEST))
        return carry

    lax.fori_loop(0, LONGEST // block, step, 0)
    attended(slice(LONGEST, rows), slice(LONGEST, rows))
    given = dot(ctxt_ref[...], pick[...]).astype(BF)
    near_ref[...] = given[:, :half].T
    away_ref[...] = given[:, half:].T


def attend(b, idx_col, qkv, seg_col, seg_row, block=256):
    rows, share = qkv.shape[1:]
    pairs = share // PAIR
    half = rows // 2
    whole = lambda shape: pl.BlockSpec((1,) + shape, lambda j: (b, 0, 0))
    three = pl.BlockSpec((3, rows, PAIR), lambda j: (0, 0, j))
    column = lambda n: pl.BlockSpec((n, PAIR), lambda j: (0, j))
    return pl.pallas_call(
        functools.partial(attend_body, block),
        grid=(pairs,),
        in_specs=[whole((rows, 1)), three, whole((rows, 1)), whole((1, rows))],
        out_specs=[column(half), column(half), pl.BlockSpec((PAIR, rows), lambda j: (j, 0)),
                   pl.BlockSpec((1, 8, rows), lambda j: (j, 0, 0))],
        out_shape=[jax.ShapeDtypeStruct((half, share), BF), jax.ShapeDtypeStruct((half, share), BF),
                   jax.ShapeDtypeStruct((share, rows), BF),
                   jax.ShapeDtypeStruct((pairs, 8, rows), F32)],
        scratch_shapes=[pltpu.VMEM((rows, rows), BF), pltpu.VMEM((rows, 2 * PAIR), BF),
                        pltpu.VMEM((PAIR, rows), BF), pltpu.VMEM((PAIR, rows), BF),
                        pltpu.VMEM((PAIR, rows), BF)],
        compiler_params=pltpu.CompilerParams(vmem_limit_bytes=60 << 20),
        cost_estimate=pl.CostEstimate(
            flops=pairs * 2 * 2 * rows * rows * 3 * PAIR, bytes_accessed=2 * 6 * rows * share,
            transcendentals=2 * pairs * rows * rows,
        ),
        name="attend",
    )(idx_col, qkv, seg_col, seg_row)


def attend_back_body(block, idx_ref, qkv_ref, seg_col_ref, seg_row_ref, lse_ref,
                     ctxt_ref, gnear_ref, gaway_ref, cos_ref, sin_ref,
                     grads_ref,
                     pick, ka, va, kt, qt, dt, go, delta, dkacc, dvacc, dqt, augt):
    rows = qkv_ref.shape[1]
    half = gnear_ref.shape[0]

    @pl.when(pl.program_id(0) == 0)
    def _():
        def fill(i, carry):
            span = pl.ds(pl.multiple_of(i * block, block), block)
            pick[span, :] = (
                lax.broadcasted_iota(jnp.int32, (block, rows), 1) == idx_ref[0, span, :]
            ).astype(BF)
            return carry

        lax.fori_loop(0, rows // block, fill, 0)
        lanes = lax.broadcasted_iota(jnp.int32, (rows, PAIR), 1)
        ones = ((lanes == seg_col_ref[0]) | (lanes >= SEG_COUNT)).astype(BF)
        ka[:, PAIR:] = ones
        va[:, PAIR:] = jnp.ones((rows, PAIR), BF)
        places = lax.broadcasted_iota(jnp.int32, (8, rows), 0)
        augt[...] = jnp.where(
            (places < SEG_COUNT) & (places != seg_row_ref[0]), -FAR, 0.0
        )

    ka[:, :PAIR] = qkv_ref[1]
    va[:, :PAIR] = qkv_ref[2]
    kt[...] = qkv_ref[1].T
    qt[...] = qkv_ref[0].T
    grad = dot(pick[:, :half], gnear_ref[...]) + dot(pick[:, half:], gaway_ref[...])
    go[...] = grad.astype(BF)
    dt[...] = go[...].T
    weighed = dt[...].astype(F32) * ctxt_ref[...].astype(F32)
    delta[0:1, :] = jnp.sum(weighed[:HEAD], axis=0, keepdims=True)
    delta[1:2, :] = jnp.sum(weighed[HEAD:], axis=0, keepdims=True)
    dkacc[...] = jnp.zeros_like(dkacc)
    dvacc[...] = jnp.zeros_like(dvacc)
    empty = jnp.zeros((HEAD, block), BF)
    blank = jnp.zeros((PAIR - 16, block), BF)
    wide = lax.broadcasted_iota(jnp.int32, (block, PAIR), 1)
    zero = jnp.zeros((block, PAIR), BF)

    def thirds(row, start):
        first = row.astype(BF).astype(F32)
        second = (row - first).astype(BF).astype(F32)
        third = row - first - second
        places = lax.broadcasted_iota(jnp.int32, (16, block), 0)
        return jnp.where(places == start, first,
                         jnp.where(places == start + 1, second,
                                   jnp.where(places == start + 2, third, 0.0)))

    def attended(span, keys):
        base = jnp.concatenate([augt[:, span], jnp.zeros((8, block), F32)], axis=0)
        for h in range(2):
            part = slice(h * HEAD, (h + 1) * HEAD)
            low = (base + thirds(-lse_ref[0, h:h + 1, span], SEG_COUNT)).astype(BF)
            mine = qt[part, span]
            order = (mine, empty) if h == 0 else (empty, mine)
            scores = dot(ka[keys, :], jnp.concatenate(order + (low, blank), axis=0))
            probs = jnp.exp2(scores)
            low = thirds(-delta[h:h + 1, span], 0).astype(BF)
            mine = dt[part, span]
            order = (mine, empty) if h == 0 else (empty, mine)
            slope = dot(va[keys, :], jnp.concatenate(order + (low, blank), axis=0))
            grads = (probs * slope).astype(BF)
            keep = wide < HEAD if h == 0 else wide >= HEAD
            dvacc[keys, :] += dot(probs.astype(BF), jnp.where(keep, go[span, :], zero))
            dkacc[keys, :] += dot(grads, jnp.where(keep, qkv_ref[0, span, :], zero))
            dqt[part, span] = dot(kt[part, keys], grads)

    def step(i, carry):
        attended(pl.ds(pl.multiple_of(i * block, block), block), slice(0, LONGEST))
        return carry

    lax.fori_loop(0, LONGEST // block, step, 0)
    attended(slice(LONGEST, rows), slice(LONGEST, rows))
    cosine, sine = cos_ref[0], sin_ref[0]
    turned = dqt[...].T
    grads_ref[0] = ((turned * cosine - pair_swap(turned) * sine) * (1.0 / math.sqrt(HEAD))).astype(BF)
    turned = dkacc[...]
    grads_ref[1] = ((turned * cosine - pair_swap(turned) * sine) * LN2).astype(BF)
    grads_ref[2] = dvacc[...].astype(BF)


def attend_back(b, idx_col, qkv, seg_col, seg_row, lse, ctxt, gnear, gaway, cosine, sine, block=256):
    rows, share = qkv.shape[1:]
    pairs = share // PAIR
    half = rows // 2
    whole = lambda shape: pl.BlockSpec((1,) + shape, lambda j: (b, 0, 0))
    three = pl.BlockSpec((3, rows, PAIR), lambda j: (0, 0, j))
    given = pl.BlockSpec((half, PAIR), lambda j: (b, j))
    column = lambda n: pl.BlockSpec((n, PAIR), lambda j: (0, j))
    return pl.pallas_call(
        functools.partial(attend_back_body, block),
        grid=(pairs,),
        in_specs=[whole((rows, 1)), three, whole((rows, 1)), whole((1, rows)),
                  pl.BlockSpec((1, 8, rows), lambda j: (j, 0, 0)),
                  pl.BlockSpec((PAIR, rows), lambda j: (j, 0)),
                  given, given, whole((rows, PAIR)), whole((rows, PAIR))],
        out_specs=pl.BlockSpec((3, rows, PAIR), lambda j: (0, 0, j)),
        out_shape=jax.ShapeDtypeStruct((3, rows, share), BF),
        scratch_shapes=[pltpu.VMEM((rows, rows), BF), pltpu.VMEM((rows, 2 * PAIR), BF),
                        pltpu.VMEM((rows, 2 * PAIR), BF), pltpu.VMEM((PAIR, rows), BF),
                        pltpu.VMEM((PAIR, rows), BF), pltpu.VMEM((PAIR, rows), BF),
                        pltpu.VMEM((rows, PAIR), BF), pltpu.VMEM((8, rows), F32),
                        pltpu.VMEM((rows, PAIR), F32), pltpu.VMEM((rows, PAIR), F32),
                        pltpu.VMEM((PAIR, rows), F32), pltpu.VMEM((8, rows), F32)],
        compiler_params=pltpu.CompilerParams(vmem_limit_bytes=60 << 20),
        cost_estimate=pl.CostEstimate(
            flops=pairs * 2 * 2 * rows * rows * 7 * PAIR, bytes_accessed=2 * 9 * rows * share,
            transcendentals=2 * pairs * rows * rows,
        ),
        name="attend_back",
    )(idx_col, qkv, seg_col, seg_row, lse, ctxt, gnear, gaway, cosine, sine)


def project_back_body(block, part_ref, g_ref, row_ref, wnear_ref, waway_ref,
                      near_ref, away_ref, work, hold, sems):
    rows, share = g_ref.shape[1:]
    half = near_ref.shape[0]
    for copy in own_columns(part_ref[0], wnear_ref, waway_ref, hold, sems):
        copy.wait()

    def step(i, carry):
        span = pl.ds(pl.multiple_of(i * block, block), block)
        total = None
        for place in range(3):
            term = dot_rt(g_ref[place, span, :], hold[:, place * share:(place + 1) * share])
            total = term if total is None else total + term
        work[span, :] = total.astype(BF)
        return carry

    lax.fori_loop(0, rows // block, step, 0)
    small = block // 2

    def back(i, carry):
        span = pl.ds(pl.multiple_of(i * small, small), small)
        for base, out_ref in ((half, away_ref), (0, near_ref)):
            pick = (lax.broadcasted_iota(jnp.int32, (small, rows), 0) + (base + i * small) == row_ref[0]).astype(BF)
            out_ref[span, :] = dot(pick, work[...]).astype(BF)
        return carry

    lax.fori_loop(0, half // small, back, 0)


def project_back(b, part, grads, idx_row, near_w, away_w, block=256):
    rows, share = grads.shape[1:]
    width = 2 * share
    half = rows // 2
    smem, anywhere = (pl.BlockSpec(memory_space=s) for s in (pltpu.SMEM, pl.ANY))
    return pl.pallas_call(
        functools.partial(project_back_body, block),
        grid=(1,),
        in_specs=[smem, pl.BlockSpec((3, rows, share), lambda i: (0, 0, 0)),
                  pl.BlockSpec((1, 1, rows), lambda i: (b, 0, 0)), anywhere, anywhere],
        out_specs=[pl.BlockSpec((half, width), lambda i: (0, 0))] * 2,
        scratch_shapes=[pltpu.VMEM((rows, width), BF), pltpu.VMEM((width, 3 * share), BF),
                        pltpu.SemaphoreType.DMA((6,))],
        out_shape=[jax.ShapeDtypeStruct((half, width), BF)] * 2,
        compiler_params=pltpu.CompilerParams(vmem_limit_bytes=40 << 20),
        cost_estimate=pl.CostEstimate(
            flops=2 * rows * width * (rows + 3 * share),
            bytes_accessed=2 * rows * (width + 3 * share) + 6 * width * share,
            transcendentals=0,
        ),
        name="project_back",
    )(part, grads, idx_row, near_w, away_w)


def weight_back_body(batches, *refs):
    xw_ref, g_refs, (gw_ref, gb_ref) = refs[0], refs[1:1 + batches], refs[1 + batches:]
    total, thin = None, None
    for b, g_ref in enumerate(g_refs):
        term = dot_lt(xw_ref[b], g_ref[0])
        line = jnp.sum(g_ref[0].astype(F32), axis=0, keepdims=True)
        total = term if total is None else total + term
        thin = line if thin is None else thin + line
    gw_ref[...] = total.astype(BF)
    gb_ref[...] = jnp.broadcast_to(thin, gb_ref.shape)


def weight_back(xws, grads):
    (batches, rows, width), share = xws.shape, grads[0].shape[2]
    each = pl.BlockSpec((1, rows, share), lambda s: (s, 0, 0))
    return pl.pallas_call(
        functools.partial(weight_back_body, batches),
        grid=(3,),
        in_specs=[pl.BlockSpec(xws.shape, lambda s: (0, 0, 0))] + [each] * batches,
        out_specs=[pl.BlockSpec((width, share), lambda s: (0, s)),
                   pl.BlockSpec((8, share), lambda s: (0, s))],
        out_shape=[jax.ShapeDtypeStruct((width, 3 * share), BF), jax.ShapeDtypeStruct((8, 3 * share), F32)],
        compiler_params=pltpu.CompilerParams(vmem_limit_bytes=60 << 20),
        cost_estimate=pl.CostEstimate(
            flops=2 * batches * rows * width * 3 * share,
            bytes_accessed=2 * batches * rows * (width + 3 * share) + 6 * width * share,
            transcendentals=0,
        ),
        name="weight_back",
    )(xws, *grads)


EPS = 1e-6
ERF_SLOPE = 0.3275911 * math.sqrt(0.5)
ERF_TERMS = (0.254829592, -0.284496736, 1.421413741, -1.453152027, 1.061405429)


def gauss_parts(u):
    bell = jnp.exp2(u * u * (-0.5 * LOG2E))
    t = 1.0 / (1.0 + ERF_SLOPE * jnp.abs(u))
    poly = 0.5 * ERF_TERMS[4]
    for term in ERF_TERMS[3::-1]:
        poly = poly * t + 0.5 * term
    tail = poly * t * bell
    below = jnp.where(u < 0.0, tail, 1.0 - tail)
    return u * below, below + u * bell * (1.0 / math.sqrt(2.0 * math.pi))


def row_mean(value):
    return jnp.sum(value, axis=1, keepdims=True) * (1.0 / value.shape[1])


def standard(hidden):
    centre = hidden - row_mean(hidden)
    root = lax.rsqrt(row_mean(centre * centre) + EPS)
    return centre * root, root


def standard_back(grad, norm, root):
    return root * (grad - row_mean(grad) - norm * row_mean(grad * norm))


def feed_body(chunk, part_ref, x_ref, near_ref, away_ref, dy_ref, thin_ref, bup_ref,
              unear_ref, uaway_ref, dnear_ref, daway_ref,
              out_ref, dh_ref, cnear_ref, caway_ref, sums_ref, bsum_ref,
              dmine_ref, dtheirs_ref, omine_ref, otheirs_ref,
              wo_near, wo_away, wup, wdown, slopes, acts, gup, gdown, go_near, go_away, sems, out_sems):
    core = part_ref[0]
    width, wide = wup.shape
    half_w, half_f = width // 2, wide // 2

    @pl.when(pl.program_id(0) == 0)
    def _():
        copies = []
        for t, (u_ref, d_ref) in enumerate(((unear_ref, dnear_ref), (uaway_ref, daway_ref))):
            side = core if t == 0 else 1 - core
            hold = wo_near if t == 0 else wo_away
            copies += [
                pltpu.make_async_copy(u_ref.at[:, :width], hold, sems.at[t]),
                pltpu.make_async_copy(
                    u_ref.at[:, width:], wup.at[pl.ds(pl.multiple_of(side * half_w, 128), half_w), :],
                    sems.at[2 + t]),
                pltpu.make_async_copy(
                    d_ref, wdown.at[pl.ds(pl.multiple_of(side * half_f, 128), half_f), :], sems.at[4 + t]),
            ]
        for copy in copies:
            copy.start()
        for ref in (sums_ref, bsum_ref, gup, gdown, go_near, go_away):
            ref[...] = jnp.zeros_like(ref)
        for copy in copies:
            copy.wait()

    b_out, gain_one, shift_one, b_down, gain_two, shift_two = (thin_ref[i:i + 1, :] for i in range(6))

    def tally(row, value):
        sums_ref[row:row + 1, :] += jnp.sum(value, axis=0, keepdims=True)

    attended = dot(near_ref[...], wo_near[...]) + dot(away_ref[...], wo_away[...]) + b_out
    norm_one, root_one = standard(x_ref[...].astype(F32) + attended)
    first = norm_one * gain_one + shift_one
    low = first.astype(BF)
    lowered = None
    for c in range(wide // chunk):
        cols = slice(c * chunk, (c + 1) * chunk)
        act, slope = gauss_parts(dot(low, wup[:, cols]) + bup_ref[:, cols])
        act = act.astype(BF)
        acts[:, cols] = act
        slopes[:, cols] = slope.astype(BF)
        term = dot(act, wdown[cols, :])
        lowered = term if lowered is None else lowered + term
    norm_two, root_two = standard(first + lowered + b_down)
    out_ref[...] = (norm_two * gain_two + shift_two).astype(BF)
    dy = dy_ref[...].astype(F32)
    tally(4, dy * norm_two)
    tally(5, dy)
    grad_two = standard_back(dy * gain_two, norm_two, root_two)
    dlow = grad_two.astype(BF)
    tally(3, dlow.astype(F32))
    total = grad_two
    low_t, dlow_t = low.T, dlow.T
    for c in range(wide // chunk):
        cols = slice(c * chunk, (c + 1) * chunk)
        dup = (dot_rt(dlow, wdown[cols, :]) * slopes[:, cols].astype(F32)).astype(BF)
        gdown[:, cols] += dot(dlow_t, acts[:, cols])
        gup[:, cols] += dot(low_t, dup)
        bsum_ref[0:1, cols] += jnp.sum(dup.astype(F32), axis=0, keepdims=True)
        total = total + dot_rt(dup, wup[:, cols])
    tally(1, total * norm_one)
    tally(2, total)
    grad_one = standard_back(total * gain_one, norm_one, root_one)
    dh_ref[...] = grad_one
    da = grad_one.astype(BF)
    tally(0, da.astype(F32))
    go_near[...] += dot(near_ref[...].T, da)
    go_away[...] += dot(away_ref[...].T, da)
    cnear_ref[...] = dot_rt(da, wo_near[...]).astype(BF)
    caway_ref[...] = dot_rt(da, wo_away[...]).astype(BF)

    @pl.when(pl.program_id(0) == pl.num_programs(0) - 1)
    def _():
        rows_d = [pl.ds(pl.multiple_of(side * half_f, 128), half_f) for side in (core, 1 - core)]
        rows_u = [pl.ds(pl.multiple_of(side * half_w, 128), half_w) for side in (core, 1 - core)]
        copies = []
        for t, (d_ref, o_ref, hold) in enumerate(((dmine_ref, omine_ref, wo_near), (dtheirs_ref, otheirs_ref, wo_away))):
            copies += [
                pltpu.make_async_copy(wdown.at[rows_d[t], :], d_ref, out_sems.at[3 * t]),
                pltpu.make_async_copy(wup.at[rows_u[t], :], o_ref.at[:, :wide], out_sems.at[3 * t + 1]),
                pltpu.make_async_copy(hold, o_ref.at[:, wide:], out_sems.at[3 * t + 2]),
            ]
        for c in range(wide // width):
            cols = slice(c * width, (c + 1) * width)
            wdown[cols, :] = gdown[:, cols].T.astype(BF)
        copies[0].start()
        copies[3].start()
        for c in range(wide // width):
            cols = slice(c * width, (c + 1) * width)
            wup[:, cols] = gup[:, cols].astype(BF)
        wo_near[...] = go_near[...].astype(BF)
        wo_away[...] = go_away[...].astype(BF)
        for k in (1, 2, 4, 5):
            copies[k].start()
        for copy in copies:
            copy.wait()


def feed(part, x, near, away, dy, thin, bup, unear, uaway, dnear, daway, block=256, chunk=768):
    rows, width = x.shape
    share = near.shape[1]
    wide = bup.shape[1]
    line = lambda n: pl.BlockSpec((block, n), lambda i: (i, 0))
    fixed = lambda shape: pl.BlockSpec(shape, lambda i: (0, 0))
    anywhere = pl.BlockSpec(memory_space=pl.ANY)
    shape = lambda n, dt: jax.ShapeDtypeStruct((rows, n), dt)
    half = lambda n, m: jax.ShapeDtypeStruct((n // 2, m), BF)
    return pl.pallas_call(
        functools.partial(feed_body, chunk),
        grid=(rows // block,),
        in_specs=[pl.BlockSpec(memory_space=pltpu.SMEM), line(width), line(share), line(share), line(width),
                  fixed(thin.shape), fixed(bup.shape), anywhere, anywhere, anywhere, anywhere],
        out_specs=[line(width), line(width), line(share), line(share), fixed((8, width)), fixed((8, wide))]
        + [anywhere] * 4,
        out_shape=[shape(width, BF), shape(width, F32), shape(share, BF), shape(share, BF),
                   jax.ShapeDtypeStruct((8, width), F32), jax.ShapeDtypeStruct((8, wide), F32),
                   half(wide, width), half(wide, width), half(width, wide + width), half(width, wide + width)],
        scratch_shapes=[pltpu.VMEM((share, width), BF), pltpu.VMEM((share, width), BF),
                        pltpu.VMEM((width, wide), BF), pltpu.VMEM((wide, width), BF),
                        pltpu.VMEM((block, wide), BF), pltpu.VMEM((block, wide), BF),
                        pltpu.VMEM((width, wide), F32), pltpu.VMEM((width, wide), F32),
                        pltpu.VMEM((share, width), F32), pltpu.VMEM((share, width), F32),
                        pltpu.SemaphoreType.DMA((6,)), pltpu.SemaphoreType.DMA((6,))],
        compiler_params=pltpu.CompilerParams(vmem_limit_bytes=60 << 20),
        cost_estimate=pl.CostEstimate(
            flops=2 * rows * width * (3 * width + 6 * wide),
            bytes_accessed=2 * rows * 7 * width + 8 * width * (wide + width),
            transcendentals=2 * rows * wide,
        ),
        name="feed",
    )(part, x, near, away, dy, thin, bup, unear, uaway, dnear, daway)


def swap_cores(value):
    return lax.ppermute(value, "seq", [(0, 1), (1, 0)])


def swap_x(value):
    return lax.ppermute(value, "fsdp", [(i, i ^ 1) for i in range(16)])


def swap_y(value):
    return lax.ppermute(value, "fsdp", [(i, i ^ 2) for i in range(16)])


def flip_z(value, k):
    return lax.ppermute(value, "fsdp", [(i, i ^ (4 * k)) for i in range(16)])


def shift_z(value, k):
    return lax.ppermute(value, "fsdp", [(i, (i + 4 * k) % 16) for i in range(16)])


def assemble_body(lines, place_ref, ax_ref, ay_ref, bx_ref, by_ref, *out_refs):
    place = place_ref[0]
    z, y, x = place // 4, (place // 2) % 2, place % 2
    n = ax_ref.shape[1]

    def put(owner, piece):
        out_refs[0][owner] = piece[:, :out_refs[0].shape[2]]
        for c in range(lines):
            width = out_refs[1].shape[2]
            at = out_refs[0].shape[2] + c * width
            out_refs[1][owner, c * n:(c + 1) * n, :] = piece[:, at:at + width]

    for j in range(4):
        k, o = j % 2, j // 2
        near_z, far_z = lax.rem(z - k + 4, 4), lax.rem(z - k + 2, 4)
        flip_x = lax.rem(x + o, 2)
        flip_y = lax.rem(y + o, 2)
        put(near_z * 4 + y * 2 + flip_x, ax_ref[j])
        put(near_z * 4 + (1 - y) * 2 + flip_x, ay_ref[j])
        put(far_z * 4 + flip_y * 2 + x, by_ref[j])
        put(far_z * 4 + flip_y * 2 + 1 - x, bx_ref[j])


def assemble(place, parts, lines=0, line=0):
    n, width = parts[0].shape[1:]
    vmem = pl.BlockSpec(memory_space=pltpu.VMEM)
    shapes = [(16, n, width - lines * line)] + ([(16, lines * n, line)] if lines else [])
    return pl.pallas_call(
        functools.partial(assemble_body, lines),
        in_specs=[pl.BlockSpec(memory_space=pltpu.SMEM)] + [vmem] * 4,
        out_shape=[jax.ShapeDtypeStruct(shape, BF) for shape in shapes],
        compiler_params=pltpu.CompilerParams(vmem_limit_bytes=40 << 20),
        cost_estimate=pl.CostEstimate(flops=0, bytes_accessed=4 * 16 * n * width, transcendentals=0),
        name="assemble",
    )(place, *parts)


def tie(values, after=()):
    return lax.optimization_barrier((values, after))[0]


def reach_z(shard):
    first = jnp.stack([shard, shift_z(shard, 1)])
    second = jnp.stack([shift_z(shard, 2), shift_z(shard, 3)])
    return first, second


def reach_one(first, second):
    return jnp.concatenate([first, swap_x(first)], axis=0), jnp.concatenate([second, swap_y(second)], axis=0)


def reach_two(first, second):
    return first, swap_y(first), swap_x(second), second


def joined(parts, lines=0, line=0):
    place = jnp.full((1,), lax.axis_index("fsdp"), jnp.int32)
    return [value.reshape(-1, value.shape[2]) for value in assemble(place, parts, lines, line)]


def pick(part, at, axis):
    return lax.dynamic_index_in_dim(part, at, axis, keepdims=False)


def corner():
    place = lax.axis_index("fsdp")
    return place // 4, (place // 2) % 2, place % 2


def fold_one(value):
    z, y, x = corner()
    rows, width = value.shape
    cube = value.reshape(2, 2, 2, 2, rows // 16, width)
    return (value,), (pick(cube[0], 1 - y, 1).astype(BF), pick(cube[1], 1 - x, 2).astype(BF))


def fold_two(stay, sends, after=()):
    z, y, x = corner()
    rows, width = stay[0].shape
    cube = stay[0].reshape(2, 2, 2, 2, rows // 16, width)
    came = tie((swap_y(sends[0]), swap_x(sends[1])), after)
    first = pick(cube[0], y, 1).astype(F32) + came[0].astype(F32)
    second = pick(cube[1], x, 2).astype(F32) + came[1].astype(F32)
    return (first, second), (pick(first, 1 - x, 1).astype(BF), pick(second, 1 - y, 1).astype(BF))


def fold_cross(stay, sends, after=()):
    z, y, x = corner()
    came = tie((swap_x(sends[0]), swap_y(sends[1])), after)
    first = pick(stay[0], x, 1) + came[0].astype(F32)
    second = pick(stay[1], y, 1) + came[1].astype(F32)
    return jnp.concatenate([first, second], axis=0)


def fold_three(stack):
    near = corner()[0] % 2
    cube = stack.reshape((2, 2) + stack.shape[1:])
    return (cube,), (pick(cube, 1 - near, 1).astype(BF),)


def fold_four(stay, sends, after=()):
    z = corner()[0]
    near, far = z % 2, z // 2
    came = tie(flip_z(sends[0], 1), after)
    total = pick(stay[0], near, 1) + came.astype(F32)
    return (pick(total, far, 0),), (pick(total, 1 - far, 0).astype(BF),)


def fold_end(stay, sends, after=()):
    return stay[0] + tie(flip_z(sends[0], 2), after).astype(F32)


def on_device(tokens, permutation, segment_ids, cotangent, *shards):
    batches = tokens.shape[0]
    half, width = tokens.shape[2], tokens.shape[3]
    core = lax.axis_index("seq")
    share = width // 2
    owners = 2 * lax.axis_size("fsdp")
    staged = owners == 32
    part = jnp.full((1,), core, jnp.int32)
    thin = [i for i, piece in enumerate(shards) if piece.ndim == 1]
    sizes = [shards[i].shape[0] for i in thin]
    count = sum(sizes)
    n_qkv = shards[0].shape[0]
    room = n_qkv * 128
    tokens, cotangent = tokens[:, 0], cotangent[:, 0]

    away_tokens = swap_cores(tokens)
    idx_col, idx_row, seg_col, seg_row, cosine, sine = ready(part, permutation[:, 0], segment_ids[:, 0])
    if staged:
        q_shard, ud_shard = pack(shards[0], shards[2], shards[6], shards[8], [shards[i] for i in thin])
        first, second = reach_z(q_shard)
        first, second, idx_col = tie((first, second, idx_col))
        first_x, second_y = swap_x(first), swap_y(second)
        ud_shard = tie(ud_shard, first_x)
        q_parts = reach_two(jnp.concatenate([first, first_x], axis=0), jnp.concatenate([second, second_y], axis=0))
        ud_z = tuple(shift_z(ud_shard, k) for k in (1, 2, 3))
        xws = arrange(idx_col, tokens, away_tokens)
        q_parts = tie(q_parts, xws)
        (q_near,) = joined(q_parts)
    else:
        xws = arrange(idx_col, tokens, away_tokens)
        packed = jnp.concatenate([shards[i] for i in thin] + [jnp.zeros((room - count,), BF)])
        q_shard = jnp.concatenate([shards[0], packed.reshape(n_qkv, 128)], axis=1)
        q_near = lax.all_gather(q_shard, "fsdp", axis=0, tiled=True)
        u_near = lax.all_gather(jnp.concatenate([shards[2], shards[6]], axis=1), "fsdp", axis=0, tiled=True)
        d_near = lax.all_gather(shards[8], "fsdp", axis=0, tiled=True)
    q_away = swap_cores(q_near)

    slabs = [value[:, 3 * width:].reshape(owners // 2, n_qkv, 128) for value in (q_near, q_away)]
    vectors = jnp.concatenate(
        [jnp.where(core == 0, slabs[0], slabs[1]), jnp.where(core == 0, slabs[1], slabs[0])], axis=0
    ).astype(F32)
    spread, at = [], 0
    for i, size in enumerate(sizes):
        if staged:
            spread.append(vectors[:, i, :size].reshape(1, owners * size))
        else:
            spread.append(vectors.reshape(owners, room)[:, at:at + size].reshape(1, owners * size))
        at += size
    b_qkv, b_out, gain_one, shift_one, b_up, b_down, gain_two, shift_two = spread
    bias_own = jnp.concatenate(
        [lax.dynamic_slice_in_dim(b_qkv, core * share + s * width, share, 1) for s in range(3)], axis=1
    )
    blank_row = jnp.zeros((1, width), F32)
    thin_rows = jnp.concatenate(
        [b_out, gain_one, shift_one, b_down, gain_two, shift_two, blank_row, blank_row], axis=0
    )

    qkvs = [project(b, part, xws, q_near, q_away, bias_own, cosine, sine) for b in range(batches)]
    if staged:
        (one, two, three), qkvs = tie((ud_z, qkvs))
        first, second = jnp.stack([ud_shard, one]), jnp.stack([two, three])
        qkvs[0], first, second = tie((qkvs[0], first, second))
        first_x, second_y = swap_x(first), swap_y(second)
    kept, ctxs = [], []
    for b in range(batches):
        if staged and b == 1:
            first_x, second_y = tie((first_x, second_y), ctxs[0][0])
            first, second = jnp.concatenate([first, first_x], axis=0), jnp.concatenate([second, second_y], axis=0)
            qkvs[1], first, second = tie((qkvs[1], first, second))
            first_y, second_x = swap_y(first), swap_x(second)
        near, away, ctxt, lse = attend(b, idx_col, qkvs[b], seg_col, seg_row)
        kept.append((qkvs[b], ctxt, lse))
        ctxs.append((near, swap_cores(away)))
    if staged:
        first_y, second_x = tie((first_y, second_x), ctxs[1][0])
        u_near, d_near = joined((first, first_y, second_x, second), 4, width)
    u_away, d_away = swap_cores(u_near), swap_cores(d_near)
    near, away = (jnp.concatenate([item[i] for item in ctxs], axis=0) for i in range(2))
    (outputs, grad_one, cnear, caway, sums, bsum, d_mine, d_theirs, uo_mine, uo_theirs) = feed(
        part, tokens.reshape(batches * half, width), near, away,
        cotangent.reshape(batches * half, width), thin_rows, b_up, u_near, u_away, d_near, d_away,
    )
    caway = swap_cores(caway)
    d_theirs, uo_theirs = swap_cores(d_theirs), swap_cores(uo_theirs)
    plus = lambda mine, theirs: (mine.astype(F32) + theirs.astype(F32)).astype(BF)

    def back(b, given):
        qkv, ctxt, lse = kept[b]
        return attend_back(b, idx_col, qkv, seg_col, seg_row, lse, ctxt, *given, cosine, sine)

    givens = [(cnear, caway)] * batches
    if staged:
        first_back = back(0, givens[0])
        d_theirs, uo_theirs = tie((d_theirs, uo_theirs), first_back)
        d_step, uo_step = fold_one(plus(d_mine, d_theirs)), fold_one(plus(uo_mine, uo_theirs))
        given, d_step, uo_step = tie((givens[1], d_step, uo_step))
        grads = [first_back, back(1, given)]
        d_step, uo_step = fold_two(*d_step, grads[1]), fold_two(*uo_step, grads[1])
        grads, d_step, uo_step = tie((grads, d_step, uo_step))
    else:
        grads = [back(b, givens[b]) for b in range(batches)]
        d_sum, uo_sum = plus(d_mine, d_theirs), plus(uo_mine, uo_theirs)
    gw_own, gb_own = weight_back(xws, grads)

    def halves(value):
        size = value.shape[0] // 2
        return (lax.dynamic_slice_in_dim(value, core * size, size, 0),
                lax.dynamic_slice_in_dim(value, (1 - core) * size, size, 0))

    blank = jnp.zeros((share,), F32)
    thin_columns = []
    for s in range(3):
        span = slice(s * share, (s + 1) * share)
        thin_columns += [jnp.where(core == 0, gb_own[0, span], blank),
                         jnp.where(core == 0, blank, gb_own[0, span])]
    six = sums[:6].reshape(6, owners, -1).transpose(1, 0, 2).reshape(owners, -1)
    slab = jnp.concatenate(
        [jnp.concatenate(thin_columns).reshape(owners, -1), bsum[0].reshape(owners, -1), six,
         jnp.zeros((owners, room - count), F32)], axis=1
    ).astype(BF).reshape(owners * n_qkv, 128)
    mine, theirs = (jnp.concatenate(pair, axis=1) for pair in zip(halves(gw_own), halves(slab)))
    theirs = swap_cores(theirs)
    q_sum = jnp.concatenate([
        mine[:, :3 * share], theirs[:, :3 * share],
        (mine[:, 3 * share:].astype(F32) + theirs[:, 3 * share:].astype(F32)).astype(BF),
    ], axis=1)
    backs = [project_back(0, part, grads[0], idx_row, q_near, q_away)]
    if staged:
        wide, lines = fold_cross(*uo_step, backs[0]), fold_cross(*d_step, backs[0])
        lines = [lines[:, i * n_qkv:(i + 1) * n_qkv] for i in range(4)]
        du_step = fold_three(jnp.concatenate([wide] + lines, axis=2))
        last, q_step, du_step = tie((grads[1], fold_one(q_sum), du_step), backs)
        backs.append(project_back(1, part, last, idx_row, q_near, q_away))
        q_step = tie(fold_two(*q_step, backs[1]))
        du_step = tie(fold_four(*du_step, q_step))
        q_step = tie(fold_three(fold_cross(*q_step, du_step)))
        q_step = fold_four(*q_step)
        g_uo = fold_end(*du_step, q_step)
        g_down = jnp.concatenate([g_uo[:, (5 + i) * width:(6 + i) * width] for i in range(4)], axis=0)
    else:
        backs.append(project_back(1, part, grads[1], idx_row, q_near, q_away))
        summed = lambda value: lax.psum_scatter(
            value.astype(BF), "fsdp", scatter_dimension=0, tiled=True
        ).astype(F32)
        g_qkv, g_down, g_uo = summed(q_sum), summed(d_sum), summed(uo_sum)
    grad_one = grad_one.reshape(batches, half, width)
    token_grad = jnp.stack([
        (grad_one[b] + backs[b][0].astype(F32) + swap_cores(backs[b][1]).astype(F32)).astype(BF)
        for b in range(batches)
    ])
    if staged:
        g_qkv = fold_end(*q_step, (g_uo, token_grad))
    own, other = g_qkv[:, :3 * share], g_qkv[:, 3 * share:6 * share]
    columns = []
    for s in range(3):
        span = slice(s * share, (s + 1) * share)
        columns += [jnp.where(core == 0, own[:, span], other[:, span]),
                    jnp.where(core == 0, other[:, span], own[:, span])]
    g_out, g_up = g_uo[:, 4 * width:5 * width], g_uo[:, :4 * width]
    flat = g_qkv[:, 3 * width:].reshape(room)
    thin_out, at = [], 0
    for size in [sizes[0], sizes[4]] + [n_qkv] * 6:
        thin_out.append(flat[at:at + size])
        at += size
    g_bqkv, g_bup, g_bout, g_g1, g_s1, g_bdown, g_g2, g_s2 = thin_out
    return (
        outputs.reshape(batches, 1, half, width), token_grad[:, None],
        jnp.concatenate(columns, axis=1), g_bqkv, g_out, g_bout, g_g1, g_s1, g_up, g_bup, g_down, g_bdown, g_g2, g_s2,
    )


def solution(mesh):
    packs = P(None, "fsdp", "seq", None)
    ids = P(None, "fsdp", None)
    deep, flat = P(("seq", "fsdp"), None), P(("seq", "fsdp"))
    layers = (deep, flat, deep, flat, flat, flat, deep, flat, deep, flat, flat, flat)
    return jax.shard_map(
        on_device, mesh=mesh, in_specs=(packs, ids, ids, packs) + layers,
        out_specs=(packs, packs) + layers, check_vma=False,
    )
```

```python
import functools
import math

import jax
import jax.numpy as jnp
from jax import lax
from jax.experimental import pallas as pl
from jax.experimental.pallas import tpu as pltpu
from jax.sharding import PartitionSpec as P

HEAD = 64
PAIR = 2 * HEAD
SEG_COUNT = 4
LONGEST = 1024
LOG2E = math.log2(math.e)
LN2 = math.log(2.0)
FAR = float(2**30)
BF = jnp.bfloat16
F32 = jnp.float32


def dot(left, right):
    return jnp.dot(left, right, preferred_element_type=F32)


def dot_rt(left, right):
    return lax.dot_general(left, right, (((1,), (1,)), ((), ())), preferred_element_type=F32)


def dot_lt(left, right):
    return lax.dot_general(left, right, (((0,), (0,)), ((), ())), preferred_element_type=F32)


def pair_swap(values):
    lanes = lax.broadcasted_iota(jnp.int32, values.shape, 1)
    width = values.shape[1]
    return jnp.where(
        lanes % 2 == 0, pltpu.roll(values, width - 1, 1), pltpu.roll(values, 1, 1)
    )


def ready_body(part_ref, order_ref, seg_ref, freq_ref, idx_col, idx_row, seg_col, seg_row, cos_ref, sin_ref):
    core = part_ref[0]
    batches, rows = order_ref.shape
    half = rows // 2
    lanes = lax.broadcasted_iota(jnp.int32, (1, rows), 1)
    wide = lax.broadcasted_iota(jnp.int32, (8, rows), 1)
    halves = freq_ref.shape[0]
    cols = lax.broadcasted_iota(jnp.int32, (halves, PAIR), 1)
    lines = lax.broadcasted_iota(jnp.int32, (halves, PAIR), 0)
    grow = ((cols % HEAD) // 2 == lines).astype(F32)
    turn = jnp.where(cols % 2 == 0, -grow, grow)
    expand = lambda value, by: lax.dot_general(
        value, by, (((0,), (0,)), ((), ())), preferred_element_type=F32, precision=lax.Precision.HIGHEST)
    for b in range(batches):
        order, seg = order_ref[b:b + 1, :], seg_ref[b:b + 1, :]
        starts, start, total = [], 0, 0
        for s in range(SEG_COUNT):
            size = jnp.sum((seg == s).astype(F32)).astype(jnp.int32)
            starts.append(total)
            start = start + jnp.where(size == LONGEST, total, 0)
            total = total + size
        table = jnp.concatenate([order, seg, lanes, jnp.zeros((5, rows), jnp.int32)], axis=0)
        main = pltpu.roll(table, rows - start, 1)
        early = pltpu.roll(table, LONGEST, 1)
        table = jnp.where(wide < LONGEST, main, jnp.where(wide - LONGEST < start, early, table))
        order, seg, place = table[0:1], table[1:2], table[2:3]
        origin = jnp.zeros_like(seg)
        for s in range(1, SEG_COUNT):
            origin = jnp.where(seg == s, starts[s], origin)
        position = (place - origin).astype(F32)
        near = (order >= half).astype(jnp.int32) == core
        idx = jnp.where(near, order - core * half, order + core * half)
        idx_row[b] = idx
        seg_row[b] = seg
        both = jnp.concatenate([idx.astype(F32), seg.astype(F32), jnp.zeros((6, rows), F32)], axis=0).T
        idx_col[b] = both[:, 0:1].astype(jnp.int32)
        seg_col[b] = both[:, 1:2].astype(jnp.int32)
        phase = freq_ref[...] * position
        cos_ref[b] = expand(jnp.cos(phase), grow)
        sin_ref[b] = expand(jnp.sin(phase), turn)


def ready(part, order, segments):
    batches, rows = order.shape
    halves = HEAD // 2
    freqs = jnp.exp(jnp.arange(halves, dtype=F32) * (-2.0 * math.log(10000.0) / HEAD))[:, None]
    vmem, smem = (pl.BlockSpec(memory_space=s) for s in (pltpu.VMEM, pltpu.SMEM))
    ints = lambda *shape: jax.ShapeDtypeStruct(shape, jnp.int32)
    return pl.pallas_call(
        ready_body,
        in_specs=[smem, vmem, vmem, vmem],
        out_shape=[ints(batches, rows, 1), ints(batches, 1, rows), ints(batches, rows, 1), ints(batches, 1, rows),
                   jax.ShapeDtypeStruct((batches, rows, PAIR), F32), jax.ShapeDtypeStruct((batches, rows, PAIR), F32)],
        compiler_params=pltpu.CompilerParams(vmem_limit_bytes=40 << 20),
        cost_estimate=pl.CostEstimate(
            flops=1 << 30, bytes_accessed=8 * batches * rows * 3 * PAIR, transcendentals=2 * batches * rows * halves
        ),
        name="ready",
    )(part, order, segments, freqs)


def pack_body(thin, w_qkv, w_out, w_up, w_down, *refs):
    q_ref, ud_ref = refs[thin:]
    n, width = w_out.shape
    wide = w_qkv.shape[1]
    q_ref[:, :wide] = w_qkv[...]
    q_ref[:, wide:] = jnp.zeros((n, q_ref.shape[1] - wide), BF)
    for i, ref in enumerate(refs[:thin]):
        q_ref[i:i + 1, wide:wide + ref.shape[1]] = ref[...]
    ud_ref[:, :width] = w_out[...]
    ud_ref[:, width:width + w_up.shape[1]] = w_up[...]
    at = width + w_up.shape[1]
    for c in range(w_down.shape[0] // n):
        ud_ref[:, at + c * width:at + (c + 1) * width] = w_down[c * n:(c + 1) * n, :]


def pack(w_qkv, w_out, w_up, w_down, thin):
    n, width = w_out.shape
    wide = width + w_up.shape[1] + w_down.shape[0] // n * width
    return pl.pallas_call(
        functools.partial(pack_body, len(thin)),
        out_shape=[jax.ShapeDtypeStruct((n, w_qkv.shape[1] + 128), BF), jax.ShapeDtypeStruct((n, wide), BF)],
        cost_estimate=pl.CostEstimate(flops=0, bytes_accessed=4 * n * (w_qkv.shape[1] + wide), transcendentals=0),
        name="pack",
    )(w_qkv, w_out, w_up, w_down, *[value[None] for value in thin])


def arrange_body(block, idx_ref, own_ref, other_ref, xw_ref):
    half = own_ref.shape[1]

    def step(i, carry):
        rows = pl.ds(pl.multiple_of(i * block, block), block)
        picks = lax.broadcasted_iota(jnp.int32, (block, half), 1)
        source = idx_ref[0, rows, :]
        near = (picks == source).astype(BF)
        away = (picks + half == source).astype(BF)
        xw_ref[0, rows, :] = (dot(near, own_ref[0]) + dot(away, other_ref[0])).astype(BF)
        return carry

    lax.fori_loop(0, idx_ref.shape[1] // block, step, 0)


def arrange(idx_col, own, other, block=256):
    batches, rows = idx_col.shape[:2]
    half, width = own.shape[1:]
    each = lambda *shape: pl.BlockSpec((1,) + shape, lambda b: (b, 0, 0))
    return pl.pallas_call(
        functools.partial(arrange_body, block),
        grid=(batches,),
        in_specs=[each(rows, 1), each(half, width), each(half, width)],
        out_specs=each(rows, width),
        out_shape=jax.ShapeDtypeStruct((batches, rows, width), BF),
        compiler_params=pltpu.CompilerParams(vmem_limit_bytes=40 << 20),
        cost_estimate=pl.CostEstimate(
            flops=2 * batches * rows * rows * width, bytes_accessed=4 * batches * rows * width, transcendentals=0
        ),
        name="arrange",
    )(idx_col, own, other)


def own_columns(core, near_ref, away_ref, hold, sems):
    span, share = near_ref.shape[0], hold.shape[1] // 3
    copies = []
    for s in range(3):
        for t, ref in enumerate((near_ref, away_ref)):
            side = core if t == 0 else 1 - core
            copies.append(
                pltpu.make_async_copy(
                    ref.at[:, pl.ds(pl.multiple_of(core * share + 2 * s * share, 128), share)],
                    hold.at[pl.ds(pl.multiple_of(side * span, 128), span), s * share:(s + 1) * share],
                    sems.at[2 * s + t],
                )
            )
    for copy in copies:
        copy.start()
    return copies


def project_body(block, part_ref, xw_ref, near_ref, away_ref, bias_ref, cos_ref, sin_ref,
                 qkv_ref, hold, sems):
    share = qkv_ref.shape[2]
    for copy in own_columns(part_ref[0], near_ref, away_ref, hold, sems):
        copy.wait()

    def step(i, carry):
        rows = pl.ds(pl.multiple_of(i * block, block), block)
        work = xw_ref[0, rows, :]
        cosine, sine = cos_ref[0, rows, :], sin_ref[0, rows, :]
        for place, scale in ((0, LOG2E / math.sqrt(HEAD)), (1, 1.0)):
            whole = slice(place * share, (place + 1) * share)
            pre = dot(work, hold[:, whole]) + bias_ref[:, whole]
            for j in range(share // PAIR):
                cols = slice(j * PAIR, (j + 1) * PAIR)
                piece = pre[:, cols]
                qkv_ref[place, rows, cols] = (
                    (piece * cosine + pair_swap(piece) * sine) * scale
                ).astype(BF)
        qkv_ref[2, rows, :] = (dot(work, hold[:, 2 * share:]) + bias_ref[:, 2 * share:]).astype(BF)
        return carry

    lax.fori_loop(0, xw_ref.shape[1] // block, step, 0)


def project(b, part, xws, near_w, away_w, bias_own, cosine, sine, block=256):
    rows, width = xws.shape[1:]
    share = bias_own.shape[1] // 3
    each = lambda n: pl.BlockSpec((1, rows, n), lambda i: (b, 0, 0))
    vmem, smem, anywhere = (pl.BlockSpec(memory_space=s) for s in (pltpu.VMEM, pltpu.SMEM, pl.ANY))
    return pl.pallas_call(
        functools.partial(project_body, block),
        grid=(1,),
        in_specs=[smem, each(width), anywhere, anywhere, vmem, each(PAIR), each(PAIR)],
        out_specs=pl.BlockSpec((3, rows, share), lambda i: (0, 0, 0)),
        out_shape=jax.ShapeDtypeStruct((3, rows, share), BF),
        scratch_shapes=[pltpu.VMEM((width, 3 * share), BF), pltpu.SemaphoreType.DMA((6,))],
        compiler_params=pltpu.CompilerParams(vmem_limit_bytes=40 << 20),
        cost_estimate=pl.CostEstimate(
            flops=2 * rows * width * 3 * share,
            bytes_accessed=2 * (rows * width + 3 * width * share + 3 * rows * share),
            transcendentals=0,
        ),
        name="project",
    )(part, xws, near_w, away_w, bias_own, cosine, sine)


def attend_body(block, idx_ref, qkv_ref, seg_col_ref, seg_row_ref,
                near_ref, away_ref, ctxt_ref, lse_ref, pick, ka, vt, qt, augt):
    rows = qkv_ref.shape[1]
    half = near_ref.shape[0]

    @pl.when(pl.program_id(0) == 0)
    def _():
        def fill(i, carry):
            span = pl.ds(pl.multiple_of(i * block, block), block)
            pick[span, :] = (
                lax.broadcasted_iota(jnp.int32, (block, rows), 1) == idx_ref[0, span, :]
            ).astype(BF)
            return carry

        lax.fori_loop(0, rows // block, fill, 0)
        lanes = lax.broadcasted_iota(jnp.int32, (rows, PAIR), 1)
        ka[:, PAIR:] = ((lanes == seg_col_ref[0]) | (lanes >= SEG_COUNT)).astype(BF)
        places = lax.broadcasted_iota(jnp.int32, (PAIR, rows), 0)
        augt[...] = jnp.where(
            (places < SEG_COUNT) & (places != seg_row_ref[0]), -FAR, 0.0
        ).astype(BF)

    ka[:, :PAIR] = qkv_ref[1]
    vt[...] = qkv_ref[2].T
    qt[...] = qkv_ref[0].T
    empty = jnp.zeros((HEAD, block), BF)

    def attended(span, keys):
        extra = augt[:, span]
        for h in range(2):
            mine = qt[h * HEAD:(h + 1) * HEAD, span]
            mixed = jnp.concatenate([mine, empty, extra] if h == 0 else [empty, mine, extra], axis=0)
            scores = dot(ka[keys, :], mixed)
            top = jnp.max(scores, axis=0, keepdims=True)
            expo = jnp.exp2(scores - top)
            total = jnp.sum(expo, axis=0, keepdims=True)
            context = dot(vt[h * HEAD:(h + 1) * HEAD, keys], expo.astype(BF))
            ctxt_ref[h * HEAD:(h + 1) * HEAD, span] = (context / total).astype(BF)
            lse_ref[0, h:h + 1, span] = top + jnp.log2(total)

    def step(i, carry):
        attended(pl.ds(pl.multiple_of(i * block, block), block), slice(0, LONGEST))
        return carry

    lax.fori_loop(0, LONGEST // block, step, 0)
    attended(slice(LONGEST, rows), slice(LONGEST, rows))
    given = dot(ctxt_ref[...], pick[...]).astype(BF)
    near_ref[...] = given[:, :half].T
    away_ref[...] = given[:, half:].T


def attend(b, idx_col, qkv, seg_col, seg_row, block=256):
    rows, share = qkv.shape[1:]
    pairs = share // PAIR
    half = rows // 2
    whole = lambda shape: pl.BlockSpec((1,) + shape, lambda j: (b, 0, 0))
    three = pl.BlockSpec((3, rows, PAIR), lambda j: (0, 0, j))
    column = lambda n: pl.BlockSpec((n, PAIR), lambda j: (0, j))
    return pl.pallas_call(
        functools.partial(attend_body, block),
        grid=(pairs,),
        in_specs=[whole((rows, 1)), three, whole((rows, 1)), whole((1, rows))],
        out_specs=[column(half), column(half), pl.BlockSpec((PAIR, rows), lambda j: (j, 0)),
                   pl.BlockSpec((1, 8, rows), lambda j: (j, 0, 0))],
        out_shape=[jax.ShapeDtypeStruct((half, share), BF), jax.ShapeDtypeStruct((half, share), BF),
                   jax.ShapeDtypeStruct((share, rows), BF),
                   jax.ShapeDtypeStruct((pairs, 8, rows), F32)],
        scratch_shapes=[pltpu.VMEM((rows, rows), BF), pltpu.VMEM((rows, 2 * PAIR), BF),
                        pltpu.VMEM((PAIR, rows), BF), pltpu.VMEM((PAIR, rows), BF),
                        pltpu.VMEM((PAIR, rows), BF)],
        compiler_params=pltpu.CompilerParams(vmem_limit_bytes=60 << 20),
        cost_estimate=pl.CostEstimate(
            flops=pairs * 2 * 2 * rows * rows * 3 * PAIR, bytes_accessed=2 * 6 * rows * share,
            transcendentals=2 * pairs * rows * rows,
        ),
        name="attend",
    )(idx_col, qkv, seg_col, seg_row)


def attend_back_body(block, idx_ref, qkv_ref, seg_col_ref, seg_row_ref, lse_ref,
                     ctxt_ref, gnear_ref, gaway_ref, cos_ref, sin_ref,
                     grads_ref,
                     pick, ka, va, kt, qt, dt, go, delta, dkacc, dvacc, dqt, augt):
    rows = qkv_ref.shape[1]
    half = gnear_ref.shape[0]

    @pl.when(pl.program_id(0) == 0)
    def _():
        def fill(i, carry):
            span = pl.ds(pl.multiple_of(i * block, block), block)
            pick[span, :] = (
                lax.broadcasted_iota(jnp.int32, (block, rows), 1) == idx_ref[0, span, :]
            ).astype(BF)
            return carry

        lax.fori_loop(0, rows // block, fill, 0)
        lanes = lax.broadcasted_iota(jnp.int32, (rows, PAIR), 1)
        ones = ((lanes == seg_col_ref[0]) | (lanes >= SEG_COUNT)).astype(BF)
        ka[:, PAIR:] = ones
        va[:, PAIR:] = jnp.ones((rows, PAIR), BF)
        places = lax.broadcasted_iota(jnp.int32, (8, rows), 0)
        augt[...] = jnp.where(
            (places < SEG_COUNT) & (places != seg_row_ref[0]), -FAR, 0.0
        )

    ka[:, :PAIR] = qkv_ref[1]
    va[:, :PAIR] = qkv_ref[2]
    kt[...] = qkv_ref[1].T
    qt[...] = qkv_ref[0].T
    grad = dot(pick[:, :half], gnear_ref[...]) + dot(pick[:, half:], gaway_ref[...])
    go[...] = grad.astype(BF)
    dt[...] = go[...].T
    weighed = dt[...].astype(F32) * ctxt_ref[...].astype(F32)
    delta[0:1, :] = jnp.sum(weighed[:HEAD], axis=0, keepdims=True)
    delta[1:2, :] = jnp.sum(weighed[HEAD:], axis=0, keepdims=True)
    dkacc[...] = jnp.zeros_like(dkacc)
    dvacc[...] = jnp.zeros_like(dvacc)
    empty = jnp.zeros((HEAD, block), BF)
    blank = jnp.zeros((PAIR - 16, block), BF)
    wide = lax.broadcasted_iota(jnp.int32, (block, PAIR), 1)
    zero = jnp.zeros((block, PAIR), BF)

    def thirds(row, start):
        first = row.astype(BF).astype(F32)
        second = (row - first).astype(BF).astype(F32)
        third = row - first - second
        places = lax.broadcasted_iota(jnp.int32, (16, block), 0)
        return jnp.where(places == start, first,
                         jnp.where(places == start + 1, second,
                                   jnp.where(places == start + 2, third, 0.0)))

    def attended(span, keys):
        base = jnp.concatenate([augt[:, span], jnp.zeros((8, block), F32)], axis=0)
        for h in range(2):
            part = slice(h * HEAD, (h + 1) * HEAD)
            low = (base + thirds(-lse_ref[0, h:h + 1, span], SEG_COUNT)).astype(BF)
            mine = qt[part, span]
            order = (mine, empty) if h == 0 else (empty, mine)
            scores = dot(ka[keys, :], jnp.concatenate(order + (low, blank), axis=0))
            probs = jnp.exp2(scores)
            low = thirds(-delta[h:h + 1, span], 0).astype(BF)
            mine = dt[part, span]
            order = (mine, empty) if h == 0 else (empty, mine)
            slope = dot(va[keys, :], jnp.concatenate(order + (low, blank), axis=0))
            grads = (probs * slope).astype(BF)
            keep = wide < HEAD if h == 0 else wide >= HEAD
            dvacc[keys, :] += dot(probs.astype(BF), jnp.where(keep, go[span, :], zero))
            dkacc[keys, :] += dot(grads, jnp.where(keep, qkv_ref[0, span, :], zero))
            dqt[part, span] = dot(kt[part, keys], grads)

    def step(i, carry):
        attended(pl.ds(pl.multiple_of(i * block, block), block), slice(0, LONGEST))
        return carry

    lax.fori_loop(0, LONGEST // block, step, 0)
    attended(slice(LONGEST, rows), slice(LONGEST, rows))
    cosine, sine = cos_ref[0], sin_ref[0]
    turned = dqt[...].T
    grads_ref[0] = ((turned * cosine - pair_swap(turned) * sine) * (1.0 / math.sqrt(HEAD))).astype(BF)
    turned = dkacc[...]
    grads_ref[1] = ((turned * cosine - pair_swap(turned) * sine) * LN2).astype(BF)
    grads_ref[2] = dvacc[...].astype(BF)


def attend_back(b, idx_col, qkv, seg_col, seg_row, lse, ctxt, gnear, gaway, cosine, sine, block=256):
    rows, share = qkv.shape[1:]
    pairs = share // PAIR
    half = rows // 2
    whole = lambda shape: pl.BlockSpec((1,) + shape, lambda j: (b, 0, 0))
    three = pl.BlockSpec((3, rows, PAIR), lambda j: (0, 0, j))
    given = pl.BlockSpec((half, PAIR), lambda j: (b, j))
    column = lambda n: pl.BlockSpec((n, PAIR), lambda j: (0, j))
    return pl.pallas_call(
        functools.partial(attend_back_body, block),
        grid=(pairs,),
        in_specs=[whole((rows, 1)), three, whole((rows, 1)), whole((1, rows)),
                  pl.BlockSpec((1, 8, rows), lambda j: (j, 0, 0)),
                  pl.BlockSpec((PAIR, rows), lambda j: (j, 0)),
                  given, given, whole((rows, PAIR)), whole((rows, PAIR))],
        out_specs=pl.BlockSpec((3, rows, PAIR), lambda j: (0, 0, j)),
        out_shape=jax.ShapeDtypeStruct((3, rows, share), BF),
        scratch_shapes=[pltpu.VMEM((rows, rows), BF), pltpu.VMEM((rows, 2 * PAIR), BF),
                        pltpu.VMEM((rows, 2 * PAIR), BF), pltpu.VMEM((PAIR, rows), BF),
                        pltpu.VMEM((PAIR, rows), BF), pltpu.VMEM((PAIR, rows), BF),
                        pltpu.VMEM((rows, PAIR), BF), pltpu.VMEM((8, rows), F32),
                        pltpu.VMEM((rows, PAIR), F32), pltpu.VMEM((rows, PAIR), F32),
                        pltpu.VMEM((PAIR, rows), F32), pltpu.VMEM((8, rows), F32)],
        compiler_params=pltpu.CompilerParams(vmem_limit_bytes=60 << 20),
        cost_estimate=pl.CostEstimate(
            flops=pairs * 2 * 2 * rows * rows * 7 * PAIR, bytes_accessed=2 * 9 * rows * share,
            transcendentals=2 * pairs * rows * rows,
        ),
        name="attend_back",
    )(idx_col, qkv, seg_col, seg_row, lse, ctxt, gnear, gaway, cosine, sine)


def project_back_body(block, part_ref, g_ref, row_ref, wnear_ref, waway_ref,
                      near_ref, away_ref, work, hold, sems):
    rows, share = g_ref.shape[1:]
    half = near_ref.shape[0]
    for copy in own_columns(part_ref[0], wnear_ref, waway_ref, hold, sems):
        copy.wait()

    def step(i, carry):
        span = pl.ds(pl.multiple_of(i * block, block), block)
        total = None
        for place in range(3):
            term = dot_rt(g_ref[place, span, :], hold[:, place * share:(place + 1) * share])
            total = term if total is None else total + term
        work[span, :] = total.astype(BF)
        return carry

    lax.fori_loop(0, rows // block, step, 0)
    small = block // 2

    def back(i, carry):
        span = pl.ds(pl.multiple_of(i * small, small), small)
        for base, out_ref in ((half, away_ref), (0, near_ref)):
            pick = (lax.broadcasted_iota(jnp.int32, (small, rows), 0) + (base + i * small) == row_ref[0]).astype(BF)
            out_ref[span, :] = dot(pick, work[...]).astype(BF)
        return carry

    lax.fori_loop(0, half // small, back, 0)


def project_back(b, part, grads, idx_row, near_w, away_w, block=256):
    rows, share = grads.shape[1:]
    width = 2 * share
    half = rows // 2
    smem, anywhere = (pl.BlockSpec(memory_space=s) for s in (pltpu.SMEM, pl.ANY))
    return pl.pallas_call(
        functools.partial(project_back_body, block),
        grid=(1,),
        in_specs=[smem, pl.BlockSpec((3, rows, share), lambda i: (0, 0, 0)),
                  pl.BlockSpec((1, 1, rows), lambda i: (b, 0, 0)), anywhere, anywhere],
        out_specs=[pl.BlockSpec((half, width), lambda i: (0, 0))] * 2,
        scratch_shapes=[pltpu.VMEM((rows, width), BF), pltpu.VMEM((width, 3 * share), BF),
                        pltpu.SemaphoreType.DMA((6,))],
        out_shape=[jax.ShapeDtypeStruct((half, width), BF)] * 2,
        compiler_params=pltpu.CompilerParams(vmem_limit_bytes=40 << 20),
        cost_estimate=pl.CostEstimate(
            flops=2 * rows * width * (rows + 3 * share),
            bytes_accessed=2 * rows * (width + 3 * share) + 6 * width * share,
            transcendentals=0,
        ),
        name="project_back",
    )(part, grads, idx_row, near_w, away_w)


def weight_back_body(batches, *refs):
    xw_ref, g_refs, (gw_ref, gb_ref) = refs[0], refs[1:1 + batches], refs[1 + batches:]
    total, thin = None, None
    for b, g_ref in enumerate(g_refs):
        term = dot_lt(xw_ref[b], g_ref[0])
        line = jnp.sum(g_ref[0].astype(F32), axis=0, keepdims=True)
        total = term if total is None else total + term
        thin = line if thin is None else thin + line
    gw_ref[...] = total.astype(BF)
    gb_ref[...] = jnp.broadcast_to(thin, gb_ref.shape)


def weight_back(xws, grads):
    (batches, rows, width), share = xws.shape, grads[0].shape[2]
    each = pl.BlockSpec((1, rows, share), lambda s: (s, 0, 0))
    return pl.pallas_call(
        functools.partial(weight_back_body, batches),
        grid=(3,),
        in_specs=[pl.BlockSpec(xws.shape, lambda s: (0, 0, 0))] + [each] * batches,
        out_specs=[pl.BlockSpec((width, share), lambda s: (0, s)),
                   pl.BlockSpec((8, share), lambda s: (0, s))],
        out_shape=[jax.ShapeDtypeStruct((width, 3 * share), BF), jax.ShapeDtypeStruct((8, 3 * share), F32)],
        compiler_params=pltpu.CompilerParams(vmem_limit_bytes=60 << 20),
        cost_estimate=pl.CostEstimate(
            flops=2 * batches * rows * width * 3 * share,
            bytes_accessed=2 * batches * rows * (width + 3 * share) + 6 * width * share,
            transcendentals=0,
        ),
        name="weight_back",
    )(xws, *grads)


EPS = 1e-6
ERF_SLOPE = 0.3275911 * math.sqrt(0.5)
ERF_TERMS = (0.254829592, -0.284496736, 1.421413741, -1.453152027, 1.061405429)


def gauss_parts(u):
    bell = jnp.exp2(u * u * (-0.5 * LOG2E))
    t = 1.0 / (1.0 + ERF_SLOPE * jnp.abs(u))
    poly = 0.5 * ERF_TERMS[4]
    for term in ERF_TERMS[3::-1]:
        poly = poly * t + 0.5 * term
    tail = poly * t * bell
    below = jnp.where(u < 0.0, tail, 1.0 - tail)
    return u * below, below + u * bell * (1.0 / math.sqrt(2.0 * math.pi))


def row_mean(value):
    return jnp.sum(value, axis=1, keepdims=True) * (1.0 / value.shape[1])


def standard(hidden):
    centre = hidden - row_mean(hidden)
    root = lax.rsqrt(row_mean(centre * centre) + EPS)
    return centre * root, root


def standard_back(grad, norm, root):
    return root * (grad - row_mean(grad) - norm * row_mean(grad * norm))


def feed_body(chunk, part_ref, x_ref, near_ref, away_ref, dy_ref, thin_ref, bup_ref,
              unear_ref, uaway_ref, dnear_ref, daway_ref,
              out_ref, dh_ref, cnear_ref, caway_ref, sums_ref, bsum_ref,
              dmine_ref, dtheirs_ref, omine_ref, otheirs_ref,
              wo_near, wo_away, wup, wdown, slopes, acts, gup, gdown, go_near, go_away, sems, out_sems):
    core = part_ref[0]
    width, wide = wup.shape
    half_w, half_f = width // 2, wide // 2

    @pl.when(pl.program_id(0) == 0)
    def _():
        copies = []
        for t, (u_ref, d_ref) in enumerate(((unear_ref, dnear_ref), (uaway_ref, daway_ref))):
            side = core if t == 0 else 1 - core
            hold = wo_near if t == 0 else wo_away
            copies += [
                pltpu.make_async_copy(u_ref.at[:, :width], hold, sems.at[t]),
                pltpu.make_async_copy(
                    u_ref.at[:, width:], wup.at[pl.ds(pl.multiple_of(side * half_w, 128), half_w), :],
                    sems.at[2 + t]),
                pltpu.make_async_copy(
                    d_ref, wdown.at[pl.ds(pl.multiple_of(side * half_f, 128), half_f), :], sems.at[4 + t]),
            ]
        for copy in copies:
            copy.start()
        for ref in (sums_ref, bsum_ref, gup, gdown, go_near, go_away):
            ref[...] = jnp.zeros_like(ref)
        for copy in copies:
            copy.wait()

    b_out, gain_one, shift_one, b_down, gain_two, shift_two = (thin_ref[i:i + 1, :] for i in range(6))

    def tally(row, value):
        sums_ref[row:row + 1, :] += jnp.sum(value, axis=0, keepdims=True)

    attended = dot(near_ref[...], wo_near[...]) + dot(away_ref[...], wo_away[...]) + b_out
    norm_one, root_one = standard(x_ref[...].astype(F32) + attended)
    first = norm_one * gain_one + shift_one
    low = first.astype(BF)
    lowered = None
    for c in range(wide // chunk):
        cols = slice(c * chunk, (c + 1) * chunk)
        act, slope = gauss_parts(dot(low, wup[:, cols]) + bup_ref[:, cols])
        act = act.astype(BF)
        acts[:, cols] = act
        slopes[:, cols] = slope.astype(BF)
        term = dot(act, wdown[cols, :])
        lowered = term if lowered is None else lowered + term
    norm_two, root_two = standard(first + lowered + b_down)
    out_ref[...] = (norm_two * gain_two + shift_two).astype(BF)
    dy = dy_ref[...].astype(F32)
    tally(4, dy * norm_two)
    tally(5, dy)
    grad_two = standard_back(dy * gain_two, norm_two, root_two)
    dlow = grad_two.astype(BF)
    tally(3, dlow.astype(F32))
    total = grad_two
    low_t, dlow_t = low.T, dlow.T
    for c in range(wide // chunk):
        cols = slice(c * chunk, (c + 1) * chunk)
        dup = (dot_rt(dlow, wdown[cols, :]) * slopes[:, cols].astype(F32)).astype(BF)
        gdown[:, cols] += dot(dlow_t, acts[:, cols])
        gup[:, cols] += dot(low_t, dup)
        bsum_ref[0:1, cols] += jnp.sum(dup.astype(F32), axis=0, keepdims=True)
        total = total + dot_rt(dup, wup[:, cols])
    tally(1, total * norm_one)
    tally(2, total)
    grad_one = standard_back(total * gain_one, norm_one, root_one)
    dh_ref[...] = grad_one
    da = grad_one.astype(BF)
    tally(0, da.astype(F32))
    go_near[...] += dot(near_ref[...].T, da)
    go_away[...] += dot(away_ref[...].T, da)
    cnear_ref[...] = dot_rt(da, wo_near[...]).astype(BF)
    caway_ref[...] = dot_rt(da, wo_away[...]).astype(BF)

    @pl.when(pl.program_id(0) == pl.num_programs(0) - 1)
    def _():
        rows_d = [pl.ds(pl.multiple_of(side * half_f, 128), half_f) for side in (core, 1 - core)]
        rows_u = [pl.ds(pl.multiple_of(side * half_w, 128), half_w) for side in (core, 1 - core)]
        copies = []
        for t, (d_ref, o_ref, hold) in enumerate(((dmine_ref, omine_ref, wo_near), (dtheirs_ref, otheirs_ref, wo_away))):
            copies += [
                pltpu.make_async_copy(wdown.at[rows_d[t], :], d_ref, out_sems.at[3 * t]),
                pltpu.make_async_copy(wup.at[rows_u[t], :], o_ref.at[:, :wide], out_sems.at[3 * t + 1]),
                pltpu.make_async_copy(hold, o_ref.at[:, wide:], out_sems.at[3 * t + 2]),
            ]
        for c in range(wide // width):
            cols = slice(c * width, (c + 1) * width)
            wdown[cols, :] = gdown[:, cols].T.astype(BF)
        copies[0].start()
        copies[3].start()
        for c in range(wide // width):
            cols = slice(c * width, (c + 1) * width)
            wup[:, cols] = gup[:, cols].astype(BF)
        wo_near[...] = go_near[...].astype(BF)
        wo_away[...] = go_away[...].astype(BF)
        for k in (1, 2, 4, 5):
            copies[k].start()
        for copy in copies:
            copy.wait()


def feed(part, x, near, away, dy, thin, bup, unear, uaway, dnear, daway, block=256, chunk=768):
    rows, width = x.shape
    share = near.shape[1]
    wide = bup.shape[1]
    line = lambda n: pl.BlockSpec((block, n), lambda i: (i, 0))
    fixed = lambda shape: pl.BlockSpec(shape, lambda i: (0, 0))
    anywhere = pl.BlockSpec(memory_space=pl.ANY)
    shape = lambda n, dt: jax.ShapeDtypeStruct((rows, n), dt)
    half = lambda n, m: jax.ShapeDtypeStruct((n // 2, m), BF)
    return pl.pallas_call(
        functools.partial(feed_body, chunk),
        grid=(rows // block,),
        in_specs=[pl.BlockSpec(memory_space=pltpu.SMEM), line(width), line(share), line(share), line(width),
                  fixed(thin.shape), fixed(bup.shape), anywhere, anywhere, anywhere, anywhere],
        out_specs=[line(width), line(width), line(share), line(share), fixed((8, width)), fixed((8, wide))]
        + [anywhere] * 4,
        out_shape=[shape(width, BF), shape(width, F32), shape(share, BF), shape(share, BF),
                   jax.ShapeDtypeStruct((8, width), F32), jax.ShapeDtypeStruct((8, wide), F32),
                   half(wide, width), half(wide, width), half(width, wide + width), half(width, wide + width)],
        scratch_shapes=[pltpu.VMEM((share, width), BF), pltpu.VMEM((share, width), BF),
                        pltpu.VMEM((width, wide), BF), pltpu.VMEM((wide, width), BF),
                        pltpu.VMEM((block, wide), BF), pltpu.VMEM((block, wide), BF),
                        pltpu.VMEM((width, wide), F32), pltpu.VMEM((width, wide), F32),
                        pltpu.VMEM((share, width), F32), pltpu.VMEM((share, width), F32),
                        pltpu.SemaphoreType.DMA((6,)), pltpu.SemaphoreType.DMA((6,))],
        compiler_params=pltpu.CompilerParams(vmem_limit_bytes=60 << 20),
        cost_estimate=pl.CostEstimate(
            flops=2 * rows * width * (3 * width + 6 * wide),
            bytes_accessed=2 * rows * 7 * width + 8 * width * (wide + width),
            transcendentals=2 * rows * wide,
        ),
        name="feed",
    )(part, x, near, away, dy, thin, bup, unear, uaway, dnear, daway)


def swap_cores(value):
    return lax.ppermute(value, "seq", [(0, 1), (1, 0)])


def swap_x(value):
    return lax.ppermute(value, "fsdp", [(i, i ^ 1) for i in range(16)])


def swap_y(value):
    return lax.ppermute(value, "fsdp", [(i, i ^ 2) for i in range(16)])


def flip_z(value, k):
    return lax.ppermute(value, "fsdp", [(i, i ^ (4 * k)) for i in range(16)])


def shift_z(value, k):
    return lax.ppermute(value, "fsdp", [(i, (i + 4 * k) % 16) for i in range(16)])


def assemble_body(lines, place_ref, ax_ref, ay_ref, bx_ref, by_ref, *out_refs):
    place = place_ref[0]
    z, y, x = place // 4, (place // 2) % 2, place % 2
    n = ax_ref.shape[1]

    def put(owner, piece):
        out_refs[0][owner] = piece[:, :out_refs[0].shape[2]]
        for c in range(lines):
            width = out_refs[1].shape[2]
            at = out_refs[0].shape[2] + c * width
            out_refs[1][owner, c * n:(c + 1) * n, :] = piece[:, at:at + width]

    for j in range(4):
        k, o = j % 2, j // 2
        near_z, far_z = lax.rem(z - k + 4, 4), lax.rem(z - k + 2, 4)
        flip_x = lax.rem(x + o, 2)
        flip_y = lax.rem(y + o, 2)
        put(near_z * 4 + y * 2 + flip_x, ax_ref[j])
        put(near_z * 4 + (1 - y) * 2 + flip_x, ay_ref[j])
        put(far_z * 4 + flip_y * 2 + x, by_ref[j])
        put(far_z * 4 + flip_y * 2 + 1 - x, bx_ref[j])


def assemble(place, parts, lines=0, line=0):
    n, width = parts[0].shape[1:]
    vmem = pl.BlockSpec(memory_space=pltpu.VMEM)
    shapes = [(16, n, width - lines * line)] + ([(16, lines * n, line)] if lines else [])
    return pl.pallas_call(
        functools.partial(assemble_body, lines),
        in_specs=[pl.BlockSpec(memory_space=pltpu.SMEM)] + [vmem] * 4,
        out_shape=[jax.ShapeDtypeStruct(shape, BF) for shape in shapes],
        compiler_params=pltpu.CompilerParams(vmem_limit_bytes=40 << 20),
        cost_estimate=pl.CostEstimate(flops=0, bytes_accessed=4 * 16 * n * width, transcendentals=0),
        name="assemble",
    )(place, *parts)


def tie(values, after=()):
    return lax.optimization_barrier((values, after))[0]


def reach_z(shard):
    first = jnp.stack([shard, shift_z(shard, 1)])
    second = jnp.stack([shift_z(shard, 2), shift_z(shard, 3)])
    return first, second


def reach_one(first, second):
    return jnp.concatenate([first, swap_x(first)], axis=0), jnp.concatenate([second, swap_y(second)], axis=0)


def reach_two(first, second):
    return first, swap_y(first), swap_x(second), second


def joined(parts, lines=0, line=0):
    place = jnp.full((1,), lax.axis_index("fsdp"), jnp.int32)
    return [value.reshape(-1, value.shape[2]) for value in assemble(place, parts, lines, line)]


def pick(part, at, axis):
    return lax.dynamic_index_in_dim(part, at, axis, keepdims=False)


def corner():
    place = lax.axis_index("fsdp")
    return place // 4, (place // 2) % 2, place % 2


def fold_call(body, name, grid, place, operands, in_specs, out_specs, out_shape):
    size = sum(math.prod(item.shape) for item in out_shape)
    return pl.pallas_call(
        body,
        grid_spec=pltpu.PrefetchScalarGridSpec(
            num_scalar_prefetch=1, grid=grid, in_specs=in_specs, out_specs=out_specs),
        out_shape=out_shape,
        compiler_params=pltpu.CompilerParams(vmem_limit_bytes=40 << 20),
        cost_estimate=pl.CostEstimate(flops=0, bytes_accessed=8 * size, transcendentals=0),
        name=name,
    )(place, *operands)


def merge_one_body(place_ref, *refs):
    count = len(refs) // 3
    for mine, theirs, out in zip(refs[:count], refs[count:2 * count], refs[2 * count:]):
        out[0, 0] = (mine[0, 0, 0, 0].astype(F32) + theirs[0, 0, 0, 0].astype(F32)).astype(BF)


def merge_one(place, mines, theirs):
    cubes = lambda values: [v.reshape(2, 2, 2, 2, v.shape[0] // 16, v.shape[1]) for v in values for _ in range(2)]
    specs, outs, shapes = [], [], []
    for value in mines:
        n, width = value.shape[0] // 16, value.shape[1]
        specs += [pl.BlockSpec((1, 1, 1, 1, n, width), lambda k, j, p: (0, k, 1 - p[1], j, 0, 0)),
                  pl.BlockSpec((1, 1, 1, 1, n, width), lambda k, j, p: (1, k, j, 1 - p[2], 0, 0))]
        outs += [pl.BlockSpec((1, 1, n, width), lambda k, j, p: (k, j, 0, 0))] * 2
        shapes += [jax.ShapeDtypeStruct((2, 2, n, width), BF)] * 2
    return fold_call(merge_one_body, "merge_one", (2, 2), place, cubes(mines) + cubes(theirs), specs * 2, outs, shapes)


def merge_two_body(place_ref, *refs):
    count = len(refs) // 5
    y, x = place_ref[1], place_ref[2]
    groups = [refs[i * count:(i + 1) * count] for i in range(5)]
    for i, (mine, theirs, came, stay, send) in enumerate(zip(*groups)):
        if i % 2 == 0:
            part = lambda at: mine[0, 0, 0, at].astype(F32) + theirs[0, 0, 0, at].astype(F32) + came[0, at].astype(F32)
            own = x
        else:
            part = lambda at: mine[0, 0, at, 0].astype(F32) + theirs[0, 0, at, 0].astype(F32) + came[0, at].astype(F32)
            own = y
        stay[0] = part(own)
        send[0] = part(1 - own).astype(BF)


def merge_two(place, mines, theirs, came):
    cubes = lambda values: [v.reshape(2, 2, 2, 2, v.shape[0] // 16, v.shape[1]) for v in values for _ in range(2)]
    specs, came_specs, outs, stays, sends = [], [], [], [], []
    for value in mines:
        n, width = value.shape[0] // 16, value.shape[1]
        specs += [pl.BlockSpec((1, 1, 1, 2, n, width), lambda k, p: (0, k, p[1], 0, 0, 0)),
                  pl.BlockSpec((1, 1, 2, 1, n, width), lambda k, p: (1, k, 0, p[2], 0, 0))]
        came_specs += [pl.BlockSpec((1, 2, n, width), lambda k, p: (k, 0, 0, 0))] * 2
        outs += [pl.BlockSpec((1, n, width), lambda k, p: (k, 0, 0))] * 2
        stays += [jax.ShapeDtypeStruct((2, n, width), F32)] * 2
        sends += [jax.ShapeDtypeStruct((2, n, width), BF)] * 2
    both = fold_call(merge_two_body, "merge_two", (2,), place, cubes(mines) + cubes(theirs) + list(came),
                     specs * 2 + came_specs, outs * 2, stays + sends)
    return both[:len(stays)], both[len(stays):]


def merge_three_body(place_ref, *refs):
    stays, came, (stay_ref, send_ref) = refs[:4], refs[4:8], refs[8:]
    near = lax.rem(place_ref[0], 2)
    n = stay_ref.shape[1]
    for half in range(2):
        for at, out in ((near, stay_ref), (1 - near, send_ref)):
            lines = stays[half][at] + came[half][at].astype(F32)
            wide = stays[2 + half][at] + came[2 + half][at].astype(F32)
            out[half, :, :wide.shape[1]] = wide.astype(out.dtype)
            for c in range(lines.shape[0] // n):
                to = wide.shape[1] + c * lines.shape[1]
                out[half, :, to:to + lines.shape[1]] = lines[c * n:(c + 1) * n].astype(out.dtype)


def merge_three(place, stays, came):
    rows, line = stays[0].shape[1:]
    n, wide = stays[2].shape[1:]
    total = wide + rows // n * line
    whole = lambda shape: pl.BlockSpec(shape, lambda p: (0,) * len(shape))
    shapes = [jax.ShapeDtypeStruct((2, n, total), F32), jax.ShapeDtypeStruct((2, n, total), BF)]
    return fold_call(merge_three_body, "merge_three", (), place, list(stays) + list(came),
                     [whole(v.shape) for v in list(stays) + list(came)], [whole(v.shape) for v in shapes], shapes)


def fold_one(value):
    z, y, x = corner()
    rows, width = value.shape
    cube = value.reshape(2, 2, 2, 2, rows // 16, width)
    return (value,), (pick(cube[0], 1 - y, 1).astype(BF), pick(cube[1], 1 - x, 2).astype(BF))


def fold_two(stay, sends, after=()):
    z, y, x = corner()
    rows, width = stay[0].shape
    cube = stay[0].reshape(2, 2, 2, 2, rows // 16, width)
    came = tie((swap_y(sends[0]), swap_x(sends[1])), after)
    first = pick(cube[0], y, 1).astype(F32) + came[0].astype(F32)
    second = pick(cube[1], x, 2).astype(F32) + came[1].astype(F32)
    return (first, second), (pick(first, 1 - x, 1).astype(BF), pick(second, 1 - y, 1).astype(BF))


def fold_cross(stay, sends, after=()):
    z, y, x = corner()
    came = tie((swap_x(sends[0]), swap_y(sends[1])), after)
    first = pick(stay[0], x, 1) + came[0].astype(F32)
    second = pick(stay[1], y, 1) + came[1].astype(F32)
    return jnp.concatenate([first, second], axis=0)


def fold_three(stack):
    near = corner()[0] % 2
    cube = stack.reshape((2, 2) + stack.shape[1:])
    return (pick(cube, near, 1),), (pick(cube, 1 - near, 1).astype(BF),)


def fold_four(stay, sends, after=()):
    z = corner()[0]
    far = z // 2
    came = tie(flip_z(sends[0], 1), after)
    total = stay[0] + came.astype(F32)
    return (pick(total, far, 0),), (pick(total, 1 - far, 0).astype(BF),)


def fold_end(stay, sends, after=()):
    return stay[0] + tie(flip_z(sends[0], 2), after).astype(F32)


def on_device(tokens, permutation, segment_ids, cotangent, *shards):
    batches = tokens.shape[0]
    half, width = tokens.shape[2], tokens.shape[3]
    core = lax.axis_index("seq")
    share = width // 2
    owners = 2 * lax.axis_size("fsdp")
    staged = owners == 32
    part = jnp.full((1,), core, jnp.int32)
    thin = [i for i, piece in enumerate(shards) if piece.ndim == 1]
    sizes = [shards[i].shape[0] for i in thin]
    count = sum(sizes)
    n_qkv = shards[0].shape[0]
    room = n_qkv * 128
    tokens, cotangent = tokens[:, 0], cotangent[:, 0]

    away_tokens = swap_cores(tokens)
    idx_col, idx_row, seg_col, seg_row, cosine, sine = ready(part, permutation[:, 0], segment_ids[:, 0])
    if staged:
        q_shard, ud_shard = pack(shards[0], shards[2], shards[6], shards[8], [shards[i] for i in thin])
        first, second = reach_z(q_shard)
        first, second, idx_col = tie((first, second, idx_col))
        first_x, second_y = swap_x(first), swap_y(second)
        ud_shard = tie(ud_shard, first_x)
        q_parts = reach_two(jnp.concatenate([first, first_x], axis=0), jnp.concatenate([second, second_y], axis=0))
        ud_z = tuple(shift_z(ud_shard, k) for k in (1, 2, 3))
        xws = arrange(idx_col, tokens, away_tokens)
        q_parts = tie(q_parts, xws)
        (q_near,) = joined(q_parts)
    else:
        xws = arrange(idx_col, tokens, away_tokens)
        packed = jnp.concatenate([shards[i] for i in thin] + [jnp.zeros((room - count,), BF)])
        q_shard = jnp.concatenate([shards[0], packed.reshape(n_qkv, 128)], axis=1)
        q_near = lax.all_gather(q_shard, "fsdp", axis=0, tiled=True)
        u_near = lax.all_gather(jnp.concatenate([shards[2], shards[6]], axis=1), "fsdp", axis=0, tiled=True)
        d_near = lax.all_gather(shards[8], "fsdp", axis=0, tiled=True)
    q_away = swap_cores(q_near)

    slabs = [value[:, 3 * width:].reshape(owners // 2, n_qkv, 128) for value in (q_near, q_away)]
    vectors = jnp.concatenate(
        [jnp.where(core == 0, slabs[0], slabs[1]), jnp.where(core == 0, slabs[1], slabs[0])], axis=0
    ).astype(F32)
    spread, at = [], 0
    for i, size in enumerate(sizes):
        if staged:
            spread.append(vectors[:, i, :size].reshape(1, owners * size))
        else:
            spread.append(vectors.reshape(owners, room)[:, at:at + size].reshape(1, owners * size))
        at += size
    b_qkv, b_out, gain_one, shift_one, b_up, b_down, gain_two, shift_two = spread
    bias_own = jnp.concatenate(
        [lax.dynamic_slice_in_dim(b_qkv, core * share + s * width, share, 1) for s in range(3)], axis=1
    )
    blank_row = jnp.zeros((1, width), F32)
    thin_rows = jnp.concatenate(
        [b_out, gain_one, shift_one, b_down, gain_two, shift_two, blank_row, blank_row], axis=0
    )

    qkvs = [project(b, part, xws, q_near, q_away, bias_own, cosine, sine) for b in range(batches)]
    if staged:
        (one, two, three), qkvs = tie((ud_z, qkvs))
        first, second = jnp.stack([ud_shard, one]), jnp.stack([two, three])
        qkvs[0], first, second = tie((qkvs[0], first, second))
        first_x, second_y = swap_x(first), swap_y(second)
    kept, ctxs = [], []
    for b in range(batches):
        if staged and b == 1:
            first_x, second_y = tie((first_x, second_y), ctxs[0][0])
            first, second = jnp.concatenate([first, first_x], axis=0), jnp.concatenate([second, second_y], axis=0)
            qkvs[1], first, second = tie((qkvs[1], first, second))
            first_y, second_x = swap_y(first), swap_x(second)
        near, away, ctxt, lse = attend(b, idx_col, qkvs[b], seg_col, seg_row)
        kept.append((qkvs[b], ctxt, lse))
        ctxs.append((near, swap_cores(away)))
    if staged:
        first_y, second_x = tie((first_y, second_x), ctxs[1][0])
        u_near, d_near = joined((first, first_y, second_x, second), 4, width)
    u_away, d_away = swap_cores(u_near), swap_cores(d_near)
    near, away = (jnp.concatenate([item[i] for item in ctxs], axis=0) for i in range(2))
    (outputs, grad_one, cnear, caway, sums, bsum, d_mine, d_theirs, uo_mine, uo_theirs) = feed(
        part, tokens.reshape(batches * half, width), near, away,
        cotangent.reshape(batches * half, width), thin_rows, b_up, u_near, u_away, d_near, d_away,
    )
    caway = swap_cores(caway)
    d_theirs, uo_theirs = swap_cores(d_theirs), swap_cores(uo_theirs)
    plus = lambda mine, theirs: (mine.astype(F32) + theirs.astype(F32)).astype(BF)

    def back(b, given):
        qkv, ctxt, lse = kept[b]
        return attend_back(b, idx_col, qkv, seg_col, seg_row, lse, ctxt, *given, cosine, sine)

    givens = [(cnear, caway)] * batches
    if staged:
        first_back = back(0, givens[0])
        place = jnp.stack(corner()).astype(jnp.int32)
        mines, theirs = (d_mine, uo_mine), tie((d_theirs, uo_theirs), first_back)
        sends = merge_one(place, mines, theirs)
        given, sends = tie((givens[1], sends))
        grads = [first_back, back(1, given)]
        swaps = (swap_y, swap_x)
        came = tie([swaps[i % 2](send) for i, send in enumerate(sends)], grads[1])
        stays, sends = merge_two(place, mines, theirs, came)
        grads, sends = tie((grads, sends))
    else:
        grads = [back(b, givens[b]) for b in range(batches)]
        d_sum, uo_sum = plus(d_mine, d_theirs), plus(uo_mine, uo_theirs)
    gw_own, gb_own = weight_back(xws, grads)
    if staged:
        came = tie([swaps[1 - i % 2](send) for i, send in enumerate(sends)], gw_own)
        stay, send = merge_three(place, stays, came)
        grads, gw_own, gb_own, send = tie((grads, gw_own, gb_own, send))
        du_step = ((stay,), (send,))

    def halves(value):
        size = value.shape[0] // 2
        return (lax.dynamic_slice_in_dim(value, core * size, size, 0),
                lax.dynamic_slice_in_dim(value, (1 - core) * size, size, 0))

    blank = jnp.zeros((share,), F32)
    thin_columns = []
    for s in range(3):
        span = slice(s * share, (s + 1) * share)
        thin_columns += [jnp.where(core == 0, gb_own[0, span], blank),
                         jnp.where(core == 0, blank, gb_own[0, span])]
    six = sums[:6].reshape(6, owners, -1).transpose(1, 0, 2).reshape(owners, -1)
    slab = jnp.concatenate(
        [jnp.concatenate(thin_columns).reshape(owners, -1), bsum[0].reshape(owners, -1), six,
         jnp.zeros((owners, room - count), F32)], axis=1
    ).astype(BF).reshape(owners * n_qkv, 128)
    mine, theirs = (jnp.concatenate(pair, axis=1) for pair in zip(halves(gw_own), halves(slab)))
    theirs = swap_cores(theirs)
    q_sum = jnp.concatenate([
        mine[:, :3 * share], theirs[:, :3 * share],
        (mine[:, 3 * share:].astype(F32) + theirs[:, 3 * share:].astype(F32)).astype(BF),
    ], axis=1)
    backs = [project_back(0, part, grads[0], idx_row, q_near, q_away)]
    if staged:
        du_step = fold_four(*du_step, backs[0])
        last, q_step, du_step = tie((grads[1], fold_one(q_sum), du_step), backs)
        backs.append(project_back(1, part, last, idx_row, q_near, q_away))
        q_step = tie(fold_two(*q_step, backs[1]))
        g_uo = fold_end(*du_step, q_step)
        q_step = tie(fold_three(fold_cross(*q_step, g_uo)))
        q_step = fold_four(*q_step)
        g_down = jnp.concatenate([g_uo[:, (5 + i) * width:(6 + i) * width] for i in range(4)], axis=0)
    else:
        backs.append(project_back(1, part, grads[1], idx_row, q_near, q_away))
        summed = lambda value: lax.psum_scatter(
            value.astype(BF), "fsdp", scatter_dimension=0, tiled=True
        ).astype(F32)
        g_qkv, g_down, g_uo = summed(q_sum), summed(d_sum), summed(uo_sum)
    grad_one = grad_one.reshape(batches, half, width)
    token_grad = jnp.stack([
        (grad_one[b] + backs[b][0].astype(F32) + swap_cores(backs[b][1]).astype(F32)).astype(BF)
        for b in range(batches)
    ])
    if staged:
        g_qkv = fold_end(*q_step, (g_uo, token_grad))
    own, other = g_qkv[:, :3 * share], g_qkv[:, 3 * share:6 * share]
    columns = []
    for s in range(3):
        span = slice(s * share, (s + 1) * share)
        columns += [jnp.where(core == 0, own[:, span], other[:, span]),
                    jnp.where(core == 0, other[:, span], own[:, span])]
    g_out, g_up = g_uo[:, 4 * width:5 * width], g_uo[:, :4 * width]
    flat = g_qkv[:, 3 * width:].reshape(room)
    thin_out, at = [], 0
    for size in [sizes[0], sizes[4]] + [n_qkv] * 6:
        thin_out.append(flat[at:at + size])
        at += size
    g_bqkv, g_bup, g_bout, g_g1, g_s1, g_bdown, g_g2, g_s2 = thin_out
    return (
        outputs.reshape(batches, 1, half, width), token_grad[:, None],
        jnp.concatenate(columns, axis=1), g_bqkv, g_out, g_bout, g_g1, g_s1, g_up, g_bup, g_down, g_bdown, g_g2, g_s2,
    )


def solution(mesh):
    packs = P(None, "fsdp", "seq", None)
    ids = P(None, "fsdp", None)
    deep, flat = P(("seq", "fsdp"), None), P(("seq", "fsdp"))
    layers = (deep, flat, deep, flat, flat, flat, deep, flat, deep, flat, flat, flat)
    return jax.shard_map(
        on_device, mesh=mesh, in_specs=(packs, ids, ids, packs) + layers,
        out_specs=(packs, packs) + layers, check_vma=False,
    )
```

```python
import functools
import math

import jax
import jax.numpy as jnp
from jax import lax
from jax.experimental import pallas as pl
from jax.experimental.pallas import tpu as pltpu
from jax.sharding import PartitionSpec as P

HEAD = 64
PAIR = 2 * HEAD
SEG_COUNT = 4
LONGEST = 1024
LOG2E = math.log2(math.e)
LN2 = math.log(2.0)
FAR = float(2**30)
BF = jnp.bfloat16
F32 = jnp.float32


def dot(left, right):
    return jnp.dot(left, right, preferred_element_type=F32)


def dot_rt(left, right):
    return lax.dot_general(left, right, (((1,), (1,)), ((), ())), preferred_element_type=F32)


def dot_lt(left, right):
    return lax.dot_general(left, right, (((0,), (0,)), ((), ())), preferred_element_type=F32)


def pair_swap(values):
    lanes = lax.broadcasted_iota(jnp.int32, values.shape, 1)
    width = values.shape[1]
    return jnp.where(
        lanes % 2 == 0, pltpu.roll(values, width - 1, 1), pltpu.roll(values, 1, 1)
    )


def ready_body(part_ref, order_ref, seg_ref, freq_ref, idx_col, idx_row, seg_col, seg_row, cos_ref, sin_ref):
    core = part_ref[0]
    batches, rows = order_ref.shape
    half = rows // 2
    lanes = lax.broadcasted_iota(jnp.int32, (1, rows), 1)
    wide = lax.broadcasted_iota(jnp.int32, (8, rows), 1)
    halves = freq_ref.shape[0]
    cols = lax.broadcasted_iota(jnp.int32, (halves, PAIR), 1)
    lines = lax.broadcasted_iota(jnp.int32, (halves, PAIR), 0)
    grow = ((cols % HEAD) // 2 == lines).astype(F32)
    turn = jnp.where(cols % 2 == 0, -grow, grow)
    expand = lambda value, by: lax.dot_general(
        value, by, (((0,), (0,)), ((), ())), preferred_element_type=F32, precision=lax.Precision.HIGHEST)
    for b in range(batches):
        order, seg = order_ref[b:b + 1, :], seg_ref[b:b + 1, :]
        starts, start, total = [], 0, 0
        for s in range(SEG_COUNT):
            size = jnp.sum((seg == s).astype(F32)).astype(jnp.int32)
            starts.append(total)
            start = start + jnp.where(size == LONGEST, total, 0)
            total = total + size
        table = jnp.concatenate([order, seg, lanes, jnp.zeros((5, rows), jnp.int32)], axis=0)
        main = pltpu.roll(table, rows - start, 1)
        early = pltpu.roll(table, LONGEST, 1)
        table = jnp.where(wide < LONGEST, main, jnp.where(wide - LONGEST < start, early, table))
        order, seg, place = table[0:1], table[1:2], table[2:3]
        origin = jnp.zeros_like(seg)
        for s in range(1, SEG_COUNT):
            origin = jnp.where(seg == s, starts[s], origin)
        position = (place - origin).astype(F32)
        near = (order >= half).astype(jnp.int32) == core
        idx = jnp.where(near, order - core * half, order + core * half)
        idx_row[b] = idx
        seg_row[b] = seg
        both = jnp.concatenate([idx.astype(F32), seg.astype(F32), jnp.zeros((6, rows), F32)], axis=0).T
        idx_col[b] = both[:, 0:1].astype(jnp.int32)
        seg_col[b] = both[:, 1:2].astype(jnp.int32)
        phase = freq_ref[...] * position
        cos_ref[b] = expand(jnp.cos(phase), grow)
        sin_ref[b] = expand(jnp.sin(phase), turn)


def ready(part, order, segments):
    batches, rows = order.shape
    halves = HEAD // 2
    freqs = jnp.exp(jnp.arange(halves, dtype=F32) * (-2.0 * math.log(10000.0) / HEAD))[:, None]
    vmem, smem = (pl.BlockSpec(memory_space=s) for s in (pltpu.VMEM, pltpu.SMEM))
    ints = lambda *shape: jax.ShapeDtypeStruct(shape, jnp.int32)
    return pl.pallas_call(
        ready_body,
        in_specs=[smem, vmem, vmem, vmem],
        out_shape=[ints(batches, rows, 1), ints(batches, 1, rows), ints(batches, rows, 1), ints(batches, 1, rows),
                   jax.ShapeDtypeStruct((batches, rows, PAIR), F32), jax.ShapeDtypeStruct((batches, rows, PAIR), F32)],
        compiler_params=pltpu.CompilerParams(vmem_limit_bytes=40 << 20),
        cost_estimate=pl.CostEstimate(
            flops=1 << 30, bytes_accessed=8 * batches * rows * 3 * PAIR, transcendentals=2 * batches * rows * halves
        ),
        name="ready",
    )(part, order, segments, freqs)


def pack_body(thin, w_qkv, w_out, w_up, w_down, *refs):
    q_ref, ud_ref = refs[thin:]
    n, width = w_out.shape
    wide = w_qkv.shape[1]
    q_ref[:, :wide] = w_qkv[...]
    q_ref[:, wide:] = jnp.zeros((n, q_ref.shape[1] - wide), BF)
    for i, ref in enumerate(refs[:thin]):
        q_ref[i:i + 1, wide:wide + ref.shape[1]] = ref[...]
    ud_ref[:, :width] = w_out[...]
    ud_ref[:, width:width + w_up.shape[1]] = w_up[...]
    at = width + w_up.shape[1]
    for c in range(w_down.shape[0] // n):
        ud_ref[:, at + c * width:at + (c + 1) * width] = w_down[c * n:(c + 1) * n, :]


def pack(w_qkv, w_out, w_up, w_down, thin):
    n, width = w_out.shape
    wide = width + w_up.shape[1] + w_down.shape[0] // n * width
    return pl.pallas_call(
        functools.partial(pack_body, len(thin)),
        out_shape=[jax.ShapeDtypeStruct((n, w_qkv.shape[1] + 128), BF), jax.ShapeDtypeStruct((n, wide), BF)],
        cost_estimate=pl.CostEstimate(flops=0, bytes_accessed=4 * n * (w_qkv.shape[1] + wide), transcendentals=0),
        name="pack",
    )(w_qkv, w_out, w_up, w_down, *[value[None] for value in thin])


def arrange_body(block, idx_ref, own_ref, other_ref, xw_ref):
    half = own_ref.shape[1]

    def step(i, carry):
        rows = pl.ds(pl.multiple_of(i * block, block), block)
        picks = lax.broadcasted_iota(jnp.int32, (block, half), 1)
        source = idx_ref[0, rows, :]
        near = (picks == source).astype(BF)
        away = (picks + half == source).astype(BF)
        xw_ref[0, rows, :] = (dot(near, own_ref[0]) + dot(away, other_ref[0])).astype(BF)
        return carry

    lax.fori_loop(0, idx_ref.shape[1] // block, step, 0)


def arrange(idx_col, own, other, block=256):
    batches, rows = idx_col.shape[:2]
    half, width = own.shape[1:]
    each = lambda *shape: pl.BlockSpec((1,) + shape, lambda b: (b, 0, 0))
    return pl.pallas_call(
        functools.partial(arrange_body, block),
        grid=(batches,),
        in_specs=[each(rows, 1), each(half, width), each(half, width)],
        out_specs=each(rows, width),
        out_shape=pltpu.HBM((batches, rows, width), BF),
        compiler_params=pltpu.CompilerParams(vmem_limit_bytes=40 << 20),
        cost_estimate=pl.CostEstimate(
            flops=2 * batches * rows * rows * width, bytes_accessed=4 * batches * rows * width, transcendentals=0
        ),
        name="arrange",
    )(idx_col, own, other)


def own_columns(core, near_ref, away_ref, hold, sems):
    span, share = near_ref.shape[0], hold.shape[1] // 3
    copies = []
    for s in range(3):
        for t, ref in enumerate((near_ref, away_ref)):
            side = core if t == 0 else 1 - core
            copies.append(
                pltpu.make_async_copy(
                    ref.at[:, pl.ds(pl.multiple_of(core * share + 2 * s * share, 128), share)],
                    hold.at[pl.ds(pl.multiple_of(side * span, 128), span), s * share:(s + 1) * share],
                    sems.at[2 * s + t],
                )
            )
    for copy in copies:
        copy.start()
    return copies


def project_body(block, part_ref, xw_ref, near_ref, away_ref, bias_ref, cos_ref, sin_ref,
                 qkv_ref, hold, sems):
    share = qkv_ref.shape[2]
    for copy in own_columns(part_ref[0], near_ref, away_ref, hold, sems):
        copy.wait()

    def step(i, carry):
        rows = pl.ds(pl.multiple_of(i * block, block), block)
        work = xw_ref[0, rows, :]
        cosine, sine = cos_ref[0, rows, :], sin_ref[0, rows, :]
        for place, scale in ((0, LOG2E / math.sqrt(HEAD)), (1, 1.0)):
            whole = slice(place * share, (place + 1) * share)
            pre = dot(work, hold[:, whole]) + bias_ref[:, whole]
            for j in range(share // PAIR):
                cols = slice(j * PAIR, (j + 1) * PAIR)
                piece = pre[:, cols]
                qkv_ref[place, rows, cols] = (
                    (piece * cosine + pair_swap(piece) * sine) * scale
                ).astype(BF)
        qkv_ref[2, rows, :] = (dot(work, hold[:, 2 * share:]) + bias_ref[:, 2 * share:]).astype(BF)
        return carry

    lax.fori_loop(0, xw_ref.shape[1] // block, step, 0)


def project(b, part, xws, near_w, away_w, bias_own, cosine, sine, block=256):
    rows, width = xws.shape[1:]
    share = bias_own.shape[1] // 3
    each = lambda n: pl.BlockSpec((1, rows, n), lambda i: (b, 0, 0))
    vmem, smem, anywhere = (pl.BlockSpec(memory_space=s) for s in (pltpu.VMEM, pltpu.SMEM, pl.ANY))
    return pl.pallas_call(
        functools.partial(project_body, block),
        grid=(1,),
        in_specs=[smem, each(width), anywhere, anywhere, vmem, each(PAIR), each(PAIR)],
        out_specs=pl.BlockSpec((3, rows, share), lambda i: (0, 0, 0)),
        out_shape=pltpu.HBM((3, rows, share), BF),
        scratch_shapes=[pltpu.VMEM((width, 3 * share), BF), pltpu.SemaphoreType.DMA((6,))],
        compiler_params=pltpu.CompilerParams(vmem_limit_bytes=40 << 20),
        cost_estimate=pl.CostEstimate(
            flops=2 * rows * width * 3 * share,
            bytes_accessed=2 * (rows * width + 3 * width * share + 3 * rows * share),
            transcendentals=0,
        ),
        name="project",
    )(part, xws, near_w, away_w, bias_own, cosine, sine)


def attend_body(block, idx_ref, qkv_ref, seg_col_ref, seg_row_ref,
                near_ref, away_ref, ctxt_ref, lse_ref, pick, ka, vt, qt, augt):
    rows = qkv_ref.shape[1]
    half = near_ref.shape[0]

    @pl.when(pl.program_id(0) == 0)
    def _():
        def fill(i, carry):
            span = pl.ds(pl.multiple_of(i * block, block), block)
            pick[span, :] = (
                lax.broadcasted_iota(jnp.int32, (block, rows), 1) == idx_ref[0, span, :]
            ).astype(BF)
            return carry

        lax.fori_loop(0, rows // block, fill, 0)
        lanes = lax.broadcasted_iota(jnp.int32, (rows, PAIR), 1)
        ka[:, PAIR:] = ((lanes == seg_col_ref[0]) | (lanes >= SEG_COUNT)).astype(BF)
        places = lax.broadcasted_iota(jnp.int32, (PAIR, rows), 0)
        augt[...] = jnp.where(
            (places < SEG_COUNT) & (places != seg_row_ref[0]), -FAR, 0.0
        ).astype(BF)

    ka[:, :PAIR] = qkv_ref[1]
    vt[...] = qkv_ref[2].T
    qt[...] = qkv_ref[0].T
    empty = jnp.zeros((HEAD, block), BF)

    def attended(span, keys):
        extra = augt[:, span]
        for h in range(2):
            mine = qt[h * HEAD:(h + 1) * HEAD, span]
            mixed = jnp.concatenate([mine, empty, extra] if h == 0 else [empty, mine, extra], axis=0)
            scores = dot(ka[keys, :], mixed)
            top = jnp.max(scores, axis=0, keepdims=True)
            expo = jnp.exp2(scores - top)
            total = jnp.sum(expo, axis=0, keepdims=True)
            context = dot(vt[h * HEAD:(h + 1) * HEAD, keys], expo.astype(BF))
            ctxt_ref[h * HEAD:(h + 1) * HEAD, span] = (context / total).astype(BF)
            lse_ref[0, h:h + 1, span] = top + jnp.log2(total)

    def step(i, carry):
        attended(pl.ds(pl.multiple_of(i * block, block), block), slice(0, LONGEST))
        return carry

    lax.fori_loop(0, LONGEST // block, step, 0)
    attended(slice(LONGEST, rows), slice(LONGEST, rows))
    given = dot(ctxt_ref[...], pick[...]).astype(BF)
    near_ref[...] = given[:, :half].T
    away_ref[...] = given[:, half:].T


def attend(b, idx_col, qkv, seg_col, seg_row, block=256):
    rows, share = qkv.shape[1:]
    pairs = share // PAIR
    half = rows // 2
    whole = lambda shape: pl.BlockSpec((1,) + shape, lambda j: (b, 0, 0))
    three = pl.BlockSpec((3, rows, PAIR), lambda j: (0, 0, j))
    column = lambda n: pl.BlockSpec((n, PAIR), lambda j: (0, j))
    return pl.pallas_call(
        functools.partial(attend_body, block),
        grid=(pairs,),
        in_specs=[whole((rows, 1)), three, whole((rows, 1)), whole((1, rows))],
        out_specs=[column(half), column(half), pl.BlockSpec((PAIR, rows), lambda j: (j, 0)),
                   pl.BlockSpec((1, 8, rows), lambda j: (j, 0, 0))],
        out_shape=[jax.ShapeDtypeStruct((half, share), BF), jax.ShapeDtypeStruct((half, share), BF),
                   jax.ShapeDtypeStruct((share, rows), BF),
                   jax.ShapeDtypeStruct((pairs, 8, rows), F32)],
        scratch_shapes=[pltpu.VMEM((rows, rows), BF), pltpu.VMEM((rows, 2 * PAIR), BF),
                        pltpu.VMEM((PAIR, rows), BF), pltpu.VMEM((PAIR, rows), BF),
                        pltpu.VMEM((PAIR, rows), BF)],
        compiler_params=pltpu.CompilerParams(vmem_limit_bytes=60 << 20),
        cost_estimate=pl.CostEstimate(
            flops=pairs * 2 * 2 * rows * rows * 3 * PAIR, bytes_accessed=2 * 6 * rows * share,
            transcendentals=2 * pairs * rows * rows,
        ),
        name="attend",
    )(idx_col, qkv, seg_col, seg_row)


def attend_back_body(block, idx_ref, qkv_ref, seg_col_ref, seg_row_ref, lse_ref,
                     ctxt_ref, gnear_ref, gaway_ref, cos_ref, sin_ref,
                     grads_ref,
                     pick, ka, va, kt, qt, dt, go, delta, dkacc, dvacc, dqt, augt):
    rows = qkv_ref.shape[1]
    half = gnear_ref.shape[0]

    @pl.when(pl.program_id(0) == 0)
    def _():
        def fill(i, carry):
            span = pl.ds(pl.multiple_of(i * block, block), block)
            pick[span, :] = (
                lax.broadcasted_iota(jnp.int32, (block, rows), 1) == idx_ref[0, span, :]
            ).astype(BF)
            return carry

        lax.fori_loop(0, rows // block, fill, 0)
        lanes = lax.broadcasted_iota(jnp.int32, (rows, PAIR), 1)
        ones = ((lanes == seg_col_ref[0]) | (lanes >= SEG_COUNT)).astype(BF)
        ka[:, PAIR:] = ones
        va[:, PAIR:] = jnp.ones((rows, PAIR), BF)
        places = lax.broadcasted_iota(jnp.int32, (8, rows), 0)
        augt[...] = jnp.where(
            (places < SEG_COUNT) & (places != seg_row_ref[0]), -FAR, 0.0
        )

    ka[:, :PAIR] = qkv_ref[1]
    va[:, :PAIR] = qkv_ref[2]
    kt[...] = qkv_ref[1].T
    qt[...] = qkv_ref[0].T
    grad = dot(pick[:, :half], gnear_ref[...]) + dot(pick[:, half:], gaway_ref[...])
    go[...] = grad.astype(BF)
    dt[...] = go[...].T
    weighed = dt[...].astype(F32) * ctxt_ref[...].astype(F32)
    delta[0:1, :] = jnp.sum(weighed[:HEAD], axis=0, keepdims=True)
    delta[1:2, :] = jnp.sum(weighed[HEAD:], axis=0, keepdims=True)
    dkacc[...] = jnp.zeros_like(dkacc)
    dvacc[...] = jnp.zeros_like(dvacc)
    empty = jnp.zeros((HEAD, block), BF)
    blank = jnp.zeros((PAIR - 16, block), BF)
    wide = lax.broadcasted_iota(jnp.int32, (block, PAIR), 1)
    zero = jnp.zeros((block, PAIR), BF)

    def thirds(row, start):
        first = row.astype(BF).astype(F32)
        second = (row - first).astype(BF).astype(F32)
        third = row - first - second
        places = lax.broadcasted_iota(jnp.int32, (16, block), 0)
        return jnp.where(places == start, first,
                         jnp.where(places == start + 1, second,
                                   jnp.where(places == start + 2, third, 0.0)))

    def attended(span, keys):
        base = jnp.concatenate([augt[:, span], jnp.zeros((8, block), F32)], axis=0)
        for h in range(2):
            part = slice(h * HEAD, (h + 1) * HEAD)
            low = (base + thirds(-lse_ref[0, h:h + 1, span], SEG_COUNT)).astype(BF)
            mine = qt[part, span]
            order = (mine, empty) if h == 0 else (empty, mine)
            scores = dot(ka[keys, :], jnp.concatenate(order + (low, blank), axis=0))
            probs = jnp.exp2(scores)
            low = thirds(-delta[h:h + 1, span], 0).astype(BF)
            mine = dt[part, span]
            order = (mine, empty) if h == 0 else (empty, mine)
            slope = dot(va[keys, :], jnp.concatenate(order + (low, blank), axis=0))
            grads = (probs * slope).astype(BF)
            keep = wide < HEAD if h == 0 else wide >= HEAD
            dvacc[keys, :] += dot(probs.astype(BF), jnp.where(keep, go[span, :], zero))
            dkacc[keys, :] += dot(grads, jnp.where(keep, qkv_ref[0, span, :], zero))
            dqt[part, span] = dot(kt[part, keys], grads)

    def step(i, carry):
        attended(pl.ds(pl.multiple_of(i * block, block), block), slice(0, LONGEST))
        return carry

    lax.fori_loop(0, LONGEST // block, step, 0)
    attended(slice(LONGEST, rows), slice(LONGEST, rows))
    cosine, sine = cos_ref[0], sin_ref[0]
    turned = dqt[...].T
    grads_ref[0] = ((turned * cosine - pair_swap(turned) * sine) * (1.0 / math.sqrt(HEAD))).astype(BF)
    turned = dkacc[...]
    grads_ref[1] = ((turned * cosine - pair_swap(turned) * sine) * LN2).astype(BF)
    grads_ref[2] = dvacc[...].astype(BF)


def attend_back(b, idx_col, qkv, seg_col, seg_row, lse, ctxt, gnear, gaway, cosine, sine, block=256):
    rows, share = qkv.shape[1:]
    pairs = share // PAIR
    half = rows // 2
    whole = lambda shape: pl.BlockSpec((1,) + shape, lambda j: (b, 0, 0))
    three = pl.BlockSpec((3, rows, PAIR), lambda j: (0, 0, j))
    given = pl.BlockSpec((half, PAIR), lambda j: (b, j))
    column = lambda n: pl.BlockSpec((n, PAIR), lambda j: (0, j))
    return pl.pallas_call(
        functools.partial(attend_back_body, block),
        grid=(pairs,),
        in_specs=[whole((rows, 1)), three, whole((rows, 1)), whole((1, rows)),
                  pl.BlockSpec((1, 8, rows), lambda j: (j, 0, 0)),
                  pl.BlockSpec((PAIR, rows), lambda j: (j, 0)),
                  given, given, whole((rows, PAIR)), whole((rows, PAIR))],
        out_specs=pl.BlockSpec((3, rows, PAIR), lambda j: (0, 0, j)),
        out_shape=pltpu.HBM((3, rows, share), BF),
        scratch_shapes=[pltpu.VMEM((rows, rows), BF), pltpu.VMEM((rows, 2 * PAIR), BF),
                        pltpu.VMEM((rows, 2 * PAIR), BF), pltpu.VMEM((PAIR, rows), BF),
                        pltpu.VMEM((PAIR, rows), BF), pltpu.VMEM((PAIR, rows), BF),
                        pltpu.VMEM((rows, PAIR), BF), pltpu.VMEM((8, rows), F32),
                        pltpu.VMEM((rows, PAIR), F32), pltpu.VMEM((rows, PAIR), F32),
                        pltpu.VMEM((PAIR, rows), F32), pltpu.VMEM((8, rows), F32)],
        compiler_params=pltpu.CompilerParams(vmem_limit_bytes=60 << 20),
        cost_estimate=pl.CostEstimate(
            flops=pairs * 2 * 2 * rows * rows * 7 * PAIR, bytes_accessed=2 * 9 * rows * share,
            transcendentals=2 * pairs * rows * rows,
        ),
        name="attend_back",
    )(idx_col, qkv, seg_col, seg_row, lse, ctxt, gnear, gaway, cosine, sine)


def project_back_body(block, part_ref, g_ref, row_ref, wnear_ref, waway_ref,
                      near_ref, away_ref, work, hold, sems):
    rows, share = g_ref.shape[1:]
    half = near_ref.shape[0]
    for copy in own_columns(part_ref[0], wnear_ref, waway_ref, hold, sems):
        copy.wait()

    def step(i, carry):
        span = pl.ds(pl.multiple_of(i * block, block), block)
        total = None
        for place in range(3):
            term = dot_rt(g_ref[place, span, :], hold[:, place * share:(place + 1) * share])
            total = term if total is None else total + term
        work[span, :] = total.astype(BF)
        return carry

    lax.fori_loop(0, rows // block, step, 0)
    small = block // 2

    def back(i, carry):
        span = pl.ds(pl.multiple_of(i * small, small), small)
        for base, out_ref in ((half, away_ref), (0, near_ref)):
            pick = (lax.broadcasted_iota(jnp.int32, (small, rows), 0) + (base + i * small) == row_ref[0]).astype(BF)
            out_ref[span, :] = dot(pick, work[...]).astype(BF)
        return carry

    lax.fori_loop(0, half // small, back, 0)


def project_back(b, part, grads, idx_row, near_w, away_w, block=256):
    rows, share = grads.shape[1:]
    width = 2 * share
    half = rows // 2
    smem, anywhere = (pl.BlockSpec(memory_space=s) for s in (pltpu.SMEM, pl.ANY))
    return pl.pallas_call(
        functools.partial(project_back_body, block),
        grid=(1,),
        in_specs=[smem, pl.BlockSpec((3, rows, share), lambda i: (0, 0, 0)),
                  pl.BlockSpec((1, 1, rows), lambda i: (b, 0, 0)), anywhere, anywhere],
        out_specs=[pl.BlockSpec((half, width), lambda i: (0, 0))] * 2,
        scratch_shapes=[pltpu.VMEM((rows, width), BF), pltpu.VMEM((width, 3 * share), BF),
                        pltpu.SemaphoreType.DMA((6,))],
        out_shape=[jax.ShapeDtypeStruct((half, width), BF)] * 2,
        compiler_params=pltpu.CompilerParams(vmem_limit_bytes=40 << 20),
        cost_estimate=pl.CostEstimate(
            flops=2 * rows * width * (rows + 3 * share),
            bytes_accessed=2 * rows * (width + 3 * share) + 6 * width * share,
            transcendentals=0,
        ),
        name="project_back",
    )(part, grads, idx_row, near_w, away_w)


def weight_back_body(batches, *refs):
    xw_ref, g_refs, (gw_ref, gb_ref) = refs[0], refs[1:1 + batches], refs[1 + batches:]
    total, thin = None, None
    for b, g_ref in enumerate(g_refs):
        term = dot_lt(xw_ref[b], g_ref[0])
        line = jnp.sum(g_ref[0].astype(F32), axis=0, keepdims=True)
        total = term if total is None else total + term
        thin = line if thin is None else thin + line
    gw_ref[...] = total.astype(BF)
    gb_ref[...] = jnp.broadcast_to(thin, gb_ref.shape)


def weight_back(xws, grads):
    (batches, rows, width), share = xws.shape, grads[0].shape[2]
    each = pl.BlockSpec((1, rows, share), lambda s: (s, 0, 0))
    return pl.pallas_call(
        functools.partial(weight_back_body, batches),
        grid=(3,),
        in_specs=[pl.BlockSpec(xws.shape, lambda s: (0, 0, 0))] + [each] * batches,
        out_specs=[pl.BlockSpec((width, share), lambda s: (0, s)),
                   pl.BlockSpec((8, share), lambda s: (0, s))],
        out_shape=[jax.ShapeDtypeStruct((width, 3 * share), BF), jax.ShapeDtypeStruct((8, 3 * share), F32)],
        compiler_params=pltpu.CompilerParams(vmem_limit_bytes=60 << 20),
        cost_estimate=pl.CostEstimate(
            flops=2 * batches * rows * width * 3 * share,
            bytes_accessed=2 * batches * rows * (width + 3 * share) + 6 * width * share,
            transcendentals=0,
        ),
        name="weight_back",
    )(xws, *grads)


EPS = 1e-6
ERF_SLOPE = 0.3275911 * math.sqrt(0.5)
ERF_TERMS = (0.254829592, -0.284496736, 1.421413741, -1.453152027, 1.061405429)


def gauss_parts(u):
    bell = jnp.exp2(u * u * (-0.5 * LOG2E))
    t = 1.0 / (1.0 + ERF_SLOPE * jnp.abs(u))
    poly = 0.5 * ERF_TERMS[4]
    for term in ERF_TERMS[3::-1]:
        poly = poly * t + 0.5 * term
    tail = poly * t * bell
    below = jnp.where(u < 0.0, tail, 1.0 - tail)
    return u * below, below + u * bell * (1.0 / math.sqrt(2.0 * math.pi))


def row_mean(value):
    return jnp.sum(value, axis=1, keepdims=True) * (1.0 / value.shape[1])


def standard(hidden):
    centre = hidden - row_mean(hidden)
    root = lax.rsqrt(row_mean(centre * centre) + EPS)
    return centre * root, root


def standard_back(grad, norm, root):
    return root * (grad - row_mean(grad) - norm * row_mean(grad * norm))


def feed_body(chunk, part_ref, x_ref, near_ref, away_ref, dy_ref, thin_ref, bup_ref,
              unear_ref, uaway_ref, dnear_ref, daway_ref,
              out_ref, dh_ref, cnear_ref, caway_ref, sums_ref, bsum_ref,
              dmine_ref, dtheirs_ref, omine_ref, otheirs_ref,
              wo_near, wo_away, wup, wdown, slopes, acts, gup, gdown, go_near, go_away, sems, out_sems):
    core = part_ref[0]
    width, wide = wup.shape
    half_w, half_f = width // 2, wide // 2

    @pl.when(pl.program_id(0) == 0)
    def _():
        copies = []
        for t, (u_ref, d_ref) in enumerate(((unear_ref, dnear_ref), (uaway_ref, daway_ref))):
            side = core if t == 0 else 1 - core
            hold = wo_near if t == 0 else wo_away
            copies += [
                pltpu.make_async_copy(u_ref.at[:, :width], hold, sems.at[t]),
                pltpu.make_async_copy(
                    u_ref.at[:, width:], wup.at[pl.ds(pl.multiple_of(side * half_w, 128), half_w), :],
                    sems.at[2 + t]),
                pltpu.make_async_copy(
                    d_ref, wdown.at[pl.ds(pl.multiple_of(side * half_f, 128), half_f), :], sems.at[4 + t]),
            ]
        for copy in copies:
            copy.start()
        for ref in (sums_ref, bsum_ref, gup, gdown, go_near, go_away):
            ref[...] = jnp.zeros_like(ref)
        for copy in copies:
            copy.wait()

    b_out, gain_one, shift_one, b_down, gain_two, shift_two = (thin_ref[i:i + 1, :] for i in range(6))

    def tally(row, value):
        sums_ref[row:row + 1, :] += jnp.sum(value, axis=0, keepdims=True)

    attended = dot(near_ref[...], wo_near[...]) + dot(away_ref[...], wo_away[...]) + b_out
    norm_one, root_one = standard(x_ref[...].astype(F32) + attended)
    first = norm_one * gain_one + shift_one
    low = first.astype(BF)
    lowered = None
    for c in range(wide // chunk):
        cols = slice(c * chunk, (c + 1) * chunk)
        act, slope = gauss_parts(dot(low, wup[:, cols]) + bup_ref[:, cols])
        act = act.astype(BF)
        acts[:, cols] = act
        slopes[:, cols] = slope.astype(BF)
        term = dot(act, wdown[cols, :])
        lowered = term if lowered is None else lowered + term
    norm_two, root_two = standard(first + lowered + b_down)
    out_ref[...] = (norm_two * gain_two + shift_two).astype(BF)
    dy = dy_ref[...].astype(F32)
    tally(4, dy * norm_two)
    tally(5, dy)
    grad_two = standard_back(dy * gain_two, norm_two, root_two)
    dlow = grad_two.astype(BF)
    tally(3, dlow.astype(F32))
    total = grad_two
    low_t, dlow_t = low.T, dlow.T
    for c in range(wide // chunk):
        cols = slice(c * chunk, (c + 1) * chunk)
        dup = (dot_rt(dlow, wdown[cols, :]) * slopes[:, cols].astype(F32)).astype(BF)
        gdown[:, cols] += dot(dlow_t, acts[:, cols])
        gup[:, cols] += dot(low_t, dup)
        bsum_ref[0:1, cols] += jnp.sum(dup.astype(F32), axis=0, keepdims=True)
        total = total + dot_rt(dup, wup[:, cols])
    tally(1, total * norm_one)
    tally(2, total)
    grad_one = standard_back(total * gain_one, norm_one, root_one)
    dh_ref[...] = grad_one
    da = grad_one.astype(BF)
    tally(0, da.astype(F32))
    go_near[...] += dot(near_ref[...].T, da)
    go_away[...] += dot(away_ref[...].T, da)
    cnear_ref[...] = dot_rt(da, wo_near[...]).astype(BF)
    caway_ref[...] = dot_rt(da, wo_away[...]).astype(BF)

    @pl.when(pl.program_id(0) == pl.num_programs(0) - 1)
    def _():
        rows_d = [pl.ds(pl.multiple_of(side * half_f, 128), half_f) for side in (core, 1 - core)]
        rows_u = [pl.ds(pl.multiple_of(side * half_w, 128), half_w) for side in (core, 1 - core)]
        copies = []
        for t, (d_ref, o_ref, hold) in enumerate(((dmine_ref, omine_ref, wo_near), (dtheirs_ref, otheirs_ref, wo_away))):
            copies += [
                pltpu.make_async_copy(wdown.at[rows_d[t], :], d_ref, out_sems.at[3 * t]),
                pltpu.make_async_copy(wup.at[rows_u[t], :], o_ref.at[:, :wide], out_sems.at[3 * t + 1]),
                pltpu.make_async_copy(hold, o_ref.at[:, wide:], out_sems.at[3 * t + 2]),
            ]
        for c in range(wide // width):
            cols = slice(c * width, (c + 1) * width)
            wdown[cols, :] = gdown[:, cols].T.astype(BF)
        copies[0].start()
        copies[3].start()
        for c in range(wide // width):
            cols = slice(c * width, (c + 1) * width)
            wup[:, cols] = gup[:, cols].astype(BF)
        wo_near[...] = go_near[...].astype(BF)
        wo_away[...] = go_away[...].astype(BF)
        for k in (1, 2, 4, 5):
            copies[k].start()
        for copy in copies:
            copy.wait()


def feed(part, x, near, away, dy, thin, bup, unear, uaway, dnear, daway, block=256, chunk=768):
    rows, width = x.shape
    share = near.shape[1]
    wide = bup.shape[1]
    line = lambda n: pl.BlockSpec((block, n), lambda i: (i, 0))
    fixed = lambda shape: pl.BlockSpec(shape, lambda i: (0, 0))
    anywhere = pl.BlockSpec(memory_space=pl.ANY)
    shape = lambda n, dt: jax.ShapeDtypeStruct((rows, n), dt)
    half = lambda n, m: jax.ShapeDtypeStruct((n // 2, m), BF)
    return pl.pallas_call(
        functools.partial(feed_body, chunk),
        grid=(rows // block,),
        in_specs=[pl.BlockSpec(memory_space=pltpu.SMEM), line(width), line(share), line(share), line(width),
                  fixed(thin.shape), fixed(bup.shape), anywhere, anywhere, anywhere, anywhere],
        out_specs=[line(width), line(width), line(share), line(share), fixed((8, width)), fixed((8, wide))]
        + [anywhere] * 4,
        out_shape=[shape(width, BF), shape(width, F32), shape(share, BF), shape(share, BF),
                   jax.ShapeDtypeStruct((8, width), F32), jax.ShapeDtypeStruct((8, wide), F32),
                   half(wide, width), half(wide, width), half(width, wide + width), half(width, wide + width)],
        scratch_shapes=[pltpu.VMEM((share, width), BF), pltpu.VMEM((share, width), BF),
                        pltpu.VMEM((width, wide), BF), pltpu.VMEM((wide, width), BF),
                        pltpu.VMEM((block, wide), BF), pltpu.VMEM((block, wide), BF),
                        pltpu.VMEM((width, wide), F32), pltpu.VMEM((width, wide), F32),
                        pltpu.VMEM((share, width), F32), pltpu.VMEM((share, width), F32),
                        pltpu.SemaphoreType.DMA((6,)), pltpu.SemaphoreType.DMA((6,))],
        compiler_params=pltpu.CompilerParams(vmem_limit_bytes=60 << 20),
        cost_estimate=pl.CostEstimate(
            flops=2 * rows * width * (3 * width + 6 * wide),
            bytes_accessed=2 * rows * 7 * width + 8 * width * (wide + width),
            transcendentals=2 * rows * wide,
        ),
        name="feed",
    )(part, x, near, away, dy, thin, bup, unear, uaway, dnear, daway)


def swap_cores(value):
    return lax.ppermute(value, "seq", [(0, 1), (1, 0)])


def swap_x(value):
    return lax.ppermute(value, "fsdp", [(i, i ^ 1) for i in range(16)])


def swap_y(value):
    return lax.ppermute(value, "fsdp", [(i, i ^ 2) for i in range(16)])


def flip_z(value, k):
    return lax.ppermute(value, "fsdp", [(i, i ^ (4 * k)) for i in range(16)])


def shift_z(value, k):
    return lax.ppermute(value, "fsdp", [(i, (i + 4 * k) % 16) for i in range(16)])


def assemble_body(lines, place_ref, ax_ref, ay_ref, bx_ref, by_ref, *out_refs):
    place = place_ref[0]
    z, y, x = place // 4, (place // 2) % 2, place % 2
    n = ax_ref.shape[1]

    def put(owner, piece):
        out_refs[0][owner] = piece[:, :out_refs[0].shape[2]]
        for c in range(lines):
            width = out_refs[1].shape[2]
            at = out_refs[0].shape[2] + c * width
            out_refs[1][owner, c * n:(c + 1) * n, :] = piece[:, at:at + width]

    for j in range(4):
        k, o = j % 2, j // 2
        near_z, far_z = lax.rem(z - k + 4, 4), lax.rem(z - k + 2, 4)
        flip_x = lax.rem(x + o, 2)
        flip_y = lax.rem(y + o, 2)
        put(near_z * 4 + y * 2 + flip_x, ax_ref[j])
        put(near_z * 4 + (1 - y) * 2 + flip_x, ay_ref[j])
        put(far_z * 4 + flip_y * 2 + x, by_ref[j])
        put(far_z * 4 + flip_y * 2 + 1 - x, bx_ref[j])


def assemble(place, parts, lines=0, line=0):
    n, width = parts[0].shape[1:]
    vmem = pl.BlockSpec(memory_space=pltpu.VMEM)
    shapes = [(16, n, width - lines * line)] + ([(16, lines * n, line)] if lines else [])
    return pl.pallas_call(
        functools.partial(assemble_body, lines),
        in_specs=[pl.BlockSpec(memory_space=pltpu.SMEM)] + [vmem] * 4,
        out_shape=[jax.ShapeDtypeStruct(shape, BF) for shape in shapes],
        compiler_params=pltpu.CompilerParams(vmem_limit_bytes=40 << 20),
        cost_estimate=pl.CostEstimate(flops=0, bytes_accessed=4 * 16 * n * width, transcendentals=0),
        name="assemble",
    )(place, *parts)


def tie(values, after=()):
    return lax.optimization_barrier((values, after))[0]


def reach_z(shard):
    first = jnp.stack([shard, shift_z(shard, 1)])
    second = jnp.stack([shift_z(shard, 2), shift_z(shard, 3)])
    return first, second


def reach_one(first, second):
    return jnp.concatenate([first, swap_x(first)], axis=0), jnp.concatenate([second, swap_y(second)], axis=0)


def reach_two(first, second):
    return first, swap_y(first), swap_x(second), second


def joined(parts, lines=0, line=0):
    place = jnp.full((1,), lax.axis_index("fsdp"), jnp.int32)
    return [value.reshape(-1, value.shape[2]) for value in assemble(place, parts, lines, line)]


def pick(part, at, axis):
    return lax.dynamic_index_in_dim(part, at, axis, keepdims=False)


def corner():
    place = lax.axis_index("fsdp")
    return place // 4, (place // 2) % 2, place % 2


def fold_call(body, name, grid, place, operands, in_specs, out_specs, out_shape):
    size = sum(math.prod(item.shape) for item in out_shape)
    return pl.pallas_call(
        body,
        grid_spec=pltpu.PrefetchScalarGridSpec(
            num_scalar_prefetch=1, grid=grid, in_specs=in_specs, out_specs=out_specs),
        out_shape=out_shape,
        compiler_params=pltpu.CompilerParams(vmem_limit_bytes=40 << 20),
        cost_estimate=pl.CostEstimate(flops=0, bytes_accessed=8 * size, transcendentals=0),
        name=name,
    )(place, *operands)


def merge_one_body(place_ref, *refs):
    count = len(refs) // 3
    for mine, theirs, out in zip(refs[:count], refs[count:2 * count], refs[2 * count:]):
        out[0, 0] = (mine[0, 0, 0, 0].astype(F32) + theirs[0, 0, 0, 0].astype(F32)).astype(BF)


def merge_one(place, mines, theirs):
    cubes = lambda values: [v.reshape(2, 2, 2, 2, v.shape[0] // 16, v.shape[1]) for v in values for _ in range(2)]
    specs, outs, shapes = [], [], []
    for value in mines:
        n, width = value.shape[0] // 16, value.shape[1]
        specs += [pl.BlockSpec((1, 1, 1, 1, n, width), lambda k, j, p: (0, k, 1 - p[1], j, 0, 0)),
                  pl.BlockSpec((1, 1, 1, 1, n, width), lambda k, j, p: (1, k, j, 1 - p[2], 0, 0))]
        outs += [pl.BlockSpec((1, 1, n, width), lambda k, j, p: (k, j, 0, 0))] * 2
        shapes += [jax.ShapeDtypeStruct((2, 2, n, width), BF)] * 2
    return fold_call(merge_one_body, "merge_one", (2, 2), place, cubes(mines) + cubes(theirs), specs * 2, outs, shapes)


def merge_two_body(place_ref, *refs):
    count = len(refs) // 5
    y, x = place_ref[1], place_ref[2]
    groups = [refs[i * count:(i + 1) * count] for i in range(5)]
    for i, (mine, theirs, came, stay, send) in enumerate(zip(*groups)):
        if i % 2 == 0:
            part = lambda at: mine[0, 0, 0, at].astype(F32) + theirs[0, 0, 0, at].astype(F32) + came[0, at].astype(F32)
            own = x
        else:
            part = lambda at: mine[0, 0, at, 0].astype(F32) + theirs[0, 0, at, 0].astype(F32) + came[0, at].astype(F32)
            own = y
        stay[0] = part(own)
        send[0] = part(1 - own).astype(BF)


def merge_two(place, mines, theirs, came):
    cubes = lambda values: [v.reshape(2, 2, 2, 2, v.shape[0] // 16, v.shape[1]) for v in values for _ in range(2)]
    specs, came_specs, outs, stays, sends = [], [], [], [], []
    for value in mines:
        n, width = value.shape[0] // 16, value.shape[1]
        specs += [pl.BlockSpec((1, 1, 1, 2, n, width), lambda k, p: (0, k, p[1], 0, 0, 0)),
                  pl.BlockSpec((1, 1, 2, 1, n, width), lambda k, p: (1, k, 0, p[2], 0, 0))]
        came_specs += [pl.BlockSpec((1, 2, n, width), lambda k, p: (k, 0, 0, 0))] * 2
        outs += [pl.BlockSpec((1, n, width), lambda k, p: (k, 0, 0))] * 2
        stays += [pltpu.HBM((2, n, width), F32)] * 2
        sends += [pltpu.HBM((2, n, width), BF)] * 2
    both = fold_call(merge_two_body, "merge_two", (2,), place, cubes(mines) + cubes(theirs) + list(came),
                     specs * 2 + came_specs, outs * 2, stays + sends)
    return both[:len(stays)], both[len(stays):]


def merge_three_body(place_ref, *refs):
    stays, came, (stay_ref, send_ref) = refs[:4], refs[4:8], refs[8:]
    near = lax.rem(place_ref[0], 2)
    n = stay_ref.shape[1]
    for half in range(2):
        for at, out in ((near, stay_ref), (1 - near, send_ref)):
            lines = stays[half][at] + came[half][at].astype(F32)
            wide = stays[2 + half][at] + came[2 + half][at].astype(F32)
            out[half, :, :wide.shape[1]] = wide.astype(out.dtype)
            for c in range(lines.shape[0] // n):
                to = wide.shape[1] + c * lines.shape[1]
                out[half, :, to:to + lines.shape[1]] = lines[c * n:(c + 1) * n].astype(out.dtype)


def merge_three(place, stays, came):
    rows, line = stays[0].shape[1:]
    n, wide = stays[2].shape[1:]
    total = wide + rows // n * line
    whole = lambda shape: pl.BlockSpec(shape, lambda p: (0,) * len(shape))
    shapes = [jax.ShapeDtypeStruct((2, n, total), F32), jax.ShapeDtypeStruct((2, n, total), BF)]
    return fold_call(merge_three_body, "merge_three", (), place, list(stays) + list(came),
                     [whole(v.shape) for v in list(stays) + list(came)], [whole(v.shape) for v in shapes], shapes)


def fold_one(value):
    z, y, x = corner()
    rows, width = value.shape
    cube = value.reshape(2, 2, 2, 2, rows // 16, width)
    return (value,), (pick(cube[0], 1 - y, 1).astype(BF), pick(cube[1], 1 - x, 2).astype(BF))


def fold_two(stay, sends, after=()):
    z, y, x = corner()
    rows, width = stay[0].shape
    cube = stay[0].reshape(2, 2, 2, 2, rows // 16, width)
    came = tie((swap_y(sends[0]), swap_x(sends[1])), after)
    first = pick(cube[0], y, 1).astype(F32) + came[0].astype(F32)
    second = pick(cube[1], x, 2).astype(F32) + came[1].astype(F32)
    return (first, second), (pick(first, 1 - x, 1).astype(BF), pick(second, 1 - y, 1).astype(BF))


def fold_cross(stay, sends, after=()):
    z, y, x = corner()
    came = tie((swap_x(sends[0]), swap_y(sends[1])), after)
    first = pick(stay[0], x, 1) + came[0].astype(F32)
    second = pick(stay[1], y, 1) + came[1].astype(F32)
    return jnp.concatenate([first, second], axis=0)


def fold_three(stack):
    near = corner()[0] % 2
    cube = stack.reshape((2, 2) + stack.shape[1:])
    return (pick(cube, near, 1),), (pick(cube, 1 - near, 1).astype(BF),)


def fold_four(stay, sends, after=()):
    z = corner()[0]
    far = z // 2
    came = tie(flip_z(sends[0], 1), after)
    total = stay[0] + came.astype(F32)
    return (pick(total, far, 0),), (pick(total, 1 - far, 0).astype(BF),)


def fold_end(stay, sends, after=()):
    return stay[0] + tie(flip_z(sends[0], 2), after).astype(F32)


def on_device(tokens, permutation, segment_ids, cotangent, *shards):
    batches = tokens.shape[0]
    half, width = tokens.shape[2], tokens.shape[3]
    core = lax.axis_index("seq")
    share = width // 2
    owners = 2 * lax.axis_size("fsdp")
    staged = owners == 32
    part = jnp.full((1,), core, jnp.int32)
    thin = [i for i, piece in enumerate(shards) if piece.ndim == 1]
    sizes = [shards[i].shape[0] for i in thin]
    count = sum(sizes)
    n_qkv = shards[0].shape[0]
    room = n_qkv * 128
    tokens, cotangent = tokens[:, 0], cotangent[:, 0]

    away_tokens = swap_cores(tokens)
    idx_col, idx_row, seg_col, seg_row, cosine, sine = ready(part, permutation[:, 0], segment_ids[:, 0])
    if staged:
        q_shard, ud_shard = pack(shards[0], shards[2], shards[6], shards[8], [shards[i] for i in thin])
        first, second = reach_z(q_shard)
        first, second, idx_col = tie((first, second, idx_col))
        first_x, second_y = swap_x(first), swap_y(second)
        ud_shard = tie(ud_shard, first_x)
        q_parts = reach_two(jnp.concatenate([first, first_x], axis=0), jnp.concatenate([second, second_y], axis=0))
        ud_z = tuple(shift_z(ud_shard, k) for k in (1, 2, 3))
        xws = arrange(idx_col, tokens, away_tokens)
        q_parts = tie(q_parts, xws)
        (q_near,) = joined(q_parts)
    else:
        xws = arrange(idx_col, tokens, away_tokens)
        packed = jnp.concatenate([shards[i] for i in thin] + [jnp.zeros((room - count,), BF)])
        q_shard = jnp.concatenate([shards[0], packed.reshape(n_qkv, 128)], axis=1)
        q_near = lax.all_gather(q_shard, "fsdp", axis=0, tiled=True)
        u_near = lax.all_gather(jnp.concatenate([shards[2], shards[6]], axis=1), "fsdp", axis=0, tiled=True)
        d_near = lax.all_gather(shards[8], "fsdp", axis=0, tiled=True)
    q_away = swap_cores(q_near)

    slabs = [value[:, 3 * width:].reshape(owners // 2, n_qkv, 128) for value in (q_near, q_away)]
    vectors = jnp.concatenate(
        [jnp.where(core == 0, slabs[0], slabs[1]), jnp.where(core == 0, slabs[1], slabs[0])], axis=0
    ).astype(F32)
    spread, at = [], 0
    for i, size in enumerate(sizes):
        if staged:
            spread.append(vectors[:, i, :size].reshape(1, owners * size))
        else:
            spread.append(vectors.reshape(owners, room)[:, at:at + size].reshape(1, owners * size))
        at += size
    b_qkv, b_out, gain_one, shift_one, b_up, b_down, gain_two, shift_two = spread
    bias_own = jnp.concatenate(
        [lax.dynamic_slice_in_dim(b_qkv, core * share + s * width, share, 1) for s in range(3)], axis=1
    )
    blank_row = jnp.zeros((1, width), F32)
    thin_rows = jnp.concatenate(
        [b_out, gain_one, shift_one, b_down, gain_two, shift_two, blank_row, blank_row], axis=0
    )

    qkvs = [project(b, part, xws, q_near, q_away, bias_own, cosine, sine) for b in range(batches)]
    if staged:
        (one, two, three), qkvs = tie((ud_z, qkvs))
        first, second = jnp.stack([ud_shard, one]), jnp.stack([two, three])
        qkvs[0], first, second = tie((qkvs[0], first, second))
        first_x, second_y = swap_x(first), swap_y(second)
    kept, ctxs = [], []
    for b in range(batches):
        if staged and b == 1:
            first_x, second_y = tie((first_x, second_y), ctxs[0][0])
            first, second = jnp.concatenate([first, first_x], axis=0), jnp.concatenate([second, second_y], axis=0)
            qkvs[1], first, second = tie((qkvs[1], first, second))
            first_y, second_x = swap_y(first), swap_x(second)
        near, away, ctxt, lse = attend(b, idx_col, qkvs[b], seg_col, seg_row)
        kept.append((qkvs[b], ctxt, lse))
        ctxs.append((near, swap_cores(away)))
    if staged:
        first_y, second_x = tie((first_y, second_x), ctxs[1][0])
        ctxs[0] = (ctxs[0][0], tie(ctxs[0][1], ctxs[1][0]))
        u_near, d_near = tie(joined((first, first_y, second_x, second), 4, width), [pair[1] for pair in ctxs])
    u_away, d_away = swap_cores(u_near), swap_cores(d_near)
    near, away = (jnp.concatenate([item[i] for item in ctxs], axis=0) for i in range(2))
    (outputs, grad_one, cnear, caway, sums, bsum, d_mine, d_theirs, uo_mine, uo_theirs) = feed(
        part, tokens.reshape(batches * half, width), near, away,
        cotangent.reshape(batches * half, width), thin_rows, b_up, u_near, u_away, d_near, d_away,
    )
    caway = swap_cores(caway)
    d_theirs, uo_theirs = (swap_cores(value) for value in tie((d_theirs, uo_theirs), caway))
    plus = lambda mine, theirs: (mine.astype(F32) + theirs.astype(F32)).astype(BF)

    def back(b, given):
        qkv, ctxt, lse = kept[b]
        return attend_back(b, idx_col, qkv, seg_col, seg_row, lse, ctxt, *given, cosine, sine)

    givens = [(cnear, caway)] * batches
    if staged:
        first_back = back(0, givens[0])
        place = jnp.stack(corner()).astype(jnp.int32)
        mines, theirs = (d_mine, uo_mine), tie((d_theirs, uo_theirs), first_back)
        sends = merge_one(place, mines, theirs)
        given, sends = tie((givens[1], sends))
        grads = [first_back, back(1, given)]
        swaps = (swap_y, swap_x)
        came = tie([swaps[i % 2](send) for i, send in enumerate(sends)], grads[1])
        stays, sends = merge_two(place, mines, theirs, came)
        grads, sends = tie((grads, sends))
    else:
        grads = [back(b, givens[b]) for b in range(batches)]
        d_sum, uo_sum = plus(d_mine, d_theirs), plus(uo_mine, uo_theirs)
    gw_own, gb_own = weight_back(xws, grads)
    if staged:
        came = tie([swaps[1 - i % 2](send) for i, send in enumerate(sends)], gw_own)
        stay, send = merge_three(place, stays, came)
        grads, gw_own, gb_own, send = tie((grads, gw_own, gb_own, send))
        du_step = ((stay,), (send,))

    def halves(value):
        size = value.shape[0] // 2
        return (lax.dynamic_slice_in_dim(value, core * size, size, 0),
                lax.dynamic_slice_in_dim(value, (1 - core) * size, size, 0))

    blank = jnp.zeros((share,), F32)
    thin_columns = []
    for s in range(3):
        span = slice(s * share, (s + 1) * share)
        thin_columns += [jnp.where(core == 0, gb_own[0, span], blank),
                         jnp.where(core == 0, blank, gb_own[0, span])]
    six = sums[:6].reshape(6, owners, -1).transpose(1, 0, 2).reshape(owners, -1)
    slab = jnp.concatenate(
        [jnp.concatenate(thin_columns).reshape(owners, -1), bsum[0].reshape(owners, -1), six,
         jnp.zeros((owners, room - count), F32)], axis=1
    ).astype(BF).reshape(owners * n_qkv, 128)
    mine, theirs = (jnp.concatenate(pair, axis=1) for pair in zip(halves(gw_own), halves(slab)))
    theirs = swap_cores(theirs)
    q_sum = jnp.concatenate([
        mine[:, :3 * share], theirs[:, :3 * share],
        (mine[:, 3 * share:].astype(F32) + theirs[:, 3 * share:].astype(F32)).astype(BF),
    ], axis=1)
    backs = [project_back(0, part, grads[0], idx_row, q_near, q_away)]
    if staged:
        du_step = fold_four(*du_step, backs[0])
        last, q_step, du_step = tie((grads[1], fold_one(q_sum), du_step), backs)
        backs.append(project_back(1, part, last, idx_row, q_near, q_away))
        q_step = tie(fold_two(*q_step, backs[1]))
        g_uo = fold_end(*du_step, q_step)
        q_step = tie(fold_three(fold_cross(*q_step, g_uo)))
        q_step = fold_four(*q_step)
        g_down = jnp.concatenate([g_uo[:, (5 + i) * width:(6 + i) * width] for i in range(4)], axis=0)
    else:
        backs.append(project_back(1, part, grads[1], idx_row, q_near, q_away))
        summed = lambda value: lax.psum_scatter(
            value.astype(BF), "fsdp", scatter_dimension=0, tiled=True
        ).astype(F32)
        g_qkv, g_down, g_uo = summed(q_sum), summed(d_sum), summed(uo_sum)
    grad_one = grad_one.reshape(batches, half, width)
    token_grad = jnp.stack([
        (grad_one[b] + backs[b][0].astype(F32) + swap_cores(backs[b][1]).astype(F32)).astype(BF)
        for b in range(batches)
    ])
    if staged:
        g_qkv = fold_end(*q_step, (g_uo, token_grad))
    own, other = g_qkv[:, :3 * share], g_qkv[:, 3 * share:6 * share]
    columns = []
    for s in range(3):
        span = slice(s * share, (s + 1) * share)
        columns += [jnp.where(core == 0, own[:, span], other[:, span]),
                    jnp.where(core == 0, other[:, span], own[:, span])]
    g_out, g_up = g_uo[:, 4 * width:5 * width], g_uo[:, :4 * width]
    flat = g_qkv[:, 3 * width:].reshape(room)
    thin_out, at = [], 0
    for size in [sizes[0], sizes[4]] + [n_qkv] * 6:
        thin_out.append(flat[at:at + size])
        at += size
    g_bqkv, g_bup, g_bout, g_g1, g_s1, g_bdown, g_g2, g_s2 = thin_out
    return (
        outputs.reshape(batches, 1, half, width), token_grad[:, None],
        jnp.concatenate(columns, axis=1), g_bqkv, g_out, g_bout, g_g1, g_s1, g_up, g_bup, g_down, g_bdown, g_g2, g_s2,
    )


def solution(mesh):
    packs = P(None, "fsdp", "seq", None)
    ids = P(None, "fsdp", None)
    deep, flat = P(("seq", "fsdp"), None), P(("seq", "fsdp"))
    layers = (deep, flat, deep, flat, flat, flat, deep, flat, deep, flat, flat, flat)
    return jax.shard_map(
        on_device, mesh=mesh, in_specs=(packs, ids, ids, packs) + layers,
        out_specs=(packs, packs) + layers, check_vma=False,
    )
```
